32 devices in a mesh: seq: 16 (over z, x, core), head: 2 (over y).
Axes of the slice: x: 2, y: 2, z: 4, core: 2. Of those that a mesh axis runs over, the one named last changes fastest.
Arguments:
- queries: bfloat16 [12288, 4096], P('seq', 'head'), may hold values from -100 to 100
- keys: bfloat16 [12288, 4096], P('seq', 'head'), may hold values from -7 to 7
- values: bfloat16 [12288, 4096], P('seq', 'head'), may hold values from -6 to 6
- targets: bfloat16 [12288, 4096], P('seq', 'head'), may hold values from -6 to 6
- token_rate: float32 [12288, 8], P('seq', 'head'), may hold values from 0.1 to 1
- window: int32 [8], P('head'), may hold values from 256 to 512, as said below
- split: int32 [1], replicated, may hold values from 4608 to 7679
- fast_init: float32 [8, 3, 512, 512], P('head'), may hold values from -0.25 to 0.25
Outputs:
- mixed: bfloat16 [12288, 4096], P('seq', 'head')
- fast_final: float32 [8, 3, 512, 512], P('head')
The draws below stay inside these ranges and needn't reach their ends.
Inputs may be any that keep to these rules, and one draw needn't show every extreme that they name: Some head has a window of exactly 512.
All inputs are finite; a program needn't handle non-finite values.
Results may differ from the reference program's by a relative error of at most 0.0073.
Values may be sent and summed in bfloat16 or wider, within the bound.
A program may use at most 192 MiB of HBM per device.

```python
import math
import jax
import jax.numpy as jnp
from jax import lax

HEADS = 8
HD = 512
HID = 512
WIN = 512
TOKENS = 12288


def joint_draw(key):
    base = jax.random.fold_in(key, 11)
    key_a, key_b = jax.random.split(base, 2)
    shape = (TOKENS, HEADS * HD)
    keys = jax.random.truncated_normal(key_a, -6.0, 6.0, shape, jnp.float32)
    queries = jax.random.truncated_normal(key_b, -6.0, 6.0, shape, jnp.float32)
    return (queries, keys)


def draw_queries(key, part):
    return joint_draw(key)[0].astype(jnp.bfloat16)


def draw_keys(key, part):
    return joint_draw(key)[1].astype(jnp.bfloat16)


def draw_window(key, part):
    base = jax.random.fold_in(key, 23)
    key_a, key_b = jax.random.split(base)
    widths = jax.random.randint(key_a, (HEADS,), WIN // 2, WIN + 1)
    chosen = jax.random.randint(key_b, (), 0, HEADS)
    return jnp.where(jnp.arange(HEADS) == chosen, WIN, widths).astype(jnp.int32)


def block_levels(stream_key, extent, cuts, low, high):
    loudness = 1.0
    for axis_at, parts in cuts:
        draws = jax.random.uniform(jax.random.fold_in(jax.random.fold_in(stream_key, 6), axis_at), (parts,), jnp.float32, low / len(cuts), high / len(cuts))
        loudness = loudness * jnp.repeat(jnp.exp(draws), extent[axis_at] // parts).reshape((-1,) + (1,) * (len(extent) - 1 - axis_at))
    return loudness


def bell_draw(key, shape, spread, most, pieces=(), kind=jnp.bfloat16):
    values = spread * jax.random.normal(key, shape, jnp.float32)
    if pieces:
        values = values * block_levels(key, shape, pieces, -0.22, 0.18)
    return jnp.clip(values, -most, most).astype(kind)


def setup_inputs(seed: int = 0) -> dict:
    seeds = jax.random.split(jax.random.key(seed), 9)
    return {
        "queries": draw_queries(jax.random.fold_in(seeds[8], 71), 0),
        "keys": draw_keys(jax.random.fold_in(seeds[8], 71), 0),
        "values": bell_draw(seeds[2], (TOKENS, HEADS * HD), 1.0, 6.0, ((0, 16), (1, 2))),
        "targets": bell_draw(seeds[3], (TOKENS, HEADS * HD), 1.0, 6.0, ((0, 16), (1, 2))),
        "token_rate": jnp.clip(jnp.exp(math.log(1.0) - 2.3025851 * jax.random.uniform(seeds[4], (TOKENS, HEADS), jnp.float32) ** block_levels(seeds[4], (TOKENS, HEADS), ((0, 16), (1, 2)), -0.2, 0.2)), 0.1, 1.0),
        "window": draw_window(jax.random.fold_in(seeds[8], 71), 0),
        "split": jax.random.randint(seeds[6], (1,), TOKENS // 2 - TOKENS // 8, TOKENS // 2 + TOKENS // 8).astype(jnp.int32),
        "fast_init": bell_draw(seeds[7], (HEADS, 3, HD, HID), HD ** -0.5, 0.25, ((0, 2),), jnp.float32),
    }


fast_rate = 0.01
epsilon = 1e-06

def fast_apply(inputs, weights):
    first = jnp.dot(inputs, weights[0], preferred_element_type=jnp.float32)
    third = jnp.dot(inputs, weights[1], preferred_element_type=jnp.float32)
    act = (jax.nn.silu(first) * third).astype(jnp.bfloat16)
    return lax.dot_general(act, weights[2], (((1,), (1,)), ((), ())), preferred_element_type=jnp.float32)

def fast_grad(inputs, targets, scaled, weights):
    first = jnp.dot(inputs, weights[0], preferred_element_type=jnp.float32)
    third = jnp.dot(inputs, weights[1], preferred_element_type=jnp.float32)
    sigma = jax.nn.sigmoid(first)
    swish = first * sigma
    act = (swish * third).astype(jnp.bfloat16)
    d_out = (-scaled * targets.astype(jnp.float32)).astype(jnp.bfloat16)
    d_act = jnp.dot(d_out, weights[2], preferred_element_type=jnp.float32)
    d_first = (d_act * third * sigma * (1.0 + first * (1.0 - sigma))).astype(jnp.bfloat16)
    d_third = (d_act * swish).astype(jnp.bfloat16)
    dims = (((0,), (0,)), ((), ()))
    grad_one = lax.dot_general(inputs, d_first, dims, preferred_element_type=jnp.float32)
    grad_three = lax.dot_general(inputs, d_third, dims, preferred_element_type=jnp.float32)
    grad_two = lax.dot_general(d_out, act, dims, preferred_element_type=jnp.float32)
    return jnp.stack([grad_one, grad_three, grad_two])

def attend_head(query_head, key_head, value_head, width):
    total = query_head.shape[0]
    block = math.gcd(total, 512)
    pad = jnp.zeros((WIN, HD), jnp.bfloat16)
    key_pad = jnp.concatenate([pad, key_head], axis=0)
    value_pad = jnp.concatenate([pad, value_head], axis=0)
    scale = HD ** (-0.5)

    def one_block(start):
        query_block = lax.dynamic_slice_in_dim(query_head, start, block, 0)
        key_block = lax.dynamic_slice_in_dim(key_pad, start, block + WIN, 0)
        value_block = lax.dynamic_slice_in_dim(value_pad, start, block + WIN, 0)
        scores = lax.dot_general(query_block, key_block, (((1,), (1,)), ((), ())), preferred_element_type=jnp.float32) * scale
        query_pos = start + jnp.arange(block, dtype=jnp.int32)[:, None]
        key_pos = start - WIN + jnp.arange(block + WIN, dtype=jnp.int32)[None, :]
        live = (key_pos <= query_pos) & (key_pos > query_pos - width) & (key_pos >= 0)
        scores = jnp.where(live, scores, -1e+30)
        peak = lax.optimization_barrier(jnp.max(scores, axis=1, keepdims=True))
        expo = jnp.where(live, jnp.exp(scores - peak), 0.0)
        probs = (expo / lax.optimization_barrier(jnp.sum(expo, axis=1, keepdims=True))).astype(jnp.bfloat16)
        return jnp.dot(probs, value_block, preferred_element_type=jnp.float32)
    starts = jnp.arange(total // block, dtype=jnp.int32) * block
    return lax.map(one_block, starts).reshape(total, HD)

def renew_weights(weights, grads):
    square = jnp.sum(grads * grads)
    count = float(HEADS * 3 * HD * HID)
    return weights - fast_rate / jnp.sqrt(square / count + epsilon) * grads

def reference(queries, keys, values, targets, token_rate, window, split, fast_init):
    positions = jnp.arange(TOKENS, dtype=jnp.int32)[:, None]
    first_block = (positions < split[0]).astype(jnp.float32)
    second_block = 1.0 - first_block

    def column(array, head):
        return lax.dynamic_slice_in_dim(array, head * HD, HD, 1)

    def grads_of(weights, mask):

        def per_head(head):
            scaled = lax.dynamic_slice_in_dim(token_rate, head, 1, 1) * mask
            return fast_grad(column(keys, head), column(targets, head), scaled, weights[head].astype(jnp.bfloat16))
        return lax.map(per_head, jnp.arange(HEADS, dtype=jnp.int32))
    weights_zero = fast_init
    weights_one = renew_weights(weights_zero, grads_of(weights_zero, first_block))
    weights_two = renew_weights(weights_one, grads_of(weights_one, second_block))

    def output_head(head):
        query_head = column(queries, head)
        attn = attend_head(query_head, column(keys, head), column(values, head), window[head])
        early = fast_apply(query_head, weights_zero[head].astype(jnp.bfloat16))
        late = fast_apply(query_head, weights_one[head].astype(jnp.bfloat16))
        fast_out = first_block * early + second_block * late
        normed = fast_out / jnp.sqrt(lax.optimization_barrier(jnp.mean(fast_out * fast_out, axis=1, keepdims=True)) + epsilon)
        return (attn + normed).astype(jnp.bfloat16)
    heads_out = lax.map(output_head, jnp.arange(HEADS, dtype=jnp.int32))
    mixed = jnp.transpose(heads_out, (1, 0, 2)).reshape(TOKENS, HEADS * HD)
    return (mixed, weights_two)
```

```python
import functools

import jax
import jax.numpy as jnp
from jax import lax
from jax.experimental import pallas as pl
from jax.experimental.pallas import tpu as pltpu
from jax.sharding import PartitionSpec as P

WIN = 512
fast_rate = 0.01
epsilon = 1e-06
CORES = 2


def mm(a, b, ca, cb):
    return lax.dot_general(
        a, b, (((ca,), (cb,)), ((), ())), preferred_element_type=jnp.float32
    )


def grad_kernel(renewed, info_ref, coef_ref, keys_ref, targets_ref, scaled_ref, w_ref, *rest):
    if renewed:
        g_ref, out_ref = rest
    else:
        (out_ref,) = rest
    head = pl.program_id(0)

    @pl.when(info_ref[0] == 0)
    def _():
        out_ref[...] = jnp.zeros_like(out_ref)

    @pl.when(info_ref[0] != 0)
    def _():
        def weight(i):
            w = w_ref[0, i]
            if renewed:
                w = w - coef_ref[0] * g_ref[0, i].astype(jnp.float32)
            return w.astype(jnp.bfloat16)

        x = keys_ref[...]
        column = lax.broadcasted_iota(jnp.int32, scaled_ref.shape, 1)
        scaled = jnp.sum(
            jnp.where(column == head, scaled_ref[...], 0.0), axis=1, keepdims=True
        )
        first = mm(x, weight(0), 1, 0)
        third = mm(x, weight(1), 1, 0)
        d_out = (-scaled * targets_ref[...].astype(jnp.float32)).astype(jnp.bfloat16)
        d_act = mm(d_out, weight(2), 1, 0)
        sigma = jax.nn.sigmoid(first)
        swish = first * sigma
        act = (swish * third).astype(jnp.bfloat16)
        d_first = (d_act * third * sigma * (1.0 + first * (1.0 - sigma))).astype(jnp.bfloat16)
        d_third = (d_act * swish).astype(jnp.bfloat16)
        out_ref[0, 0] = mm(x, d_first, 0, 0).astype(jnp.bfloat16)
        out_ref[0, 1] = mm(x, d_third, 0, 0).astype(jnp.bfloat16)
        out_ref[0, 2] = mm(d_out, act, 0, 0).astype(jnp.bfloat16)


def gradients(info, coef, keys, targets, scaled, weights, g):
    local = keys.shape[0]
    heads, _, hd, hid = weights.shape
    wspec = pl.BlockSpec((1, 3, hd, hid), lambda h: (h, 0, 0, 0))
    smem = pl.BlockSpec(memory_space=pltpu.SMEM)
    col = pl.BlockSpec((local, hd), lambda h: (0, h))
    args = [info, coef, keys, targets, scaled, weights]
    specs = [smem, smem, col, col, pl.BlockSpec(scaled.shape, lambda h: (0, 0)), wspec]
    if g is not None:
        args.append(g)
        specs.append(wspec)
    return pl.pallas_call(
        functools.partial(grad_kernel, g is not None),
        grid=(heads,),
        in_specs=specs,
        out_specs=wspec,
        out_shape=jax.ShapeDtypeStruct(weights.shape, jnp.bfloat16),
        compiler_params=pltpu.CompilerParams(vmem_limit_bytes=56 << 20),
        cost_estimate=pl.CostEstimate(
            flops=12 * heads * local * hd * hid, bytes_accessed=30 << 20, transcendentals=0
        ),
        name="grad",
    )(*args)


def attention_kernel(head, chained, info_ref, win_ref, q_ref, k_ref, kh_ref, v_ref, vh_ref, *rest):
    out_ref = rest[-1]
    local, hd = q_ref.shape
    block = 256
    width = win_ref[head]
    anchor = info_ref[2]
    k_all = jnp.concatenate([kh_ref[...], k_ref[...]], axis=0)
    v_all = jnp.concatenate([vh_ref[...], v_ref[...]], axis=0)
    span = WIN + block
    for start in range(0, local, block):
        scores = mm(q_ref[start : start + block], k_all[start : start + span], 1, 1) * (
            hd ** (-0.5)
        )
        row = lax.broadcasted_iota(jnp.int32, (block, span), 0)
        colm = lax.broadcasted_iota(jnp.int32, (block, span), 1)
        back = row + WIN - colm
        live = (back >= 0) & (back < width) & (colm >= WIN - start - anchor)
        scores = jnp.where(live, scores, -1e30)
        peak = jnp.max(scores, axis=1, keepdims=True)
        expo = jnp.exp(scores - peak)
        probs = (expo * (1.0 / jnp.sum(expo, axis=1, keepdims=True))).astype(jnp.bfloat16)
        out_ref[start : start + block] = mm(probs, v_all[start : start + span], 1, 0)


def attention(head, prev, info, window, q, k, kh, v, vh, heads):
    local = q.shape[0]
    hd = q.shape[1] // heads
    smem = pl.BlockSpec(memory_space=pltpu.SMEM)
    col = pl.BlockSpec((local, hd), lambda i: (0, head))
    halo = pl.BlockSpec((WIN, hd), lambda i: (0, head))
    args = [info, window, q, k, kh, v, vh]
    specs = [smem, smem, col, col, halo, col, halo]
    aliases = {}
    if prev is not None:
        args.append(prev)
        specs.append(pl.BlockSpec(memory_space=pl.ANY))
        aliases = {len(args) - 1: 0}
    return pl.pallas_call(
        functools.partial(attention_kernel, head, prev is not None),
        grid=(1,),
        in_specs=specs,
        out_specs=col,
        out_shape=jax.ShapeDtypeStruct(q.shape, jnp.float32),
        input_output_aliases=aliases,
        compiler_params=pltpu.CompilerParams(vmem_limit_bytes=40 << 20),
        cost_estimate=pl.CostEstimate(
            flops=6 * 4 * local * 768 * hd, bytes_accessed=8 << 20, transcendentals=0
        ),
        name="attend",
    )(*args)


def mix_kernel(info_ref, coef_ref, q_ref, attn_ref, w_ref, g_ref, out_ref, y_ref):
    position = info_ref[2] + lax.broadcasted_iota(jnp.int32, (q_ref.shape[0], 1), 0)
    for c in range(2):

        @pl.when(info_ref[c] != 0)
        def _():
            def weight(i):
                w = w_ref[0, i]
                if c:
                    w = w - coef_ref[0] * g_ref[0, i].astype(jnp.float32)
                return w.astype(jnp.bfloat16)

            q = q_ref[...]
            first = mm(q, weight(0), 1, 0)
            third = mm(q, weight(1), 1, 0)
            act = (first * jax.nn.sigmoid(first) * third).astype(jnp.bfloat16)
            y = mm(act, weight(2), 1, 1)
            mine = (position < info_ref[3]) == (c == 0)
            y_ref[...] = jnp.where(mine, y, y_ref[...])

    y = y_ref[...]
    mean = jnp.mean(y * y, axis=1, keepdims=True)
    out_ref[...] = (attn_ref[...] + y / jnp.sqrt(mean + epsilon)).astype(jnp.bfloat16)


def mix(info, coef, q, attn, weights, g):
    local = q.shape[0]
    heads, _, hd, hid = weights.shape
    wspec = pl.BlockSpec((1, 3, hd, hid), lambda h: (h, 0, 0, 0))
    smem = pl.BlockSpec(memory_space=pltpu.SMEM)
    col = pl.BlockSpec((local, hd), lambda h: (0, h))
    return pl.pallas_call(
        mix_kernel,
        grid=(heads,),
        in_specs=[smem, smem, col, col, wspec, wspec],
        out_specs=col,
        out_shape=jax.ShapeDtypeStruct(q.shape, jnp.bfloat16),
        scratch_shapes=[pltpu.VMEM((local, hd), jnp.float32)],
        compiler_params=pltpu.CompilerParams(vmem_limit_bytes=56 << 20),
        cost_estimate=pl.CostEstimate(
            flops=8 * heads * local * hd * hid, bytes_accessed=30 << 20, transcendentals=0
        ),
        name="mix",
    )(info, coef, q, attn, weights, g)


SHARES = (8, 4, 4)
STEPS = (1, 2, 2)
CHUNK = 256


class Link:
    def __init__(self, net, src, dst, to, gives):
        self.net, self.src, self.dst, self.to, self.gives = net, src, dst, to, gives
        self.kind = len(net.links)
        net.links.append(self)

    def copy(self, n, slot):
        return pltpu.make_async_remote_copy(
            src_ref=self.src(n),
            dst_ref=self.dst(n),
            send_sem=self.net.send.at[self.kind],
            recv_sem=self.net.recv.at[self.kind, slot],
            device_id={"seq": self.to},
            device_id_type=pl.DeviceIdType.MESH,
        )

    def start(self, n):
        @pl.when(self.gives)
        def _():
            self.copy(n, n).start()

    def wait(self, n):
        self.copy(n, n).wait_recv()

    def drain(self):
        @pl.when(self.gives)
        def _():
            self.copy(pl.ds(0, self.net.chunks), 0).wait_send()


def total(ref, at, parts):
    out = ref[at].astype(jnp.float32)
    for part in parts:
        out += part.astype(jnp.float32)
    return out.astype(ref.dtype)


def link_kinds(near):
    return 2 + (4 + 2 * (near - 1)) + 2 * (4 + 2 * (near - 1))


class Net:
    def __init__(self, mirror, near_size, far_size, g, out, acc, got, send, recv):
        self.links, self.stages = [], []
        self.send, self.recv = send, recv
        self.chunks, rows, width = g.shape
        half = rows // CORES
        fine = width // near_size
        me = lax.axis_index("seq")
        core = me % CORES
        near = (me // CORES) % near_size
        far = me // (CORES * near_size)
        line = far_size - 1 - far if mirror else far
        last = (5 * far_size - 1) // 8
        gives = line <= last
        step_core, step_near, step_line = STEPS

        def device(line_to, near_to, core_to):
            far_to = far_size - 1 - line_to if mirror else line_to
            return (far_to * near_size + near_to) * CORES + core_to

        def peer(d):
            return device(line, (near + d) % near_size, core)

        def piece(d):
            index = (near + d) % near_size
            return pl.ds(pl.multiple_of(index * fine, 128), fine)

        def rows_of(c, first, count):
            return pl.ds(pl.multiple_of(c * half + first, 16), count)

        other = 1 - core
        mate = device(line, near, other)
        swap = Link(self, lambda n: g.at[n, rows_of(other, 0, half)], lambda n: acc.at[n], mate, gives)
        join = Link(
            self,
            lambda n: out.at[n, rows_of(core, 0, half)],
            lambda n: out.at[n, rows_of(core, 0, half)],
            mate,
            me >= 0,
        )
        self.stage(0, swap.start)

        unit = half // sum(SHARES)
        count = [s * unit for s in SHARES]
        first = [sum(count[:i]) for i in range(3)]
        mid = last // 2
        ends = []
        starts = []

        def line_links(root, src, base, n_cols, final):
            left = Link(self, src, lambda n: got.at[0, n, base, n_cols], device(line + 1, near, core), line < root)
            right = Link(
                self, src, lambda n: got.at[1, n, base, n_cols], device(line - 1, near, core),
                (line > root) & gives,
            )
            out_right = Link(self, final, final, device(line + 1, near, core), (line >= root) & (line < far_size - 1))
            out_left = Link(self, final, final, device(line - 1, near, core), (line <= root) & (line > 0))
            return left, right, out_right, out_left

        def line_in(at, root, left, right, base, cols, done):
            depth = max(root, last - root)

            def begin(n):
                @pl.when(line == 0)
                def _():
                    left.start(n)

                @pl.when(line == last)
                def _():
                    right.start(n)

            def hop(k, n):
                if k < root:
                    @pl.when(line == k)
                    def _():
                        left.wait(n)
                        acc[n, base, cols] = total(acc, (n, base, cols), [got[0, n, base, cols]])
                        left.start(n)
                if last - k > root:
                    @pl.when(line == last - k)
                    def _():
                        right.wait(n)
                        acc[n, base, cols] = total(acc, (n, base, cols), [got[1, n, base, cols]])
                        right.start(n)

            def end(n):
                @pl.when(line == root)
                def _():
                    parts = []
                    if root > 0:
                        left.wait(n)
                        parts.append(got[0, n, base, cols])
                    if last > root:
                        right.wait(n)
                        parts.append(got[1, n, base, cols])
                    done(n, total(acc, (n, base, cols), parts))

            for k in range(1, depth):
                self.stage(at + k * step_line, functools.partial(hop, k))
            self.stage(at + depth * step_line, end)
            return begin, at + depth * step_line

        def line_out(at, root, out_right, out_left, then):
            def hop(k, n):
                if root + k < far_size:
                    @pl.when(line == root + k)
                    def _():
                        out_right.wait(n)
                        out_right.start(n)
                        then(n)
                if root - k >= 0:
                    @pl.when(line == root - k)
                    def _():
                        out_left.wait(n)
                        out_left.start(n)
                        then(n)

            depth = max(far_size - 1 - root, root)
            for k in range(1, depth + 1):
                self.stage(at + k * step_line, functools.partial(hop, k))
            return at + depth * step_line

        t = step_core

        if count[0]:
            base = pl.ds(first[0], count[0])
            wide = rows_of(core, first[0], count[0])
            mine = piece(0)
            spread = [
                Link(
                    self,
                    lambda n, d=d: acc.at[n, base, piece(d)],
                    lambda n, d=d: got.at[2, n, base, pl.ds((d - 1) * fine, fine)],
                    peer(d),
                    gives,
                )
                for d in range(1, near_size)
            ]
            final = lambda n: out.at[n, wide, mine]
            left, right, out_right, out_left = line_links(mid, lambda n: acc.at[n, base, mine], base, mine, final)
            fill = [Link(self, final, final, peer(d), me >= 0) for d in range(1, near_size)]
            starts += spread

            def give(n):
                for f in fill:
                    f.start(n)

            def done(n, value):
                out[n, wide, mine] = value
                out_right.start(n)
                out_left.start(n)
                give(n)

            begin, t1 = line_in(t + step_near, mid, left, right, base, mine, done)

            def gathered(n):
                @pl.when(gives)
                def _():
                    for s in spread:
                        s.wait(n)
                    acc[n, base, mine] = total(
                        acc, (n, base, mine),
                        [got[2, n, base, pl.ds((d - 1) * fine, fine)] for d in range(1, near_size)],
                    )
                    begin(n)

            self.stage(t + step_near, gathered)
            t1 = line_out(t1, mid, out_right, out_left, give) + step_near

            def filled(n):
                for d in range(1, near_size):
                    fill[d - 1].wait(n)

            self.stage(t1, filled)
            ends.append(t1)

        def whole(index, root):
            base = pl.ds(first[index], count[index])
            wide = rows_of(core, first[index], count[index])
            every = pl.ds(0, width)
            mine = piece(0)
            final = lambda n: out.at[n, wide, every]
            part = lambda n: out.at[n, wide, mine]
            left, right, out_right, out_left = line_links(root, lambda n: acc.at[n, base, every], base, every, final)
            spread = [
                Link(
                    self,
                    lambda n, d=d: acc.at[n, base, piece(d)],
                    lambda n, d=d: got.at[2, n, base, pl.ds((d - 1) * fine, fine)],
                    peer(d),
                    line == root,
                )
                for d in range(1, near_size)
            ]
            fill = [Link(self, part, part, peer(d), line == root) for d in range(1, near_size)]

            def done(n, value):
                acc[n, base, every] = value
                for s in spread:
                    s.start(n)

            begin, t1 = line_in(t, root, left, right, base, every, done)

            def gathered(n):
                @pl.when(line == root)
                def _():
                    for s in spread:
                        s.wait(n)
                    out[n, wide, mine] = total(
                        acc, (n, base, mine),
                        [got[2, n, base, pl.ds((d - 1) * fine, fine)] for d in range(1, near_size)],
                    )
                    for f in fill:
                        f.start(n)

            def filled(n):
                @pl.when(line == root)
                def _():
                    for f in fill:
                        f.wait(n)
                    out_right.start(n)
                    out_left.start(n)

            self.stage(t1 + step_near, gathered)
            self.stage(t1 + 2 * step_near, filled)
            t1 = line_out(t1 + 2 * step_near, root, out_right, out_left, lambda n: None)
            ends.append(t1)
            return begin

        begins = [whole(i, root) for i, root in ((1, mid), (2, last)) if count[i]]

        def paired(n):
            @pl.when(gives)
            def _():
                swap.wait(n)
                acc[n] = total(acc, (n,), [g[n, rows_of(core, 0, half)]])
                for s in starts:
                    s.start(n)
                for begin in begins:
                    begin(n)

        self.stage(t, paired)
        t = max(ends)
        self.stage(t, join.start)
        self.stage(t + step_core, join.wait)
        self.length = self.chunks + t + step_core

    def stage(self, at, fn):
        self.stages.append((at, fn))

    def advance(self, i, finish):
        end = max(at for at, _ in self.stages)
        for at, fn in sorted(self.stages, key=lambda s: -s[0]):
            n = i - at

            @pl.when((n >= 0) & (n < self.chunks))
            def _():
                fn(n)
                if at == end:
                    finish(n)

    def drain(self):
        for link in self.links:
            link.drain()


def greet(near_size, far_size):
    me = lax.axis_index("seq")
    strides = (1, CORES, CORES * near_size)
    sizes = (CORES, near_size, far_size)
    barrier = pltpu.get_barrier_semaphore()
    count = 0
    for stride, size in zip(strides, sizes):
        place = (me // stride) % size
        for d in range(1, size):
            pl.semaphore_signal(
                barrier,
                inc=1,
                device_id={"seq": me + ((place + d) % size - place) * stride},
                device_id_type=pl.DeviceIdType.MESH,
            )
            count += 1
    pl.semaphore_wait(barrier, count)


def reduce_kernel(mirror, near_size, far_size, g_ref, out_ref, sq_ref, acc, got, send, recv):
    greet(near_size, far_size)
    net = Net(mirror, near_size, far_size, g_ref, out_ref, acc, got, send, recv)
    sq_ref[...] = jnp.zeros_like(sq_ref)

    def finish(n):
        part = jnp.square(out_ref[n].astype(jnp.float32))
        sq_ref[...] += jnp.sum(part.reshape(-1, *sq_ref.shape), axis=0)

    @pl.loop(0, net.length)
    def _(i):
        net.advance(i, finish)

    net.drain()


def sizes_of_seq():
    chips = lax.axis_size("seq") // CORES
    near = 1
    while near * near * 4 <= chips:
        near *= 2
    return near, chips // near


def summed(ident, grads, total_count):
    near, far = sizes_of_seq()
    width = grads.shape[-1]
    flat = grads.reshape(-1, CHUNK, width)
    chunks = flat.shape[0]
    vmem = pl.BlockSpec(memory_space=pltpu.VMEM)
    kinds = link_kinds(near)
    out, squares = pl.pallas_call(
        functools.partial(reduce_kernel, ident == 1, near, far),
        in_specs=[vmem],
        out_specs=(vmem, vmem),
        out_shape=(
            jax.ShapeDtypeStruct(flat.shape, flat.dtype),
            jax.ShapeDtypeStruct((8, width), jnp.float32),
        ),
        scratch_shapes=[
            pltpu.VMEM((chunks, CHUNK // CORES, width), jnp.bfloat16),
            pltpu.VMEM((3, chunks, CHUNK // CORES, width), jnp.bfloat16),
            pltpu.SemaphoreType.DMA((kinds,)),
            pltpu.SemaphoreType.DMA((kinds, chunks)),
        ],
        compiler_params=pltpu.CompilerParams(
            collective_id=ident, has_side_effects=True, vmem_limit_bytes=58 << 20
        ),
        cost_estimate=pl.CostEstimate(
            flops=10**11, bytes_accessed=4 * flat.size, transcendentals=0
        ),
        name="reduce",
    )(flat)
    square = lax.psum(jnp.sum(squares), "head")
    factor = fast_rate / jnp.sqrt(square / total_count + epsilon)
    return out.reshape(grads.shape), factor


def per_device(queries, keys, values, targets, token_rate, window, split, fast_init):
    local = queries.shape[0]
    heads = fast_init.shape[0]
    count = lax.axis_size("seq")
    total_count = float(fast_init.size * lax.axis_size("head"))
    anchor = (lax.axis_index("seq") * local).astype(jnp.int32)
    edge = split[0]
    early = (anchor < edge).astype(jnp.int32)
    late = (anchor + local > edge).astype(jnp.int32)
    info = jnp.stack([early, late, anchor, edge])
    info_late = jnp.stack([late, late, anchor, edge])
    positions = anchor + jnp.arange(local, dtype=jnp.int32)[:, None]
    first_block = (positions < edge).astype(jnp.float32)

    forward = [(i, i + 1) for i in range(count - 1)]
    key_halo = lax.ppermute(keys[local - WIN :], "seq", forward)
    value_halo = lax.ppermute(values[local - WIN :], "seq", forward)

    zero = jnp.zeros((1,), jnp.float32)
    g0 = gradients(info, zero, keys, targets, token_rate * first_block, fast_init, None)
    g0, c0 = summed(0, g0, total_count)
    c0, key_halo, value_halo = lax.optimization_barrier((c0, key_halo, value_halo))
    attn = None
    for head in range(heads):
        attn = attention(
            head, attn, info, window, queries, keys, key_halo, values, value_halo, heads
        )
    coef = c0.reshape(1)
    g1 = gradients(
        info_late, coef, keys, targets, token_rate * (1.0 - first_block), fast_init, g0
    )
    g1, c1 = summed(1, g1, total_count)
    mixed = mix(info, coef, queries, attn, fast_init, g0)
    weights = fast_init - c0 * g0.astype(jnp.float32) - c1 * g1.astype(jnp.float32)
    return mixed, weights


def solution(mesh):
    return jax.shard_map(
        per_device,
        mesh=mesh,
        in_specs=(
            P("seq", "head"),
            P("seq", "head"),
            P("seq", "head"),
            P("seq", "head"),
            P("seq", "head"),
            P("head"),
            P(),
            P("head", None, None, None),
        ),
        out_specs=(P("seq", "head"), P("head", None, None, None)),
        check_vma=False,
    )
```

```python
import functools

import jax
import jax.numpy as jnp
from jax import lax
from jax.experimental import pallas as pl
from jax.experimental.pallas import tpu as pltpu
from jax.sharding import PartitionSpec as P

WIN = 512
fast_rate = 0.01
epsilon = 1e-06
CORES = 2


def mm(a, b, ca, cb):
    return lax.dot_general(
        a, b, (((ca,), (cb,)), ((), ())), preferred_element_type=jnp.float32
    )


SHARES = (8, 4, 4)
STEPS = (1, 2, 2)
CHUNK = 256


class Link:
    def __init__(self, net, src, dst, to, gives):
        self.net, self.src, self.dst, self.to, self.gives = net, src, dst, to, gives
        self.kind = len(net.links)
        net.links.append(self)

    def copy(self, n, slot):
        return pltpu.make_async_remote_copy(
            src_ref=self.src(n),
            dst_ref=self.dst(n),
            send_sem=self.net.send.at[self.kind],
            recv_sem=self.net.recv.at[self.kind, slot],
            device_id={"seq": self.to},
            device_id_type=pl.DeviceIdType.MESH,
        )

    def start(self, n):
        @pl.when(self.gives)
        def _():
            self.copy(n, n).start()

    def wait(self, n):
        self.copy(n, n).wait_recv()

    def drain(self):
        @pl.when(self.gives)
        def _():
            self.copy(pl.ds(0, self.net.chunks), 0).wait_send()


def total(ref, at, parts):
    out = ref[at].astype(jnp.float32)
    for part in parts:
        out += part.astype(jnp.float32)
    return out.astype(ref.dtype)


def link_kinds(near):
    return 2 + (4 + 2 * (near - 1)) + 2 * (4 + 2 * (near - 1))


class Net:
    def __init__(self, mirror, near_size, far_size, g, out, acc, got, send, recv):
        self.links, self.stages = [], []
        self.send, self.recv = send, recv
        self.chunks, rows, width = g.shape
        half = rows // CORES
        fine = width // near_size
        me = lax.axis_index("seq")
        core = me % CORES
        near = (me // CORES) % near_size
        far = me // (CORES * near_size)
        line = far_size - 1 - far if mirror else far
        last = (5 * far_size - 1) // 8
        gives = line <= last
        step_core, step_near, step_line = STEPS

        def device(line_to, near_to, core_to):
            far_to = far_size - 1 - line_to if mirror else line_to
            return (far_to * near_size + near_to) * CORES + core_to

        def peer(d):
            return device(line, (near + d) % near_size, core)

        def piece(d):
            index = (near + d) % near_size
            return pl.ds(pl.multiple_of(index * fine, 128), fine)

        def rows_of(c, first, count):
            return pl.ds(pl.multiple_of(c * half + first, 16), count)

        other = 1 - core
        mate = device(line, near, other)
        swap = Link(self, lambda n: g.at[n, rows_of(other, 0, half)], lambda n: acc.at[n], mate, gives)
        join = Link(
            self,
            lambda n: out.at[n, rows_of(core, 0, half)],
            lambda n: out.at[n, rows_of(core, 0, half)],
            mate,
            me >= 0,
        )
        self.stage(0, swap.start)

        unit = half // sum(SHARES)
        count = [s * unit for s in SHARES]
        first = [sum(count[:i]) for i in range(3)]
        mid = last // 2
        ends = []
        starts = []

        def line_links(root, src, base, n_cols, final):
            left = Link(self, src, lambda n: got.at[0, n, base, n_cols], device(line + 1, near, core), line < root)
            right = Link(
                self, src, lambda n: got.at[1, n, base, n_cols], device(line - 1, near, core),
                (line > root) & gives,
            )
            out_right = Link(self, final, final, device(line + 1, near, core), (line >= root) & (line < far_size - 1))
            out_left = Link(self, final, final, device(line - 1, near, core), (line <= root) & (line > 0))
            return left, right, out_right, out_left

        def line_in(at, root, left, right, base, cols, done):
            depth = max(root, last - root)

            def begin(n):
                @pl.when(line == 0)
                def _():
                    left.start(n)

                @pl.when(line == last)
                def _():
                    right.start(n)

            def hop(k, n):
                if k < root:
                    @pl.when(line == k)
                    def _():
                        left.wait(n)
                        acc[n, base, cols] = total(acc, (n, base, cols), [got[0, n, base, cols]])
                        left.start(n)
                if last - k > root:
                    @pl.when(line == last - k)
                    def _():
                        right.wait(n)
                        acc[n, base, cols] = total(acc, (n, base, cols), [got[1, n, base, cols]])
                        right.start(n)

            def end(n):
                @pl.when(line == root)
                def _():
                    parts = []
                    if root > 0:
                        left.wait(n)
                        parts.append(got[0, n, base, cols])
                    if last > root:
                        right.wait(n)
                        parts.append(got[1, n, base, cols])
                    done(n, total(acc, (n, base, cols), parts))

            for k in range(1, depth):
                self.stage(at + k * step_line, functools.partial(hop, k))
            self.stage(at + depth * step_line, end)
            return begin, at + depth * step_line

        def line_out(at, root, out_right, out_left, then):
            def hop(k, n):
                if root + k < far_size:
                    @pl.when(line == root + k)
                    def _():
                        out_right.wait(n)
                        out_right.start(n)
                        then(n)
                if root - k >= 0:
                    @pl.when(line == root - k)
                    def _():
                        out_left.wait(n)
                        out_left.start(n)
                        then(n)

            depth = max(far_size - 1 - root, root)
            for k in range(1, depth + 1):
                self.stage(at + k * step_line, functools.partial(hop, k))
            return at + depth * step_line

        t = step_core

        if count[0]:
            base = pl.ds(first[0], count[0])
            wide = rows_of(core, first[0], count[0])
            mine = piece(0)
            spread = [
                Link(
                    self,
                    lambda n, d=d: acc.at[n, base, piece(d)],
                    lambda n, d=d: got.at[2, n, base, pl.ds((d - 1) * fine, fine)],
                    peer(d),
                    gives,
                )
                for d in range(1, near_size)
            ]
            final = lambda n: out.at[n, wide, mine]
            left, right, out_right, out_left = line_links(mid, lambda n: acc.at[n, base, mine], base, mine, final)
            fill = [Link(self, final, final, peer(d), me >= 0) for d in range(1, near_size)]
            starts += spread

            def give(n):
                for f in fill:
                    f.start(n)

            def done(n, value):
                out[n, wide, mine] = value
                out_right.start(n)
                out_left.start(n)
                give(n)

            begin, t1 = line_in(t + step_near, mid, left, right, base, mine, done)

            def gathered(n):
                @pl.when(gives)
                def _():
                    for s in spread:
                        s.wait(n)
                    acc[n, base, mine] = total(
                        acc, (n, base, mine),
                        [got[2, n, base, pl.ds((d - 1) * fine, fine)] for d in range(1, near_size)],
                    )
                    begin(n)

            self.stage(t + step_near, gathered)
            t1 = line_out(t1, mid, out_right, out_left, give) + step_near

            def filled(n):
                for d in range(1, near_size):
                    fill[d - 1].wait(n)

            self.stage(t1, filled)
            ends.append(t1)

        def whole(index, root):
            base = pl.ds(first[index], count[index])
            wide = rows_of(core, first[index], count[index])
            every = pl.ds(0, width)
            mine = piece(0)
            final = lambda n: out.at[n, wide, every]
            part = lambda n: out.at[n, wide, mine]
            left, right, out_right, out_left = line_links(root, lambda n: acc.at[n, base, every], base, every, final)
            spread = [
                Link(
                    self,
                    lambda n, d=d: acc.at[n, base, piece(d)],
                    lambda n, d=d: got.at[2, n, base, pl.ds((d - 1) * fine, fine)],
                    peer(d),
                    line == root,
                )
                for d in range(1, near_size)
            ]
            fill = [Link(self, part, part, peer(d), line == root) for d in range(1, near_size)]

            def done(n, value):
                acc[n, base, every] = value
                for s in spread:
                    s.start(n)

            begin, t1 = line_in(t, root, left, right, base, every, done)

            def gathered(n):
                @pl.when(line == root)
                def _():
                    for s in spread:
                        s.wait(n)
                    out[n, wide, mine] = total(
                        acc, (n, base, mine),
                        [got[2, n, base, pl.ds((d - 1) * fine, fine)] for d in range(1, near_size)],
                    )
                    for f in fill:
                        f.start(n)

            def filled(n):
                @pl.when(line == root)
                def _():
                    for f in fill:
                        f.wait(n)
                    out_right.start(n)
                    out_left.start(n)

            self.stage(t1 + step_near, gathered)
            self.stage(t1 + 2 * step_near, filled)
            t1 = line_out(t1 + 2 * step_near, root, out_right, out_left, lambda n: None)
            ends.append(t1)
            return begin

        begins = [whole(i, root) for i, root in ((1, mid), (2, last)) if count[i]]

        def paired(n):
            @pl.when(gives)
            def _():
                swap.wait(n)
                acc[n] = total(acc, (n,), [g[n, rows_of(core, 0, half)]])
                for s in starts:
                    s.start(n)
                for begin in begins:
                    begin(n)

        self.stage(t, paired)
        t = max(ends)
        self.stage(t, join.start)
        self.stage(t + step_core, join.wait)
        self.length = self.chunks + t + step_core

    def stage(self, at, fn):
        self.stages.append((at, fn))

    def advance(self, i, finish):
        end = max(at for at, _ in self.stages)
        for at, fn in sorted(self.stages, key=lambda s: -s[0]):
            n = i - at

            @pl.when((n >= 0) & (n < self.chunks))
            def _():
                fn(n)
                if at == end:
                    finish(n)

    def drain(self):
        for link in self.links:
            link.drain()


BLOCK = 256
HALO_EVERY = 5


def sizes_of_seq():
    chips = lax.axis_size("seq") // CORES
    near = 1
    while near * near * 4 <= chips:
        near *= 2
    return near, chips // near


def greet(near_size, far_size):
    me = lax.axis_index("seq")
    strides = (1, CORES, CORES * near_size)
    sizes = (CORES, near_size, far_size)
    all_count = CORES * near_size * far_size
    barrier = pltpu.get_barrier_semaphore()
    targets = [{"seq": (me + d) % all_count} for d in (1, all_count - 1)]
    for stride, size in zip(strides, sizes):
        place = (me // stride) % size
        for d in range(1, size):
            targets.append({"seq": me + ((place + d) % size - place) * stride})
    mine = lax.axis_index("head")
    heads = lax.axis_size("head")
    for d in range(1, heads):
        targets.append({"head": (mine + d) % heads})
    for target in targets:
        pl.semaphore_signal(barrier, inc=1, device_id=target, device_id_type=pl.DeviceIdType.MESH)
    pl.semaphore_wait(barrier, len(targets))


def fast_output(x, wb, head):
    first = mm(x, wb[head, 0], 1, 0)
    third = mm(x, wb[head, 1], 1, 0)
    act = (first * jax.nn.sigmoid(first) * third).astype(jnp.bfloat16)
    y = mm(act, wb[head, 2], 1, 1)
    return y / jnp.sqrt(jnp.mean(y * y, axis=1, keepdims=True) + epsilon)


def share_squares(sq_all, sq_ref, sq_send, sq_recv):
    mine = lax.axis_index("head")
    heads = lax.axis_size("head")
    copies = []
    for d in range(1, heads):
        copies.append(
            pltpu.make_async_remote_copy(
                src_ref=sq_all.at[mine],
                dst_ref=sq_all.at[mine],
                send_sem=sq_send.at[d],
                recv_sem=sq_recv.at[d],
                device_id={"head": (mine + d) % heads},
                device_id_type=pl.DeviceIdType.MESH,
            )
        )
    for c in copies:
        c.start()
    for c in copies:
        c.wait()
    sq_ref[...] = jnp.sum(sq_all[...], axis=0)


def block_kernel(second, near_size, far_size, total_count, *refs):
    refs = list(refs)

    def take(count):
        out = refs[:count]
        del refs[:count]
        return out

    if second:
        edge_ref, rate_ref, sq_in, keys, queries, targets, weights, g_in, attn = take(9)
        sums, sq_ref, mixed = take(3)
    else:
        edge_ref, win_ref, rate_ref, keys, values, queries, targets, weights = take(8)
        sums, sq_ref, attn = take(3)
    kbuf, qbuf, tbuf, wbuf, wb, g, res, acc, got, dbuf, stage, sq_all = take(12)
    send, recv, sq_send, sq_recv, load, wload, out_sem, stage_sem = take(8)
    if second:
        gbuf, mstage, in_sem = take(3)
        pad = 0
    else:
        vbuf, halo_send, halo_recv = take(3)
        pad = WIN
    assert not refs

    heads = weights.shape[0]
    local, hd = qbuf.shape[1:]
    me = lax.axis_index("seq")
    count = lax.axis_size("seq")
    mine = lax.axis_index("head")
    anchor = me * local
    early = 8 * me < 5 * count
    late = 8 * (me + 1) > 3 * count
    works = late if second else early
    far = me // (CORES * near_size)
    line = far_size - 1 - far if second else far
    gives = line <= (5 * far_size - 1) // 8
    pieces = hd // CHUNK
    per = 3 * pieces
    blocks = local // BLOCK
    units = blocks * heads
    begin = (heads - 1) * (per - 1)
    edge = edge_ref[0]

    def columns(ref, h, rows=None):
        cols = pl.ds(pl.multiple_of(h * hd, 128), hd)
        return ref.at[pl.ds(0, local) if rows is None else rows, cols]

    def load_weights(h):
        copies = [pltpu.make_async_copy(weights.at[h], wbuf, wload.at[0])]
        if second:
            copies.append(
                pltpu.make_async_copy(g_in.at[pl.ds(pl.multiple_of(h * per, per), per)], gbuf, wload.at[1])
            )
        return copies

    def load_one(i, h):
        src = (keys, targets, queries, None if second else values)[i]
        dst = (kbuf, tbuf, qbuf, None if second else vbuf)[i]
        at = dst.at[h, pl.ds(pad, local)] if i in (0, 3) else dst.at[h]
        return pltpu.make_async_copy(columns(src, h), at, load.at[i, h])

    def place(u):
        return blocks - 1 - u // heads, u % heads

    def attn_block(u):
        block, h = place(u)
        rows = pl.ds(pl.multiple_of(block * BLOCK, BLOCK), BLOCK)
        return columns(attn, h, rows)

    def attn_in(u):
        return pltpu.make_async_copy(attn_block(u), stage.at[u % 2], in_sem.at[u % 2])

    def block_out(u):
        if second:
            block, h = place(u)
            rows = pl.ds(pl.multiple_of(block * BLOCK, BLOCK), BLOCK)
            return pltpu.make_async_copy(mstage.at[u % 2], columns(mixed, h, rows), stage_sem.at[u % 2])
        return pltpu.make_async_copy(stage.at[u % 2], attn_block(u), stage_sem.at[u % 2])

    for c in load_weights(0):
        c.start()
    for h in range(heads):
        for i in (0, 1, 2) if second else (0, 1, 2, 3):
            load_one(i, h).start()
    if second:
        attn_in(0).start()
    sq_all[mine] = jnp.zeros(sq_all.shape[1:], jnp.float32)

    @pl.when(gives & jnp.logical_not(works))
    def _():
        @pl.loop(0, g.shape[0])
        def _(n):
            g[n] = jnp.zeros(g.shape[1:], g.dtype)

    if not second:

        @pl.when(me == 0)
        def _():
            @pl.loop(0, heads)
            def _(h):
                kbuf[h, pl.ds(0, WIN)] = jnp.zeros((WIN, hd), kbuf.dtype)
                vbuf[h, pl.ds(0, WIN)] = jnp.zeros((WIN, hd), vbuf.dtype)

    greet(near_size, far_size)

    def halo(h):
        rows = pl.ds(local - WIN, WIN)
        out = []
        for i, (src, dst) in enumerate(((keys, kbuf), (values, vbuf))):
            out.append(
                pltpu.make_async_remote_copy(
                    src_ref=columns(src, h, rows),
                    dst_ref=dst.at[h, pl.ds(0, WIN)],
                    send_sem=halo_send.at[i],
                    recv_sem=halo_recv.at[i, h],
                    device_id={"seq": me + 1},
                    device_id_type=pl.DeviceIdType.MESH,
                )
            )
        return out

    netw = Net(second, near_size, far_size, g, res, acc, got, send, recv)

    def position(rows):
        return anchor + rows + lax.broadcasted_iota(jnp.int32, (BLOCK, 1), 0)

    def backward(h):
        for c in load_weights(h):
            c.wait()
        if second:
            coef = fast_rate / jnp.sqrt(jnp.sum(sq_in[...]) / total_count + epsilon)
        for j in range(3):
            for p in range(pieces):
                rows = pl.ds(p * CHUNK, CHUNK)
                w = wbuf[j, rows]
                if second:
                    w = w - coef * gbuf[j * pieces + p].astype(jnp.float32)
                wb[h, j, rows] = w.astype(jnp.bfloat16)

        @pl.when(h + 1 < heads)
        def _():
            for c in load_weights(h + 1):
                c.start()

        for k in (0, 1):
            load_one(k, h).wait()

        @pl.loop(0, blocks)
        def _(b):
            start = pl.multiple_of(b * BLOCK, BLOCK)
            rows = pl.ds(start, BLOCK)
            x = kbuf[h, pl.ds(pad + start, BLOCK)]
            rate = rate_ref[rows]
            column = lax.broadcasted_iota(jnp.int32, rate.shape, 1)
            scaled = jnp.sum(jnp.where(column == h, rate, 0.0), axis=1, keepdims=True)
            inside = (position(start) >= edge) if second else (position(start) < edge)
            scaled = scaled * jnp.where(inside, 1.0, 0.0)
            first = mm(x, wb[h, 0], 1, 0)
            third = mm(x, wb[h, 1], 1, 0)
            d_out = (-scaled * tbuf[h, rows].astype(jnp.float32)).astype(jnp.bfloat16)
            d_act = mm(d_out, wb[h, 2], 1, 0)
            sigma = jax.nn.sigmoid(first)
            swish = first * sigma
            dbuf[0, rows] = (d_act * third * sigma * (1.0 + first * (1.0 - sigma))).astype(jnp.bfloat16)
            dbuf[1, rows] = (d_act * swish).astype(jnp.bfloat16)
            dbuf[2, rows] = (swish * third).astype(jnp.bfloat16)
            dbuf[3, rows] = d_out

    def outer(h, j):
        left = kbuf[h, pl.ds(pad, local)] if j < 2 else dbuf[3]
        value = mm(left, dbuf[j], 0, 0).astype(jnp.bfloat16)
        for p in range(pieces):
            g[h * per + j * pieces + p] = value[p * CHUNK : (p + 1) * CHUNK]

    def attend(u):
        block, h = place(u)
        start = pl.multiple_of(block * BLOCK, BLOCK)
        slot = u % 2

        @pl.when(block == blocks - 1)
        def _():
            for k in (2, 3):
                load_one(k, h).wait()

            @pl.when(jnp.logical_not(early))
            def _():
                for k in (0, 1):
                    load_one(k, h).wait()

        @pl.when((block == WIN // BLOCK - 1) & (me > 0))
        def _():
            for c in halo(h):
                c.wait_recv()

        @pl.when(u >= 2)
        def _():
            block_out(u - 2).wait()

        span = WIN + BLOCK
        q = qbuf[h, pl.ds(start, BLOCK)]
        scores = mm(q, kbuf[h, pl.ds(start, span)], 1, 1) * (hd ** (-0.5))
        row = lax.broadcasted_iota(jnp.int32, (BLOCK, span), 0)
        colm = lax.broadcasted_iota(jnp.int32, (BLOCK, span), 1)
        back = row + WIN - colm
        live = (back >= 0) & (back < win_ref[h]) & (colm >= WIN - start - anchor)
        scores = jnp.where(live, scores, -1e30)
        peak = jnp.max(scores, axis=1, keepdims=True)
        expo = jnp.exp(scores - peak)
        probs = (expo * (1.0 / jnp.sum(expo, axis=1, keepdims=True))).astype(jnp.bfloat16)
        stage[slot] = mm(probs, vbuf[h, pl.ds(start, span)], 1, 0)

        @pl.when(early)
        def _():
            y = fast_output(q, wb, h)
            stage[slot] += jnp.where(position(start) < edge, y, 0.0)

        block_out(u).start()

    def combine(u):
        block, h = place(u)
        start = pl.multiple_of(block * BLOCK, BLOCK)
        slot = u % 2

        @pl.when(u + 1 < units)
        def _():
            attn_in(u + 1).start()

        attn_in(u).wait()

        @pl.when(block == blocks - 1)
        def _():
            load_one(2, h).wait()

            @pl.when(jnp.logical_not(late))
            def _():
                for k in (0, 1):
                    load_one(k, h).wait()

        @pl.when(u >= 2)
        def _():
            block_out(u - 2).wait()

        @pl.when(late)
        def _():
            y = fast_output(qbuf[h, pl.ds(start, BLOCK)], wb, h)
            mstage[slot] = (stage[slot] + jnp.where(position(start) >= edge, y, 0.0)).astype(jnp.bfloat16)

        @pl.when(jnp.logical_not(late))
        def _():
            mstage[slot] = stage[slot].astype(jnp.bfloat16)

        block_out(u).start()

    def put(n):
        return pltpu.make_async_copy(res.at[n], sums.at[n], out_sem.at[0])

    def finish(n):
        put(n).start()
        part = jnp.square(res[n].astype(jnp.float32))
        sq_all[mine] += jnp.sum(part.reshape(-1, *sq_all.shape[1:]), axis=0)

    @pl.loop(0, max(netw.length, begin + units))
    def _(i):
        h = i // per

        if not second:

            @pl.when((i % HALO_EVERY == 0) & (i // HALO_EVERY < heads) & (me < count - 1))
            def _():
                for c in halo(i // HALO_EVERY):
                    c.start()

        @pl.when((h < heads) & works)
        def _():
            for j in range(3):

                @pl.when(i % per == j * pieces)
                def _():
                    if j == 0:
                        backward(h)
                    outer(h, j)

        netw.advance(i, finish)
        u = i - begin

        @pl.when((u >= 0) & (u < units))
        def _():
            (combine if second else attend)(u)

    netw.drain()
    share_squares(sq_all, sq_ref, sq_send, sq_recv)
    if not second:

        @pl.when(me < count - 1)
        def _():
            for i, buf in enumerate((kbuf, vbuf)):
                every = buf.at[pl.ds(0, heads), pl.ds(0, WIN)]
                pltpu.make_async_remote_copy(
                    src_ref=every, dst_ref=every, send_sem=halo_send.at[i], recv_sem=halo_recv.at[i, 0],
                    device_id={"seq": me + 1}, device_id_type=pl.DeviceIdType.MESH,
                ).wait_send()

    @pl.when(jnp.logical_not(works))
    def _():
        for c in load_weights(0):
            c.wait()

    for u in (units - 2, units - 1):
        block_out(u).wait()
    pltpu.make_async_copy(res, sums, out_sem.at[0]).wait()


def block_step(second, arrays, total_count):
    near, far = sizes_of_seq()
    if second:
        edge, rate, sq_in, keys, queries, targets, weights, g_in, attn = arrays
    else:
        edge, window, rate, keys, values, queries, targets, weights = arrays
    heads, _, hd, hid = weights.shape
    local = keys.shape[0]
    chunks = heads * 3 * hd // CHUNK
    vmem = pl.BlockSpec(memory_space=pltpu.VMEM)
    smem = pl.BlockSpec(memory_space=pltpu.SMEM)
    hbm = pl.BlockSpec(memory_space=pl.ANY)
    half = CHUNK // CORES
    kinds = link_kinds(near)
    ranks = lax.axis_size("head")
    dma = pltpu.SemaphoreType.DMA
    bf16, f32 = jnp.bfloat16, jnp.float32
    pad = 0 if second else WIN
    scratch = [
        pltpu.VMEM((heads, pad + local, hd), bf16),
        pltpu.VMEM((heads, local, hd), bf16),
        pltpu.VMEM((heads, local, hd), bf16),
        pltpu.VMEM((3, hd, hid), f32),
        pltpu.VMEM((heads, 3, hd, hid), bf16),
        pltpu.VMEM((chunks, CHUNK, hid), bf16),
        pltpu.VMEM((chunks, CHUNK, hid), bf16),
        pltpu.VMEM((chunks, half, hid), bf16),
        pltpu.VMEM((3, chunks, half, hid), bf16),
        pltpu.VMEM((4, local, hd), bf16),
        pltpu.VMEM((2, BLOCK, hd), f32),
        pltpu.VMEM((ranks, 8, hid), f32),
        dma((kinds,)),
        dma((kinds, chunks)),
        dma((ranks,)),
        dma((ranks,)),
        dma((4, heads)),
        dma((2,)),
        dma((1,)),
        dma((2,)),
    ]
    if second:
        scratch += [pltpu.VMEM((3 * hd // CHUNK, CHUNK, hid), bf16), pltpu.VMEM((2, BLOCK, hd), bf16), dma((2,))]
        in_specs = [smem, vmem, vmem, hbm, hbm, hbm, hbm, hbm, hbm]
        wide = jax.ShapeDtypeStruct(keys.shape, bf16)
    else:
        scratch += [pltpu.VMEM((heads, pad + local, hd), bf16), dma((2,)), dma((2, heads))]
        in_specs = [smem, smem, vmem, hbm, hbm, hbm, hbm, hbm]
        wide = jax.ShapeDtypeStruct(keys.shape, f32)
    return pl.pallas_call(
        functools.partial(block_kernel, second, near, far, total_count),
        in_specs=in_specs,
        out_specs=(hbm, vmem, hbm),
        out_shape=(
            jax.ShapeDtypeStruct((chunks, CHUNK, hid), bf16),
            jax.ShapeDtypeStruct((8, hid), f32),
            wide,
        ),
        scratch_shapes=scratch,
        compiler_params=pltpu.CompilerParams(
            collective_id=int(second), has_side_effects=True, vmem_limit_bytes=67043328
        ),
        cost_estimate=pl.CostEstimate(flops=10**11, bytes_accessed=60 << 20, transcendentals=0),
        name="second" if second else "first",
    )(*arrays)


def renew_kernel(total_count, sq0_ref, sq1_ref, w_ref, g0_ref, g1_ref, out_ref):
    coef = [
        fast_rate / jnp.sqrt(jnp.sum(s[...]) / total_count + epsilon) for s in (sq0_ref, sq1_ref)
    ]
    out_ref[...] = (
        w_ref[...] - coef[0] * g0_ref[...].astype(jnp.float32) - coef[1] * g1_ref[...].astype(jnp.float32)
    )


def renew(total_count, sq0, sq1, weights, g0, g1):
    rows = 3 * weights.shape[2]
    flat = (-1, weights.shape[-1])
    w = weights.reshape(flat)
    small = pl.BlockSpec(sq0.shape, lambda i: (0, 0))
    tile = pl.BlockSpec((rows, w.shape[1]), lambda i: (i, 0))
    return pl.pallas_call(
        functools.partial(renew_kernel, total_count),
        grid=(w.shape[0] // rows,),
        in_specs=[small, small, tile, tile, tile],
        out_specs=tile,
        out_shape=jax.ShapeDtypeStruct(w.shape, jnp.float32),
        compiler_params=pltpu.CompilerParams(vmem_limit_bytes=40 << 20),
        cost_estimate=pl.CostEstimate(flops=4 * w.size, bytes_accessed=12 * w.size, transcendentals=0),
        name="renew",
    )(sq0, sq1, w, g0.reshape(flat), g1.reshape(flat)).reshape(weights.shape)


def per_device(queries, keys, values, targets, token_rate, window, split, fast_init):
    total_count = float(fast_init.size * lax.axis_size("head"))
    g0, sq0, attn = block_step(
        False, (split, window, token_rate, keys, values, queries, targets, fast_init), total_count
    )
    g1, sq1, mixed = block_step(
        True, (split, token_rate, sq0, keys, queries, targets, fast_init, g0, attn), total_count
    )
    return mixed, renew(total_count, sq0, sq1, fast_init, g0, g1)


def solution(mesh):
    return jax.shard_map(
        per_device,
        mesh=mesh,
        in_specs=(
            P("seq", "head"),
            P("seq", "head"),
            P("seq", "head"),
            P("seq", "head"),
            P("seq", "head"),
            P("head"),
            P(),
            P("head", None, None, None),
        ),
        out_specs=(P("seq", "head"), P("head", None, None, None)),
        check_vma=False,
    )
```

```python
import functools

import jax
import jax.numpy as jnp
from jax import lax
from jax.experimental import pallas as pl
from jax.experimental.pallas import tpu as pltpu
from jax.sharding import PartitionSpec as P

WIN = 512
fast_rate = 0.01
epsilon = 1e-06
CORES = 2


def mm(a, b, ca, cb):
    return lax.dot_general(
        a, b, (((ca,), (cb,)), ((), ())), preferred_element_type=jnp.float32
    )


SHARES = ((8, 4, 4), (8, 4, 4))
STEPS = ((1, 2, 2), (1, 2, 2))
CHUNK = 256


class Link:
    def __init__(self, net, src, dst, to, gives):
        self.net, self.src, self.dst, self.to, self.gives = net, src, dst, to, gives
        self.kind = len(net.links)
        net.links.append(self)

    def copy(self, n, slot):
        return pltpu.make_async_remote_copy(
            src_ref=self.src(n),
            dst_ref=self.dst(n),
            send_sem=self.net.send.at[self.kind],
            recv_sem=self.net.recv.at[self.kind, slot],
            device_id={"seq": self.to},
            device_id_type=pl.DeviceIdType.MESH,
        )

    def start(self, n):
        @pl.when(self.gives)
        def _():
            self.copy(n, n).start()

    def wait(self, n):
        self.copy(n, n).wait_recv()

    def drain(self):
        @pl.when(self.gives)
        def _():
            self.copy(pl.ds(0, self.net.chunks), 0).wait_send()


def total(ref, at, parts):
    out = ref[at].astype(jnp.float32)
    for part in parts:
        out += part.astype(jnp.float32)
    return out.astype(ref.dtype)


def link_kinds(near):
    return 2 + (4 + 2 * (near - 1)) + 2 * (4 + 2 * (near - 1))


class Net:
    def __init__(self, mirror, near_size, far_size, g, out, acc, got, send, recv):
        self.links, self.stages = [], []
        self.send, self.recv = send, recv
        self.chunks, rows, width = g.shape
        half = rows // CORES
        fine = width // near_size
        me = lax.axis_index("seq")
        core = me % CORES
        near = (me // CORES) % near_size
        far = me // (CORES * near_size)
        line = far_size - 1 - far if mirror else far
        last = (5 * far_size - 1) // 8
        gives = line <= last
        step_core, step_near, step_line = STEPS[mirror]

        def device(line_to, near_to, core_to):
            far_to = far_size - 1 - line_to if mirror else line_to
            return (far_to * near_size + near_to) * CORES + core_to

        def peer(d):
            return device(line, (near + d) % near_size, core)

        def piece(d):
            index = (near + d) % near_size
            return pl.ds(pl.multiple_of(index * fine, 128), fine)

        def rows_of(c, first, count):
            return pl.ds(pl.multiple_of(c * half + first, 16), count)

        other = 1 - core
        mate = device(line, near, other)
        swap = Link(self, lambda n: g.at[n, rows_of(other, 0, half)], lambda n: acc.at[n], mate, gives)
        join = Link(
            self,
            lambda n: out.at[n, rows_of(core, 0, half)],
            lambda n: out.at[n, rows_of(core, 0, half)],
            mate,
            me >= 0,
        )
        self.stage(0, swap.start)

        shares = SHARES[mirror]
        unit = half // sum(shares)
        count = [s * unit for s in shares]
        first = [sum(count[:i]) for i in range(3)]
        mid = last // 2
        ends = []
        starts = []

        def line_links(root, src, base, n_cols, final):
            left = Link(self, src, lambda n: got.at[0, n, base, n_cols], device(line + 1, near, core), line < root)
            right = Link(
                self, src, lambda n: got.at[1, n, base, n_cols], device(line - 1, near, core),
                (line > root) & gives,
            )
            out_right = Link(self, final, final, device(line + 1, near, core), (line >= root) & (line < far_size - 1))
            out_left = Link(self, final, final, device(line - 1, near, core), (line <= root) & (line > 0))
            return left, right, out_right, out_left

        def line_in(at, root, left, right, base, cols, done):
            depth = max(root, last - root)

            def begin(n):
                @pl.when(line == 0)
                def _():
                    left.start(n)

                @pl.when(line == last)
                def _():
                    right.start(n)

            def hop(k, n):
                if k < root:
                    @pl.when(line == k)
                    def _():
                        left.wait(n)
                        acc[n, base, cols] = total(acc, (n, base, cols), [got[0, n, base, cols]])
                        left.start(n)
                if last - k > root:
                    @pl.when(line == last - k)
                    def _():
                        right.wait(n)
                        acc[n, base, cols] = total(acc, (n, base, cols), [got[1, n, base, cols]])
                        right.start(n)

            def end(n):
                @pl.when(line == root)
                def _():
                    parts = []
                    if root > 0:
                        left.wait(n)
                        parts.append(got[0, n, base, cols])
                    if last > root:
                        right.wait(n)
                        parts.append(got[1, n, base, cols])
                    done(n, total(acc, (n, base, cols), parts))

            for k in range(1, depth):
                self.stage(at + k * step_line, functools.partial(hop, k))
            self.stage(at + depth * step_line, end)
            return begin, at + depth * step_line

        def line_out(at, root, out_right, out_left, then):
            def hop(k, n):
                if root + k < far_size:
                    @pl.when(line == root + k)
                    def _():
                        out_right.wait(n)
                        out_right.start(n)
                        then(n)
                if root - k >= 0:
                    @pl.when(line == root - k)
                    def _():
                        out_left.wait(n)
                        out_left.start(n)
                        then(n)

            depth = max(far_size - 1 - root, root)
            for k in range(1, depth + 1):
                self.stage(at + k * step_line, functools.partial(hop, k))
            return at + depth * step_line

        t = step_core

        if count[0]:
            base = pl.ds(first[0], count[0])
            wide = rows_of(core, first[0], count[0])
            mine = piece(0)
            spread = [
                Link(
                    self,
                    lambda n, d=d: acc.at[n, base, piece(d)],
                    lambda n, d=d: got.at[2, n, base, pl.ds((d - 1) * fine, fine)],
                    peer(d),
                    gives,
                )
                for d in range(1, near_size)
            ]
            final = lambda n: out.at[n, wide, mine]
            left, right, out_right, out_left = line_links(mid, lambda n: acc.at[n, base, mine], base, mine, final)
            fill = [Link(self, final, final, peer(d), me >= 0) for d in range(1, near_size)]
            starts += spread

            def give(n):
                for f in fill:
                    f.start(n)

            def done(n, value):
                out[n, wide, mine] = value
                out_right.start(n)
                out_left.start(n)
                give(n)

            begin, t1 = line_in(t + step_near, mid, left, right, base, mine, done)

            def gathered(n):
                @pl.when(gives)
                def _():
                    for s in spread:
                        s.wait(n)
                    acc[n, base, mine] = total(
                        acc, (n, base, mine),
                        [got[2, n, base, pl.ds((d - 1) * fine, fine)] for d in range(1, near_size)],
                    )
                    begin(n)

            self.stage(t + step_near, gathered)
            t1 = line_out(t1, mid, out_right, out_left, give) + step_near

            def filled(n):
                for d in range(1, near_size):
                    fill[d - 1].wait(n)

            self.stage(t1, filled)
            ends.append(t1)

        def whole(index, root):
            base = pl.ds(first[index], count[index])
            wide = rows_of(core, first[index], count[index])
            every = pl.ds(0, width)
            mine = piece(0)
            final = lambda n: out.at[n, wide, every]
            part = lambda n: out.at[n, wide, mine]
            left, right, out_right, out_left = line_links(root, lambda n: acc.at[n, base, every], base, every, final)
            spread = [
                Link(
                    self,
                    lambda n, d=d: acc.at[n, base, piece(d)],
                    lambda n, d=d: got.at[2, n, base, pl.ds((d - 1) * fine, fine)],
                    peer(d),
                    line == root,
                )
                for d in range(1, near_size)
            ]
            fill = [Link(self, part, part, peer(d), line == root) for d in range(1, near_size)]

            def done(n, value):
                acc[n, base, every] = value
                for s in spread:
                    s.start(n)

            begin, t1 = line_in(t, root, left, right, base, every, done)

            def gathered(n):
                @pl.when(line == root)
                def _():
                    for s in spread:
                        s.wait(n)
                    out[n, wide, mine] = total(
                        acc, (n, base, mine),
                        [got[2, n, base, pl.ds((d - 1) * fine, fine)] for d in range(1, near_size)],
                    )
                    for f in fill:
                        f.start(n)

            def filled(n):
                @pl.when(line == root)
                def _():
                    for f in fill:
                        f.wait(n)
                    out_right.start(n)
                    out_left.start(n)

            self.stage(t1 + step_near, gathered)
            self.stage(t1 + 2 * step_near, filled)
            t1 = line_out(t1 + 2 * step_near, root, out_right, out_left, lambda n: None)
            ends.append(t1)
            return begin

        begins = [whole(i, root) for i, root in ((1, mid), (2, last)) if count[i]]

        def paired(n):
            @pl.when(gives)
            def _():
                swap.wait(n)
                acc[n] = total(acc, (n,), [g[n, rows_of(core, 0, half)]])
                for s in starts:
                    s.start(n)
                for begin in begins:
                    begin(n)

        self.stage(t, paired)
        t = max(ends)
        self.stage(t, join.start)
        self.stage(t + step_core, join.wait)
        self.length = self.chunks + t + step_core

    def stage(self, at, fn):
        self.stages.append((at, fn))

    def advance(self, i, finish):
        end = max(at for at, _ in self.stages)
        for at, fn in sorted(self.stages, key=lambda s: -s[0]):
            n = i - at

            @pl.when((n >= 0) & (n < self.chunks))
            def _():
                fn(n)
                if at == end:
                    finish(n)

    def drain(self):
        for link in self.links:
            link.drain()


BLOCK = 256
RENEW_STEPS = 4
HALO_PIECES = 8
HALO_LEAD = 4
NEAR_AT = 19
NEAR_EVERY = 2


def sizes_of_seq():
    chips = lax.axis_size("seq") // CORES
    near = 1
    while near * near * 4 <= chips:
        near *= 2
    return near, chips // near


def greet(near_size, far_size):
    me = lax.axis_index("seq")
    strides = (1, CORES, CORES * near_size)
    sizes = (CORES, near_size, far_size)
    all_count = CORES * near_size * far_size
    barrier = pltpu.get_barrier_semaphore()
    targets = [{"seq": (me + d) % all_count} for d in (1, all_count - 1)]
    for stride, size in zip(strides, sizes):
        place = (me // stride) % size
        for d in range(1, size):
            targets.append({"seq": me + ((place + d) % size - place) * stride})
    mine = lax.axis_index("head")
    heads = lax.axis_size("head")
    for d in range(1, heads):
        targets.append({"head": (mine + d) % heads})
    for target in targets:
        pl.semaphore_signal(barrier, inc=1, device_id=target, device_id_type=pl.DeviceIdType.MESH)
    pl.semaphore_wait(barrier, len(targets))


def fast_output(x, wb, head):
    first = mm(x, wb[head, 0], 1, 0)
    third = mm(x, wb[head, 1], 1, 0)
    act = (first * jax.nn.sigmoid(first) * third).astype(jnp.bfloat16)
    y = mm(act, wb[head, 2], 1, 1)
    return y / jnp.sqrt(jnp.mean(y * y, axis=1, keepdims=True) + epsilon)


def share_squares(sq_all, sq_ref, sq_send, sq_recv):
    mine = lax.axis_index("head")
    heads = lax.axis_size("head")
    copies = []
    for d in range(1, heads):
        copies.append(
            pltpu.make_async_remote_copy(
                src_ref=sq_all.at[mine],
                dst_ref=sq_all.at[mine],
                send_sem=sq_send.at[d],
                recv_sem=sq_recv.at[d],
                device_id={"head": (mine + d) % heads},
                device_id_type=pl.DeviceIdType.MESH,
            )
        )
    for c in copies:
        c.start()
    for c in copies:
        c.wait()
    sq_ref[...] = jnp.sum(sq_all[...], axis=0)


def block_kernel(second, near_size, far_size, total_count, *refs):
    refs = list(refs)

    def take(count):
        out = refs[:count]
        del refs[:count]
        return out

    if second:
        edge_ref, win_ref, rate_ref, sq_in, keys, values, queries, targets, weights = take(9)
        g_in, attn, k_far, v_far = take(4)
        sums, sq_ref, mixed = take(3)
    else:
        edge_ref, win_ref, rate_ref, keys, values, queries, targets, weights = take(8)
        sums, sq_ref, attn, k_far, v_far = take(5)
    kbuf, qbuf, tbuf, wbuf, wb, g, res, acc, got, dbuf, stage, sq_all = take(12)
    send, recv, sq_send, sq_recv, load, wload, out_sem, stage_sem = take(8)
    if second:
        vbuf, gbuf, mstage, in_sem, far_sem = take(5)
    else:
        vbuf, halo_send, halo_recv, far_sem = take(4)
    pad = WIN
    assert not refs

    heads = weights.shape[0]
    local, hd = qbuf.shape[1:]
    me = lax.axis_index("seq")
    count = lax.axis_size("seq")
    mine = lax.axis_index("head")
    anchor = me * local
    early = 8 * me < 5 * count
    late = 8 * (me + 1) > 3 * count
    works = late if second else early
    far = me // (CORES * near_size)
    line = far_size - 1 - far if second else far
    gives = line <= (5 * far_size - 1) // 8
    pieces = hd // CHUNK
    per = 3 * pieces
    blocks = local // BLOCK
    units = blocks * heads
    begin = (heads - 1) * (per - 1)
    ahead = per - 3
    assert blocks % ahead == 0
    halo_blocks = WIN // BLOCK
    plain = (blocks - halo_blocks) * heads
    here = heads - heads // 2

    def far_copies(h):
        k = h - here
        pairs = [(kbuf.at[h, pl.ds(0, WIN)], k_far.at[k]), (vbuf.at[k if second else h, pl.ds(0, WIN)], v_far.at[k])]
        if second:
            pairs = [(b, a) for a, b in pairs]
            rows = pl.ds(0, WIN)
            pairs.append((columns(values, h, rows), vbuf.at[k, pl.ds(WIN, WIN)]))
        return [pltpu.make_async_copy(a, b, far_sem.at[i, k]) for i, (a, b) in enumerate(pairs)]

    def attention(q, v_all, h, start):
        span = WIN + BLOCK
        scores = mm(q, kbuf[h, pl.ds(start, span)], 1, 1) * (hd ** (-0.5))
        row = lax.broadcasted_iota(jnp.int32, (BLOCK, span), 0)
        colm = lax.broadcasted_iota(jnp.int32, (BLOCK, span), 1)
        back = row + WIN - colm
        live = (back >= 0) & (back < win_ref[h]) & (colm >= WIN - start - anchor)
        scores = jnp.where(live, scores, -1e30)
        peak = jnp.max(scores, axis=1, keepdims=True)
        expo = jnp.exp(scores - peak)
        probs = (expo * (1.0 / jnp.sum(expo, axis=1, keepdims=True))).astype(jnp.bfloat16)
        return mm(probs, v_all[pl.ds(start, span)], 1, 0)
    edge = edge_ref[0]

    def columns(ref, h, rows=None):
        cols = pl.ds(pl.multiple_of(h * hd, 128), hd)
        return ref.at[pl.ds(0, local) if rows is None else rows, cols]

    def load_weights(h):
        copies = [pltpu.make_async_copy(weights.at[h], wbuf, wload.at[0])]
        if second:
            copies.append(
                pltpu.make_async_copy(g_in.at[pl.ds(pl.multiple_of(h * per, per), per)], gbuf, wload.at[1])
            )
        return copies

    def load_one(i, h):
        src = (keys, targets, queries, None if second else values)[i]
        dst = (kbuf, tbuf, qbuf, None if second else vbuf)[i]
        at = dst.at[h, pl.ds(pad, local)] if i in (0, 3) else dst.at[h]
        return pltpu.make_async_copy(columns(src, h), at, load.at[i, h])

    def place(u):
        return blocks - 1 - u // heads, u % heads

    def block_of(ref, block, h):
        return columns(ref, h, pl.ds(pl.multiple_of(block * BLOCK, BLOCK), BLOCK))

    def attn_in(u):
        return pltpu.make_async_copy(block_of(attn, *place(u)), stage.at[u % 2], in_sem.at[u % 2])

    def block_out(block, h, slot):
        src, dst = (mstage, mixed) if second else (stage, attn)
        return pltpu.make_async_copy(src.at[slot], block_of(dst, block, h), stage_sem.at[slot])

    for c in load_weights(0):
        c.start()
    for h in range(heads):
        for i in (0, 1, 2) if second else (0, 1, 2, 3):
            load_one(i, h).start()
    if second:
        attn_in(0).start()
        for h in range(here, heads):
            for c in far_copies(h):
                c.start()
    sq_all[mine] = jnp.zeros(sq_all.shape[1:], jnp.float32)

    @pl.when(gives & jnp.logical_not(works))
    def _():
        @pl.loop(0, g.shape[0])
        def _(n):
            g[n] = jnp.zeros(g.shape[1:], g.dtype)

    if not second:

        @pl.when(me == 0)
        def _():
            @pl.loop(0, heads)
            def _(h):
                kbuf[h, pl.ds(0, WIN)] = jnp.zeros((WIN, hd), kbuf.dtype)
                vbuf[h, pl.ds(0, WIN)] = jnp.zeros((WIN, hd), vbuf.dtype)

    greet(near_size, far_size)

    def halo(h, first=0, size=WIN):
        rows = pl.ds(pl.multiple_of(local - WIN + first, 16), size)
        out = []
        for i, (src, dst) in enumerate(((keys, kbuf), (values, vbuf))):
            out.append(
                pltpu.make_async_remote_copy(
                    src_ref=columns(src, h, rows),
                    dst_ref=dst.at[h, pl.ds(first, size)],
                    send_sem=halo_send.at[i],
                    recv_sem=halo_recv.at[i, h],
                    device_id={"seq": me + 1},
                    device_id_type=pl.DeviceIdType.MESH,
                )
            )
        return out

    netw = Net(second, near_size, far_size, g, res, acc, got, send, recv)

    def position(rows):
        return anchor + rows + lax.broadcasted_iota(jnp.int32, (BLOCK, 1), 0)

    def prepare(h):
        for c in load_weights(h):
            c.wait()
        if second:
            coef = fast_rate / jnp.sqrt(jnp.sum(sq_in[...]) / total_count + epsilon)
        for j in range(3):
            for p in range(pieces):
                rows = pl.ds(p * CHUNK, CHUNK)
                w = wbuf[j, rows]
                if second:
                    w = w - coef * gbuf[j * pieces + p].astype(jnp.float32)
                wb[h, j, rows] = w.astype(jnp.bfloat16)

        @pl.when(h + 1 < heads)
        def _():
            for c in load_weights(h + 1):
                c.start()

    def backward(h, kind):
        @pl.when(kind == 0)
        def _():
            for k in (0, 1):
                load_one(k, h).wait()

        for turn in range(0, blocks, ahead):
            b = kind + turn
            start = pl.multiple_of(b * BLOCK, BLOCK)
            rows = pl.ds(start, BLOCK)
            x = kbuf[h, pl.ds(pad + start, BLOCK)]
            rate = rate_ref[pl.ds(h, 1), rows]
            down = lax.broadcasted_iota(jnp.int32, (BLOCK, BLOCK), 0)
            across = lax.broadcasted_iota(jnp.int32, (BLOCK, BLOCK), 1)
            scaled = jnp.sum(jnp.where(down == across, rate, 0.0), axis=1, keepdims=True)
            inside = (position(start) >= edge) if second else (position(start) < edge)
            scaled = scaled * jnp.where(inside, 1.0, 0.0)
            first = mm(x, wb[h, 0], 1, 0)
            third = mm(x, wb[h, 1], 1, 0)
            d_out = (-scaled * tbuf[h, rows].astype(jnp.float32)).astype(jnp.bfloat16)
            d_act = mm(d_out, wb[h, 2], 1, 0)
            sigma = jax.nn.sigmoid(first)
            swish = first * sigma
            dbuf[0, rows] = (d_act * third * sigma * (1.0 + first * (1.0 - sigma))).astype(jnp.bfloat16)
            dbuf[1, rows] = (d_act * swish).astype(jnp.bfloat16)
            dbuf[2, rows] = (swish * third).astype(jnp.bfloat16)
            dbuf[3, rows] = d_out

    def outer(h, j):
        left = kbuf[h, pl.ds(pad, local)] if j < 2 else dbuf[3]
        value = mm(left, dbuf[j], 0, 0).astype(jnp.bfloat16)
        for p in range(pieces):
            g[h * per + j * pieces + p] = value[p * CHUNK : (p + 1) * CHUNK]

    def attend(block, h, order):
        start = pl.multiple_of(block * BLOCK, BLOCK)
        slot = order % 2

        @pl.when(block == blocks - 1)
        def _():
            for k in (2, 3):
                load_one(k, h).wait()

            @pl.when(jnp.logical_not(early))
            def _():
                for k in (0, 1):
                    load_one(k, h).wait()

        @pl.when((block == halo_blocks - 1) & (h < here) & (me > 0))
        def _():
            for c in halo(h):
                c.wait_recv()

        @pl.when(order >= 2)
        def _():
            block_out(block, h, slot).wait()

        q = qbuf[h, pl.ds(start, BLOCK)]
        inside = (block >= halo_blocks) | (h < here)

        @pl.when(inside)
        def _():
            stage[slot] = attention(q, vbuf.at[h], h, start)

        @pl.when(jnp.logical_not(inside))
        def _():
            stage[slot] = jnp.zeros(stage.shape[1:], jnp.float32)

        @pl.when(early)
        def _():
            y = fast_output(q, wb, h)
            stage[slot] += jnp.where(position(start) < edge, y, 0.0)

        block_out(block, h, slot).start()

    def combine(u):
        block, h = place(u)
        start = pl.multiple_of(block * BLOCK, BLOCK)
        slot = u % 2

        @pl.when(u + 1 < units)
        def _():
            attn_in(u + 1).start()

        attn_in(u).wait()

        @pl.when(block == blocks - 1)
        def _():
            load_one(2, h).wait()

            @pl.when(jnp.logical_not(late))
            def _():
                for k in (0, 1):
                    load_one(k, h).wait()

        @pl.when(u >= 2)
        def _():
            block_out(block, h, slot).wait()

        if here < heads:

            @pl.when((block == halo_blocks - 1) & (h >= here))
            def _():
                for c in far_copies(h):
                    c.wait()

            @pl.when((block < halo_blocks) & (h >= here))
            def _():
                q = qbuf[h, pl.ds(start, BLOCK)]
                stage[slot] += attention(q, vbuf.at[h - here], h, start)

        @pl.when(late)
        def _():
            y = fast_output(qbuf[h, pl.ds(start, BLOCK)], wb, h)
            mstage[slot] = (stage[slot] + jnp.where(position(start) >= edge, y, 0.0)).astype(jnp.bfloat16)

        @pl.when(jnp.logical_not(late))
        def _():
            mstage[slot] = stage[slot].astype(jnp.bfloat16)

        block_out(block, h, slot).start()

    def put(n):
        return pltpu.make_async_copy(res.at[n], sums.at[n], out_sem.at[0])

    def finish(n):
        put(n).start()
        part = jnp.square(res[n].astype(jnp.float32))
        sq_all[mine] += jnp.sum(part.reshape(-1, *sq_all.shape[1:]), axis=0)

    def gradient(i):
        h = i // per
        kind = i % per

        @pl.when(h < heads)
        def _():
            @pl.when(kind < ahead)
            def _():
                backward(h, kind)

            for j in range(3):

                @pl.when(kind == ahead + j)
                def _():
                    outer(h, j)

        @pl.when((h < heads - 1) & (kind == per - 1))
        def _():
            prepare(h + 1)

    def send_halo(i):
        size = WIN // HALO_PIECES

        @pl.when((i < heads * HALO_PIECES) & (me < count - 1))
        def _():
            for c in halo(i // HALO_PIECES, pl.multiple_of((i % HALO_PIECES) * size, size), size):
                c.start()

    if not second:

        @pl.loop(0, HALO_LEAD)
        def _(i):
            send_halo(i)

    @pl.when(works)
    def _():
        prepare(0)

        @pl.loop(0, ahead)
        def _(i):
            gradient(i)

    if second:
        steps = [begin + units]
    else:
        near_at = max(NEAR_AT, begin + plain)
        steps = [begin + plain, near_at + NEAR_EVERY * (units - plain)]

    @pl.loop(0, max(netw.length, *steps))
    def _(i):
        if not second:
            send_halo(i + HALO_LEAD)

        @pl.when(works)
        def _():
            gradient(i + ahead)

        netw.advance(i, finish)
        u = i - begin
        if second:

            @pl.when((u >= 0) & (u < units))
            def _():
                combine(u)
        else:

            @pl.when((u >= 0) & (u < plain))
            def _():
                block, h = place(u)
                attend(block, h, u)

            v = i - near_at
            w = v // NEAR_EVERY

            @pl.when((v >= 0) & (v % NEAR_EVERY == 0) & (w < units - plain))
            def _():
                attend(halo_blocks - 1 - w % halo_blocks, w // halo_blocks, plain + w)

    netw.drain()
    share_squares(sq_all, sq_ref, sq_send, sq_recv)
    if not second:
        for h in range(here, heads):

            @pl.when(me > 0)
            def _():
                for c in halo(h):
                    c.wait_recv()

            for c in far_copies(h):
                c.start()
        for h in range(here, heads):
            for c in far_copies(h):
                c.wait()

        @pl.when(me < count - 1)
        def _():
            for i, buf in enumerate((kbuf, vbuf)):
                every = buf.at[pl.ds(0, heads), pl.ds(0, WIN)]
                pltpu.make_async_remote_copy(
                    src_ref=every, dst_ref=every, send_sem=halo_send.at[i], recv_sem=halo_recv.at[i, 0],
                    device_id={"seq": me + 1}, device_id_type=pl.DeviceIdType.MESH,
                ).wait_send()

    @pl.when(jnp.logical_not(works))
    def _():
        for c in load_weights(0):
            c.wait()

    for slot in range(2):
        block_out(0, 0, slot).wait()
    pltpu.make_async_copy(res, sums, out_sem.at[0]).wait()


def block_step(second, arrays, total_count):
    near, far = sizes_of_seq()
    if second:
        keys, weights = arrays[4], arrays[8]
    else:
        keys, weights = arrays[3], arrays[7]
    heads, _, hd, hid = weights.shape
    local = keys.shape[0]
    chunks = heads * 3 * hd // CHUNK
    vmem = pl.BlockSpec(memory_space=pltpu.VMEM)
    smem = pl.BlockSpec(memory_space=pltpu.SMEM)
    hbm = pl.BlockSpec(memory_space=pl.ANY)
    half = CHUNK // CORES
    kinds = link_kinds(near)
    ranks = lax.axis_size("head")
    dma = pltpu.SemaphoreType.DMA
    bf16, f32 = jnp.bfloat16, jnp.float32
    pad = WIN
    away = heads // 2
    far_shape = (max(away, 1), WIN, hd)
    scratch = [
        pltpu.VMEM((heads, pad + local, hd), bf16),
        pltpu.VMEM((heads, local, hd), bf16),
        pltpu.VMEM((heads, local, hd), bf16),
        pltpu.VMEM((3, hd, hid), f32),
        pltpu.VMEM((heads, 3, hd, hid), bf16),
        pltpu.VMEM((chunks, CHUNK, hid), bf16),
        pltpu.VMEM((chunks, CHUNK, hid), bf16),
        pltpu.VMEM((chunks, half, hid), bf16),
        pltpu.VMEM((3, chunks, half, hid), bf16),
        pltpu.VMEM((4, local, hd), bf16),
        pltpu.VMEM((2, BLOCK, hd), f32),
        pltpu.VMEM((ranks, 8, hid), f32),
        dma((kinds,)),
        dma((kinds, chunks)),
        dma((ranks,)),
        dma((ranks,)),
        dma((4, heads)),
        dma((2,)),
        dma((1,)),
        dma((2,)),
    ]
    if second:
        scratch += [
            pltpu.VMEM((max(away, 1), 2 * WIN, hd), bf16),
            pltpu.VMEM((3 * hd // CHUNK, CHUNK, hid), bf16),
            pltpu.VMEM((2, BLOCK, hd), bf16),
            dma((2,)),
            dma((3, max(away, 1))),
        ]
        in_specs = [smem, smem, vmem, vmem] + [hbm] * 9
        more = ()
        wide = jax.ShapeDtypeStruct(keys.shape, bf16)
    else:
        scratch += [
            pltpu.VMEM((heads, pad + local, hd), bf16),
            dma((2,)),
            dma((2, heads)),
            dma((2, max(away, 1))),
        ]
        more = (jax.ShapeDtypeStruct(far_shape, bf16),) * 2
        in_specs = [smem, smem, vmem, hbm, hbm, hbm, hbm, hbm]
        wide = jax.ShapeDtypeStruct(keys.shape, f32)
    return pl.pallas_call(
        functools.partial(block_kernel, second, near, far, total_count),
        in_specs=in_specs,
        out_specs=(hbm, vmem, hbm) + (hbm,) * len(more),
        out_shape=(
            jax.ShapeDtypeStruct((chunks, CHUNK, hid), bf16),
            jax.ShapeDtypeStruct((8, hid), f32),
            wide,
        )
        + more,
        scratch_shapes=scratch,
        compiler_params=pltpu.CompilerParams(
            collective_id=int(second), has_side_effects=True, vmem_limit_bytes=67043328
        ),
        cost_estimate=pl.CostEstimate(flops=10**11, bytes_accessed=60 << 20, transcendentals=0),
        name="second" if second else "first",
    )(*arrays)


def renew_kernel(total_count, sq0_ref, sq1_ref, w_ref, g0_ref, g1_ref, mixed_ref, out_ref, copy_ref):
    coef = [
        fast_rate / jnp.sqrt(jnp.sum(s[...]) / total_count + epsilon) for s in (sq0_ref, sq1_ref)
    ]
    out_ref[...] = (
        w_ref[...] - coef[0] * g0_ref[...].astype(jnp.float32) - coef[1] * g1_ref[...].astype(jnp.float32)
    )
    copy_ref[...] = mixed_ref[...]


def renew(total_count, sq0, sq1, weights, g0, g1, mixed):
    flat = (-1, weights.shape[-1])
    w = weights.reshape(flat)
    steps = RENEW_STEPS
    small = pl.BlockSpec(sq0.shape, lambda i: (0, 0))
    tile = pl.BlockSpec((w.shape[0] // steps, w.shape[1]), lambda i: (i, 0))
    rows = pl.BlockSpec((mixed.shape[0] // steps, mixed.shape[1]), lambda i: (i, 0))
    out, mixed = pl.pallas_call(
        functools.partial(renew_kernel, total_count),
        grid=(steps,),
        in_specs=[small, small, tile, tile, tile, rows],
        out_specs=(tile, rows),
        out_shape=(
            jax.ShapeDtypeStruct(w.shape, jnp.float32),
            jax.ShapeDtypeStruct(mixed.shape, mixed.dtype),
        ),
        compiler_params=pltpu.CompilerParams(vmem_limit_bytes=67043328),
        cost_estimate=pl.CostEstimate(flops=4 * w.size, bytes_accessed=16 * w.size, transcendentals=0),
        name="renew",
    )(sq0, sq1, w, g0.reshape(flat), g1.reshape(flat), mixed)
    return mixed, out.reshape(weights.shape)


def per_device(queries, keys, values, targets, token_rate, window, split, fast_init):
    total_count = float(fast_init.size * lax.axis_size("head"))
    g0, sq0, attn, k_far, v_far = block_step(
        False, (split, window, token_rate.T, keys, values, queries, targets, fast_init), total_count
    )
    g1, sq1, mixed = block_step(
        True,
        (split, window, token_rate.T, sq0, keys, values, queries, targets, fast_init, g0, attn, k_far, v_far),
        total_count,
    )
    return renew(total_count, sq0, sq1, fast_init, g0, g1, mixed)


def solution(mesh):
    return jax.shard_map(
        per_device,
        mesh=mesh,
        in_specs=(
            P("seq", "head"),
            P("seq", "head"),
            P("seq", "head"),
            P("seq", "head"),
            P("seq", "head"),
            P("head"),
            P(),
            P("head", None, None, None),
        ),
        out_specs=(P("seq", "head"), P("head", None, None, None)),
        check_vma=False,
    )
```

```python
import functools

import jax
import jax.numpy as jnp
from jax import lax
from jax.experimental import pallas as pl
from jax.experimental.pallas import tpu as pltpu
from jax.sharding import PartitionSpec as P

WIN = 512
fast_rate = 0.01
epsilon = 1e-06
CORES = 2


def mm(a, b, ca, cb):
    return lax.dot_general(
        a, b, (((ca,), (cb,)), ((), ())), preferred_element_type=jnp.float32
    )


SHARES = ((8, 4, 4), (8, 4, 4))
STEPS = ((2, 2, 2), (2, 2, 2))
CHUNK = 256


class Link:
    def __init__(self, net, src, dst, to, gives):
        self.net, self.src, self.dst, self.to, self.gives = net, src, dst, to, gives
        self.kind = len(net.links)
        net.links.append(self)

    def copy(self, n, slot):
        return pltpu.make_async_remote_copy(
            src_ref=self.src(n),
            dst_ref=self.dst(n),
            send_sem=self.net.send.at[self.kind],
            recv_sem=self.net.recv.at[self.kind, slot],
            device_id={"seq": self.to},
            device_id_type=pl.DeviceIdType.MESH,
        )

    def start(self, n):
        @pl.when(self.gives)
        def _():
            self.copy(n, n).start()

    def wait(self, n):
        self.copy(n, n).wait_recv()

    def drain(self):
        @pl.when(self.gives)
        def _():
            self.copy(pl.ds(0, self.net.chunks), 0).wait_send()


def total(ref, at, parts):
    out = ref[at].astype(jnp.float32)
    for part in parts:
        out += part.astype(jnp.float32)
    return out.astype(ref.dtype)


def link_kinds(near):
    return 2 + (4 + 2 * (near - 1)) + 2 * (4 + 2 * (near - 1))


class Net:
    def __init__(self, mirror, near_size, far_size, g, out, acc, got, send, recv):
        self.links, self.stages = [], []
        self.send, self.recv = send, recv
        self.chunks, rows, width = g.shape
        half = rows // CORES
        fine = width // near_size
        me = lax.axis_index("seq")
        core = me % CORES
        near = (me // CORES) % near_size
        far = me // (CORES * near_size)
        line = far_size - 1 - far if mirror else far
        last = (5 * far_size - 1) // 8
        gives = line <= last
        step_core, step_near, step_line = STEPS[mirror]

        def device(line_to, near_to, core_to):
            far_to = far_size - 1 - line_to if mirror else line_to
            return (far_to * near_size + near_to) * CORES + core_to

        def peer(d):
            return device(line, (near + d) % near_size, core)

        def piece(d):
            index = (near + d) % near_size
            return pl.ds(pl.multiple_of(index * fine, 128), fine)

        def rows_of(c, first, count):
            return pl.ds(pl.multiple_of(c * half + first, 16), count)

        other = 1 - core
        mate = device(line, near, other)
        swap = Link(self, lambda n: g.at[n, rows_of(other, 0, half)], lambda n: acc.at[n], mate, gives)
        join = Link(
            self,
            lambda n: out.at[n, rows_of(core, 0, half)],
            lambda n: out.at[n, rows_of(core, 0, half)],
            mate,
            me >= 0,
        )
        self.stage(0, swap.start)

        shares = SHARES[mirror]
        unit = half // sum(shares)
        count = [s * unit for s in shares]
        first = [sum(count[:i]) for i in range(3)]
        mid = last // 2
        ends = []
        starts = []

        def line_links(root, src, base, n_cols, final):
            left = Link(self, src, lambda n: got.at[0, n, base, n_cols], device(line + 1, near, core), line < root)
            right = Link(
                self, src, lambda n: got.at[1, n, base, n_cols], device(line - 1, near, core),
                (line > root) & gives,
            )
            out_right = Link(self, final, final, device(line + 1, near, core), (line >= root) & (line < far_size - 1))
            out_left = Link(self, final, final, device(line - 1, near, core), (line <= root) & (line > 0))
            return left, right, out_right, out_left

        def line_in(at, root, left, right, base, cols, done):
            depth = max(root, last - root)

            def begin(n):
                @pl.when(line == 0)
                def _():
                    left.start(n)

                @pl.when(line == last)
                def _():
                    right.start(n)

            def hop(k, n):
                if k < root:
                    @pl.when(line == k)
                    def _():
                        left.wait(n)
                        acc[n, base, cols] = total(acc, (n, base, cols), [got[0, n, base, cols]])
                        left.start(n)
                if last - k > root:
                    @pl.when(line == last - k)
                    def _():
                        right.wait(n)
                        acc[n, base, cols] = total(acc, (n, base, cols), [got[1, n, base, cols]])
                        right.start(n)

            def end(n):
                @pl.when(line == root)
                def _():
                    parts = []
                    if root > 0:
                        left.wait(n)
                        parts.append(got[0, n, base, cols])
                    if last > root:
                        right.wait(n)
                        parts.append(got[1, n, base, cols])
                    done(n, total(acc, (n, base, cols), parts))

            for k in range(1, depth):
                self.stage(at + k * step_line, functools.partial(hop, k))
            self.stage(at + depth * step_line, end)
            return begin, at + depth * step_line

        def line_out(at, root, out_right, out_left, then):
            def hop(k, n):
                if root + k < far_size:
                    @pl.when(line == root + k)
                    def _():
                        out_right.wait(n)
                        out_right.start(n)
                        then(n)
                if root - k >= 0:
                    @pl.when(line == root - k)
                    def _():
                        out_left.wait(n)
                        out_left.start(n)
                        then(n)

            depth = max(far_size - 1 - root, root)
            for k in range(1, depth + 1):
                self.stage(at + k * step_line, functools.partial(hop, k))
            return at + depth * step_line

        t = step_core

        if count[0]:
            base = pl.ds(first[0], count[0])
            wide = rows_of(core, first[0], count[0])
            mine = piece(0)
            spread = [
                Link(
                    self,
                    lambda n, d=d: acc.at[n, base, piece(d)],
                    lambda n, d=d: got.at[2, n, base, pl.ds((d - 1) * fine, fine)],
                    peer(d),
                    gives,
                )
                for d in range(1, near_size)
            ]
            final = lambda n: out.at[n, wide, mine]
            left, right, out_right, out_left = line_links(mid, lambda n: acc.at[n, base, mine], base, mine, final)
            fill = [Link(self, final, final, peer(d), me >= 0) for d in range(1, near_size)]
            starts += spread

            def give(n):
                for f in fill:
                    f.start(n)

            def done(n, value):
                out[n, wide, mine] = value
                out_right.start(n)
                out_left.start(n)
                give(n)

            begin, t1 = line_in(t + step_near, mid, left, right, base, mine, done)

            def gathered(n):
                @pl.when(gives)
                def _():
                    for s in spread:
                        s.wait(n)
                    acc[n, base, mine] = total(
                        acc, (n, base, mine),
                        [got[2, n, base, pl.ds((d - 1) * fine, fine)] for d in range(1, near_size)],
                    )
                    begin(n)

            self.stage(t + step_near, gathered)
            t1 = line_out(t1, mid, out_right, out_left, give) + step_near

            def filled(n):
                for d in range(1, near_size):
                    fill[d - 1].wait(n)

            self.stage(t1, filled)
            ends.append(t1)

        def whole(index, root):
            base = pl.ds(first[index], count[index])
            wide = rows_of(core, first[index], count[index])
            every = pl.ds(0, width)
            mine = piece(0)
            final = lambda n: out.at[n, wide, every]
            part = lambda n: out.at[n, wide, mine]
            left, right, out_right, out_left = line_links(root, lambda n: acc.at[n, base, every], base, every, final)
            spread = [
                Link(
                    self,
                    lambda n, d=d: acc.at[n, base, piece(d)],
                    lambda n, d=d: got.at[2, n, base, pl.ds((d - 1) * fine, fine)],
                    peer(d),
                    line == root,
                )
                for d in range(1, near_size)
            ]
            fill = [Link(self, part, part, peer(d), line == root) for d in range(1, near_size)]

            def done(n, value):
                acc[n, base, every] = value
                for s in spread:
                    s.start(n)

            begin, t1 = line_in(t, root, left, right, base, every, done)

            def gathered(n):
                @pl.when(line == root)
                def _():
                    for s in spread:
                        s.wait(n)
                    out[n, wide, mine] = total(
                        acc, (n, base, mine),
                        [got[2, n, base, pl.ds((d - 1) * fine, fine)] for d in range(1, near_size)],
                    )
                    for f in fill:
                        f.start(n)

            def filled(n):
                @pl.when(line == root)
                def _():
                    for f in fill:
                        f.wait(n)
                    out_right.start(n)
                    out_left.start(n)

            self.stage(t1 + step_near, gathered)
            self.stage(t1 + 2 * step_near, filled)
            t1 = line_out(t1 + 2 * step_near, root, out_right, out_left, lambda n: None)
            ends.append(t1)
            return begin

        begins = [whole(i, root) for i, root in ((1, mid), (2, last)) if count[i]]

        def paired(n):
            @pl.when(gives)
            def _():
                swap.wait(n)
                acc[n] = total(acc, (n,), [g[n, rows_of(core, 0, half)]])
                for s in starts:
                    s.start(n)
                for begin in begins:
                    begin(n)

        self.stage(t, paired)
        t = max(ends)
        self.stage(t, join.start)
        self.stage(t + step_core, join.wait)
        self.length = self.chunks + t + step_core

    def stage(self, at, fn):
        self.stages.append((at, fn))

    def advance(self, i, finish):
        end = max(at for at, _ in self.stages)
        for at, fn in sorted(self.stages, key=lambda s: -s[0]):
            n = i - at

            @pl.when((n >= 0) & (n < self.chunks))
            def _():
                fn(n)
                if at == end:
                    finish(n)

    def drain(self):
        for link in self.links:
            link.drain()


BLOCK = 256
RENEW_STEPS = 4
HALO_PIECES = 8
HALO_LEAD = 10
NEAR_AT = 19
NEAR_EVERY = 2


def sizes_of_seq():
    chips = lax.axis_size("seq") // CORES
    near = 1
    while near * near * 4 <= chips:
        near *= 2
    return near, chips // near


def greet(near_size, far_size):
    me = lax.axis_index("seq")
    strides = (1, CORES, CORES * near_size)
    sizes = (CORES, near_size, far_size)
    all_count = CORES * near_size * far_size
    barrier = pltpu.get_barrier_semaphore()
    targets = [{"seq": (me + d) % all_count} for d in (1, all_count - 1)]
    for stride, size in zip(strides, sizes):
        place = (me // stride) % size
        for d in range(1, size):
            targets.append({"seq": me + ((place + d) % size - place) * stride})
    mine = lax.axis_index("head")
    heads = lax.axis_size("head")
    for d in range(1, heads):
        targets.append({"head": (mine + d) % heads})
    for target in targets:
        pl.semaphore_signal(barrier, inc=1, device_id=target, device_id_type=pl.DeviceIdType.MESH)
    pl.semaphore_wait(barrier, len(targets))


def fast_output(x, wb, head):
    first = mm(x, wb[head, 0], 1, 0)
    third = mm(x, wb[head, 1], 1, 0)
    act = (first * jax.nn.sigmoid(first) * third).astype(jnp.bfloat16)
    y = mm(act, wb[head, 2], 1, 1)
    return y / jnp.sqrt(jnp.mean(y * y, axis=1, keepdims=True) + epsilon)


def share_squares(sq_all, sq_ref, sq_send, sq_recv):
    mine = lax.axis_index("head")
    heads = lax.axis_size("head")
    copies = []
    for d in range(1, heads):
        copies.append(
            pltpu.make_async_remote_copy(
                src_ref=sq_all.at[mine],
                dst_ref=sq_all.at[mine],
                send_sem=sq_send.at[d],
                recv_sem=sq_recv.at[d],
                device_id={"head": (mine + d) % heads},
                device_id_type=pl.DeviceIdType.MESH,
            )
        )
    for c in copies:
        c.start()
    for c in copies:
        c.wait()
    sq_ref[...] = jnp.sum(sq_all[...], axis=0)


def block_kernel(second, near_size, far_size, total_count, *refs):
    refs = list(refs)

    def take(count):
        out = refs[:count]
        del refs[:count]
        return out

    if second:
        edge_ref, win_ref, rate_ref, sq_in, keys, values, queries, targets, weights = take(9)
        g_in, attn = take(2)
        sums, sq_ref, mixed = take(3)
    else:
        edge_ref, win_ref, rate_ref, keys, values, queries, targets, weights = take(8)
        sums, sq_ref, attn = take(3)
    kbuf, qbuf, tbuf, wbuf, wb, g, res, acc, got, dbuf, stage, sq_all = take(12)
    send, recv, sq_send, sq_recv, load, wload, out_sem, stage_sem = take(8)
    vbuf, halo_send, halo_recv = take(3)
    if second:
        gbuf, mstage, in_sem, own_sem = take(4)
    pad = WIN
    assert not refs

    heads = weights.shape[0]
    local, hd = qbuf.shape[1:]
    me = lax.axis_index("seq")
    count = lax.axis_size("seq")
    mine = lax.axis_index("head")
    anchor = me * local
    early = 8 * me < 5 * count
    late = 8 * (me + 1) > 3 * count
    works = late if second else early
    far = me // (CORES * near_size)
    line = far_size - 1 - far if second else far
    gives = line <= (5 * far_size - 1) // 8
    pieces = hd // CHUNK
    per = 3 * pieces
    blocks = local // BLOCK
    units = blocks * heads
    begin = (heads - 1) * (per - 1)
    ahead = per - 3
    assert blocks % ahead == 0
    halo_blocks = WIN // BLOCK
    plain = (blocks - halo_blocks) * heads
    here = heads - heads // 2

    low, away = (here, heads - here) if second else (0, here)

    def own_values(h):
        k = h - low
        return pltpu.make_async_copy(columns(values, h, pl.ds(0, WIN)), vbuf.at[k, pl.ds(WIN, WIN)], own_sem.at[k])

    def attention(q, v_all, h, start):
        span = WIN + BLOCK
        scores = mm(q, kbuf[h, pl.ds(start, span)], 1, 1) * (hd ** (-0.5))
        row = lax.broadcasted_iota(jnp.int32, (BLOCK, span), 0)
        colm = lax.broadcasted_iota(jnp.int32, (BLOCK, span), 1)
        back = row + WIN - colm
        live = (back >= 0) & (back < win_ref[h]) & (colm >= WIN - start - anchor)
        scores = jnp.where(live, scores, -1e30)
        peak = jnp.max(scores, axis=1, keepdims=True)
        expo = jnp.exp(scores - peak)
        probs = (expo * (1.0 / jnp.sum(expo, axis=1, keepdims=True))).astype(jnp.bfloat16)
        return mm(probs, v_all[pl.ds(start, span)], 1, 0)
    edge = edge_ref[0]

    def columns(ref, h, rows=None):
        cols = pl.ds(pl.multiple_of(h * hd, 128), hd)
        return ref.at[pl.ds(0, local) if rows is None else rows, cols]

    def load_weights(h):
        copies = [pltpu.make_async_copy(weights.at[h], wbuf, wload.at[0])]
        if second:
            copies.append(
                pltpu.make_async_copy(g_in.at[pl.ds(pl.multiple_of(h * per, per), per)], gbuf, wload.at[1])
            )
        return copies

    def load_one(i, h):
        src = (keys, targets, queries, None if second else values)[i]
        dst = (kbuf, tbuf, qbuf, None if second else vbuf)[i]
        at = dst.at[h, pl.ds(pad, local)] if i in (0, 3) else dst.at[h]
        return pltpu.make_async_copy(columns(src, h), at, load.at[i, h])

    def place(u):
        return blocks - 1 - u // heads, u % heads

    def block_of(ref, block, h):
        return columns(ref, h, pl.ds(pl.multiple_of(block * BLOCK, BLOCK), BLOCK))

    def attn_in(u):
        return pltpu.make_async_copy(block_of(attn, *place(u)), stage.at[u % 2], in_sem.at[u % 2])

    def block_out(block, h, slot):
        src, dst = (mstage, mixed) if second else (stage, attn)
        return pltpu.make_async_copy(src.at[slot], block_of(dst, block, h), stage_sem.at[slot])

    for c in load_weights(0):
        c.start()
    for h in range(heads):
        for i in (0, 1, 2) if second else (0, 1, 2, 3):
            load_one(i, h).start()
    if second:
        attn_in(0).start()
        for h in range(here, heads):
            own_values(h).start()
    sq_all[mine] = jnp.zeros(sq_all.shape[1:], jnp.float32)

    @pl.when(gives & jnp.logical_not(works))
    def _():
        @pl.loop(0, g.shape[0])
        def _(n):
            g[n] = jnp.zeros(g.shape[1:], g.dtype)

    if away:

        @pl.when(me == 0)
        def _():
            @pl.loop(0, away)
            def _(k):
                kbuf[low + k, pl.ds(0, WIN)] = jnp.zeros((WIN, hd), kbuf.dtype)
                vbuf[k, pl.ds(0, WIN)] = jnp.zeros((WIN, hd), vbuf.dtype)

    greet(near_size, far_size)

    def halo(h, first=0, size=WIN):
        rows = pl.ds(pl.multiple_of(local - WIN + first, 16), size)
        out = []
        for i, (src, dst) in enumerate(((keys, kbuf.at[h]), (values, vbuf.at[h - low]))):
            out.append(
                pltpu.make_async_remote_copy(
                    src_ref=columns(src, h, rows),
                    dst_ref=dst.at[pl.ds(first, size)],
                    send_sem=halo_send.at[i],
                    recv_sem=halo_recv.at[i, h - low],
                    device_id={"seq": me + 1},
                    device_id_type=pl.DeviceIdType.MESH,
                )
            )
        return out

    netw = Net(second, near_size, far_size, g, res, acc, got, send, recv)

    def position(rows):
        return anchor + rows + lax.broadcasted_iota(jnp.int32, (BLOCK, 1), 0)

    def prepare(h):
        for c in load_weights(h):
            c.wait()
        if second:
            coef = fast_rate / jnp.sqrt(jnp.sum(sq_in[...]) / total_count + epsilon)
        for j in range(3):
            for p in range(pieces):
                rows = pl.ds(p * CHUNK, CHUNK)
                w = wbuf[j, rows]
                if second:
                    w = w - coef * gbuf[j * pieces + p].astype(jnp.float32)
                wb[h, j, rows] = w.astype(jnp.bfloat16)

        @pl.when(h + 1 < heads)
        def _():
            for c in load_weights(h + 1):
                c.start()

    def backward(h, kind):
        @pl.when(kind == 0)
        def _():
            for k in (0, 1):
                load_one(k, h).wait()

        for turn in range(0, blocks, ahead):
            b = kind + turn
            start = pl.multiple_of(b * BLOCK, BLOCK)
            rows = pl.ds(start, BLOCK)
            x = kbuf[h, pl.ds(pad + start, BLOCK)]
            rate = rate_ref[pl.ds(h, 1), rows]
            down = lax.broadcasted_iota(jnp.int32, (BLOCK, BLOCK), 0)
            across = lax.broadcasted_iota(jnp.int32, (BLOCK, BLOCK), 1)
            scaled = jnp.sum(jnp.where(down == across, rate, 0.0), axis=1, keepdims=True)
            inside = (position(start) >= edge) if second else (position(start) < edge)
            scaled = scaled * jnp.where(inside, 1.0, 0.0)
            first = mm(x, wb[h, 0], 1, 0)
            third = mm(x, wb[h, 1], 1, 0)
            d_out = (-scaled * tbuf[h, rows].astype(jnp.float32)).astype(jnp.bfloat16)
            d_act = mm(d_out, wb[h, 2], 1, 0)
            sigma = jax.nn.sigmoid(first)
            swish = first * sigma
            dbuf[0, rows] = (d_act * third * sigma * (1.0 + first * (1.0 - sigma))).astype(jnp.bfloat16)
            dbuf[1, rows] = (d_act * swish).astype(jnp.bfloat16)
            dbuf[2, rows] = (swish * third).astype(jnp.bfloat16)
            dbuf[3, rows] = d_out

    def outer(h, j):
        left = kbuf[h, pl.ds(pad, local)] if j < 2 else dbuf[3]
        value = mm(left, dbuf[j], 0, 0).astype(jnp.bfloat16)
        for p in range(pieces):
            g[h * per + j * pieces + p] = value[p * CHUNK : (p + 1) * CHUNK]

    def attend(block, h, order):
        start = pl.multiple_of(block * BLOCK, BLOCK)
        slot = order % 2

        @pl.when(block == blocks - 1)
        def _():
            for k in (2, 3):
                load_one(k, h).wait()

            @pl.when(jnp.logical_not(early))
            def _():
                for k in (0, 1):
                    load_one(k, h).wait()

        @pl.when((block == halo_blocks - 1) & (h < here) & (me > 0))
        def _():
            for c in halo(h):
                c.wait_recv()

        @pl.when(order >= 2)
        def _():
            block_out(block, h, slot).wait()

        q = qbuf[h, pl.ds(start, BLOCK)]
        inside = (block >= halo_blocks) | (h < here)

        @pl.when(inside)
        def _():
            stage[slot] = attention(q, vbuf.at[h], h, start)

        @pl.when(jnp.logical_not(inside))
        def _():
            stage[slot] = jnp.zeros(stage.shape[1:], jnp.float32)

        @pl.when(early)
        def _():
            y = fast_output(q, wb, h)
            stage[slot] += jnp.where(position(start) < edge, y, 0.0)

        block_out(block, h, slot).start()

    def combine(u):
        block, h = place(u)
        start = pl.multiple_of(block * BLOCK, BLOCK)
        slot = u % 2

        @pl.when(u + 1 < units)
        def _():
            attn_in(u + 1).start()

        attn_in(u).wait()

        @pl.when(block == blocks - 1)
        def _():
            load_one(2, h).wait()

            @pl.when(jnp.logical_not(late))
            def _():
                for k in (0, 1):
                    load_one(k, h).wait()

        @pl.when(u >= 2)
        def _():
            block_out(block, h, slot).wait()

        if here < heads:

            @pl.when((block == halo_blocks - 1) & (h >= here))
            def _():
                own_values(h).wait()

            @pl.when((block == halo_blocks - 1) & (h >= here) & (me > 0))
            def _():
                for c in halo(h):
                    c.wait_recv()

            @pl.when((block < halo_blocks) & (h >= here))
            def _():
                q = qbuf[h, pl.ds(start, BLOCK)]
                stage[slot] += attention(q, vbuf.at[h - here], h, start)

        @pl.when(late)
        def _():
            y = fast_output(qbuf[h, pl.ds(start, BLOCK)], wb, h)
            mstage[slot] = (stage[slot] + jnp.where(position(start) >= edge, y, 0.0)).astype(jnp.bfloat16)

        @pl.when(jnp.logical_not(late))
        def _():
            mstage[slot] = stage[slot].astype(jnp.bfloat16)

        block_out(block, h, slot).start()

    def put(n):
        return pltpu.make_async_copy(res.at[n], sums.at[n], out_sem.at[0])

    def finish(n):
        put(n).start()
        part = jnp.square(res[n].astype(jnp.float32))
        sq_all[mine] += jnp.sum(part.reshape(-1, *sq_all.shape[1:]), axis=0)

    def gradient(i):
        h = i // per
        kind = i % per

        @pl.when(h < heads)
        def _():
            @pl.when(kind < ahead)
            def _():
                backward(h, kind)

            for j in range(3):

                @pl.when(kind == ahead + j)
                def _():
                    outer(h, j)

        @pl.when((h < heads - 1) & (kind == per - 1))
        def _():
            prepare(h + 1)

    def send_halo(i):
        size = WIN // HALO_PIECES

        @pl.when((i < away * HALO_PIECES) & (me < count - 1))
        def _():
            for c in halo(low + i // HALO_PIECES, pl.multiple_of((i % HALO_PIECES) * size, size), size):
                c.start()

    if away:

        @pl.loop(0, HALO_LEAD)
        def _(i):
            send_halo(i)

    @pl.when(works)
    def _():
        prepare(0)

        @pl.loop(0, ahead)
        def _(i):
            gradient(i)

    if second:
        steps = [begin + units]
    else:
        near_at = max(NEAR_AT, begin + plain)
        steps = [begin + plain, near_at + NEAR_EVERY * (units - plain)]

    @pl.loop(0, max(netw.length, *steps))
    def _(i):
        if away:

            @pl.when(i % 2 == 0)
            def _():
                send_halo(i // 2 + HALO_LEAD)


        @pl.when(works)
        def _():
            gradient(i + ahead)

        netw.advance(i, finish)
        u = i - begin
        if second:

            @pl.when((u >= 0) & (u < units))
            def _():
                combine(u)
        else:

            @pl.when((u >= 0) & (u < plain))
            def _():
                block, h = place(u)
                attend(block, h, u)

            v = i - near_at
            w = v // NEAR_EVERY

            @pl.when((v >= 0) & (v % NEAR_EVERY == 0) & (w < units - plain))
            def _():
                attend(halo_blocks - 1 - w % halo_blocks, w // halo_blocks, plain + w)

    netw.drain()
    share_squares(sq_all, sq_ref, sq_send, sq_recv)
    if away:

        @pl.when(me < count - 1)
        def _():
            for i in range(2):
                every = kbuf.at[pl.ds(low, away), pl.ds(0, WIN)]
                pltpu.make_async_remote_copy(
                    src_ref=every, dst_ref=every, send_sem=halo_send.at[i], recv_sem=halo_recv.at[i, 0],
                    device_id={"seq": me + 1}, device_id_type=pl.DeviceIdType.MESH,
                ).wait_send()

    @pl.when(jnp.logical_not(works))
    def _():
        for c in load_weights(0):
            c.wait()

    for slot in range(2):
        block_out(0, 0, slot).wait()
    pltpu.make_async_copy(res, sums, out_sem.at[0]).wait()


def block_step(second, arrays, total_count):
    near, far = sizes_of_seq()
    if second:
        keys, weights = arrays[4], arrays[8]
    else:
        keys, weights = arrays[3], arrays[7]
    heads, _, hd, hid = weights.shape
    local = keys.shape[0]
    chunks = heads * 3 * hd // CHUNK
    vmem = pl.BlockSpec(memory_space=pltpu.VMEM)
    smem = pl.BlockSpec(memory_space=pltpu.SMEM)
    hbm = pl.BlockSpec(memory_space=pl.ANY)
    half = CHUNK // CORES
    kinds = link_kinds(near)
    ranks = lax.axis_size("head")
    dma = pltpu.SemaphoreType.DMA
    bf16, f32 = jnp.bfloat16, jnp.float32
    pad = WIN
    away = max(heads // 2, 1)
    scratch = [
        pltpu.VMEM((heads, pad + local, hd), bf16),
        pltpu.VMEM((heads, local, hd), bf16),
        pltpu.VMEM((heads, local, hd), bf16),
        pltpu.VMEM((3, hd, hid), f32),
        pltpu.VMEM((heads, 3, hd, hid), bf16),
        pltpu.VMEM((chunks, CHUNK, hid), bf16),
        pltpu.VMEM((chunks, CHUNK, hid), bf16),
        pltpu.VMEM((chunks, half, hid), bf16),
        pltpu.VMEM((3, chunks, half, hid), bf16),
        pltpu.VMEM((4, local, hd), bf16),
        pltpu.VMEM((2, BLOCK, hd), f32),
        pltpu.VMEM((ranks, 8, hid), f32),
        dma((kinds,)),
        dma((kinds, chunks)),
        dma((ranks,)),
        dma((ranks,)),
        dma((4, heads)),
        dma((2,)),
        dma((1,)),
        dma((2,)),
    ]
    scratch += [
        pltpu.VMEM((away, 2 * WIN, hd) if second else (heads, pad + local, hd), bf16),
        dma((2,)),
        dma((2, heads)),
    ]
    if second:
        scratch += [
            pltpu.VMEM((3 * hd // CHUNK, CHUNK, hid), bf16),
            pltpu.VMEM((2, BLOCK, hd), bf16),
            dma((2,)),
            dma((away,)),
        ]
        in_specs = [smem, smem, vmem, vmem] + [hbm] * 7
        wide = jax.ShapeDtypeStruct(keys.shape, bf16)
    else:
        in_specs = [smem, smem, vmem, hbm, hbm, hbm, hbm, hbm]
        wide = jax.ShapeDtypeStruct(keys.shape, f32)
    return pl.pallas_call(
        functools.partial(block_kernel, second, near, far, total_count),
        in_specs=in_specs,
        out_specs=(hbm, vmem, hbm),
        out_shape=(
            jax.ShapeDtypeStruct((chunks, CHUNK, hid), bf16),
            jax.ShapeDtypeStruct((8, hid), f32),
            wide,
        ),
        scratch_shapes=scratch,
        compiler_params=pltpu.CompilerParams(
            collective_id=int(second), has_side_effects=True, vmem_limit_bytes=67043328
        ),
        cost_estimate=pl.CostEstimate(flops=10**11, bytes_accessed=60 << 20, transcendentals=0),
        name="second" if second else "first",
    )(*arrays)


def renew_kernel(total_count, sq0_ref, sq1_ref, w_ref, g0_ref, g1_ref, mixed_ref, out_ref, copy_ref):
    coef = [
        fast_rate / jnp.sqrt(jnp.sum(s[...]) / total_count + epsilon) for s in (sq0_ref, sq1_ref)
    ]
    out_ref[...] = (
        w_ref[...] - coef[0] * g0_ref[...].astype(jnp.float32) - coef[1] * g1_ref[...].astype(jnp.float32)
    )
    copy_ref[...] = mixed_ref[...]


def renew(total_count, sq0, sq1, weights, g0, g1, mixed):
    flat = (-1, weights.shape[-1])
    w = weights.reshape(flat)
    steps = RENEW_STEPS
    small = pl.BlockSpec(sq0.shape, lambda i: (0, 0))
    tile = pl.BlockSpec((w.shape[0] // steps, w.shape[1]), lambda i: (i, 0))
    rows = pl.BlockSpec((mixed.shape[0] // steps, mixed.shape[1]), lambda i: (i, 0))
    out, mixed = pl.pallas_call(
        functools.partial(renew_kernel, total_count),
        grid=(steps,),
        in_specs=[small, small, tile, tile, tile, rows],
        out_specs=(tile, rows),
        out_shape=(
            jax.ShapeDtypeStruct(w.shape, jnp.float32),
            jax.ShapeDtypeStruct(mixed.shape, mixed.dtype),
        ),
        compiler_params=pltpu.CompilerParams(vmem_limit_bytes=67043328),
        cost_estimate=pl.CostEstimate(flops=4 * w.size, bytes_accessed=16 * w.size, transcendentals=0),
        name="renew",
    )(sq0, sq1, w, g0.reshape(flat), g1.reshape(flat), mixed)
    return mixed, out.reshape(weights.shape)


def per_device(queries, keys, values, targets, token_rate, window, split, fast_init):
    total_count = float(fast_init.size * lax.axis_size("head"))
    g0, sq0, attn = block_step(
        False, (split, window, token_rate.T, keys, values, queries, targets, fast_init), total_count
    )
    g1, sq1, mixed = block_step(
        True,
        (split, window, token_rate.T, sq0, keys, values, queries, targets, fast_init, g0, attn),
        total_count,
    )
    return renew(total_count, sq0, sq1, fast_init, g0, g1, mixed)


def solution(mesh):
    return jax.shard_map(
        per_device,
        mesh=mesh,
        in_specs=(
            P("seq", "head"),
            P("seq", "head"),
            P("seq", "head"),
            P("seq", "head"),
            P("seq", "head"),
            P("head"),
            P(),
            P("head", None, None, None),
        ),
        out_specs=(P("seq", "head"), P("head", None, None, None)),
        check_vma=False,
    )
```

```python
import functools

import jax
import jax.numpy as jnp
from jax import lax
from jax.experimental import pallas as pl
from jax.experimental.pallas import tpu as pltpu
from jax.sharding import PartitionSpec as P

WIN = 512
fast_rate = 0.01
epsilon = 1e-06
CORES = 2


def mm(a, b, ca, cb):
    return lax.dot_general(
        a, b, (((ca,), (cb,)), ((), ())), preferred_element_type=jnp.float32
    )


SHARES = ((8, 4, 4), (8, 4, 4))
STEPS = ((2, 2, 2), (2, 2, 2))
CHUNK = 256


class Link:
    def __init__(self, net, src, dst, to, gives):
        self.net, self.src, self.dst, self.to, self.gives = net, src, dst, to, gives
        self.kind = len(net.links)
        net.links.append(self)

    def copy(self, n, slot):
        return pltpu.make_async_remote_copy(
            src_ref=self.src(n),
            dst_ref=self.dst(n),
            send_sem=self.net.send.at[self.kind],
            recv_sem=self.net.recv.at[self.kind, slot],
            device_id={"seq": self.to},
            device_id_type=pl.DeviceIdType.MESH,
        )

    def start(self, n):
        @pl.when(self.gives)
        def _():
            self.copy(n, n).start()

    def wait(self, n):
        self.copy(n, n).wait_recv()

    def drain(self):
        @pl.when(self.gives)
        def _():
            self.copy(pl.ds(0, self.net.chunks), 0).wait_send()


def total(ref, at, parts):
    out = ref[at].astype(jnp.float32)
    for part in parts:
        out += part.astype(jnp.float32)
    return out.astype(ref.dtype)


def link_kinds(near):
    return 2 + (4 + 2 * (near - 1)) + 2 * (4 + 2 * (near - 1))


class Net:
    def __init__(self, mirror, near_size, far_size, g, out, acc, got, send, recv):
        self.links, self.stages = [], []
        self.send, self.recv = send, recv
        self.chunks, rows, width = g.shape
        half = rows // CORES
        fine = width // near_size
        me = lax.axis_index("seq")
        core = me % CORES
        near = (me // CORES) % near_size
        far = me // (CORES * near_size)
        line = far_size - 1 - far if mirror else far
        last = (5 * far_size - 1) // 8
        gives = line <= last
        step_core, step_near, step_line = STEPS[mirror]

        def device(line_to, near_to, core_to):
            far_to = far_size - 1 - line_to if mirror else line_to
            return (far_to * near_size + near_to) * CORES + core_to

        def peer(d):
            return device(line, (near + d) % near_size, core)

        def piece(d):
            index = (near + d) % near_size
            return pl.ds(pl.multiple_of(index * fine, 128), fine)

        def rows_of(c, first, count):
            return pl.ds(pl.multiple_of(c * half + first, 16), count)

        other = 1 - core
        mate = device(line, near, other)
        swap = Link(self, lambda n: g.at[n, rows_of(other, 0, half)], lambda n: acc.at[n], mate, gives)
        join = Link(
            self,
            lambda n: out.at[n, rows_of(core, 0, half)],
            lambda n: out.at[n, rows_of(core, 0, half)],
            mate,
            me >= 0,
        )
        self.stage(0, swap.start)

        shares = SHARES[mirror]
        unit = half // sum(shares)
        count = [s * unit for s in shares]
        first = [sum(count[:i]) for i in range(3)]
        mid = last // 2
        ends = []
        starts = []

        def line_links(root, src, base, n_cols, final):
            left = Link(self, src, lambda n: got.at[0, n, base, n_cols], device(line + 1, near, core), line < root)
            right = Link(
                self, src, lambda n: got.at[1, n, base, n_cols], device(line - 1, near, core),
                (line > root) & gives,
            )
            out_right = Link(self, final, final, device(line + 1, near, core), (line >= root) & (line < far_size - 1))
            out_left = Link(self, final, final, device(line - 1, near, core), (line <= root) & (line > 0))
            return left, right, out_right, out_left

        def line_in(at, root, left, right, base, cols, done):
            depth = max(root, last - root)

            def begin(n):
                @pl.when(line == 0)
                def _():
                    left.start(n)

                @pl.when(line == last)
                def _():
                    right.start(n)

            def hop(k, n):
                if k < root:
                    @pl.when(line == k)
                    def _():
                        left.wait(n)
                        acc[n, base, cols] = total(acc, (n, base, cols), [got[0, n, base, cols]])
                        left.start(n)
                if last - k > root:
                    @pl.when(line == last - k)
                    def _():
                        right.wait(n)
                        acc[n, base, cols] = total(acc, (n, base, cols), [got[1, n, base, cols]])
                        right.start(n)

            def end(n):
                @pl.when(line == root)
                def _():
                    parts = []
                    if root > 0:
                        left.wait(n)
                        parts.append(got[0, n, base, cols])
                    if last > root:
                        right.wait(n)
                        parts.append(got[1, n, base, cols])
                    done(n, total(acc, (n, base, cols), parts))

            for k in range(1, depth):
                self.stage(at + k * step_line, functools.partial(hop, k))
            self.stage(at + depth * step_line, end)
            return begin, at + depth * step_line

        def line_out(at, root, out_right, out_left, then):
            def hop(k, n):
                if root + k < far_size:
                    @pl.when(line == root + k)
                    def _():
                        out_right.wait(n)
                        out_right.start(n)
                        then(n)
                if root - k >= 0:
                    @pl.when(line == root - k)
                    def _():
                        out_left.wait(n)
                        out_left.start(n)
                        then(n)

            depth = max(far_size - 1 - root, root)
            for k in range(1, depth + 1):
                self.stage(at + k * step_line, functools.partial(hop, k))
            return at + depth * step_line

        t = step_core

        if count[0]:
            base = pl.ds(first[0], count[0])
            wide = rows_of(core, first[0], count[0])
            mine = piece(0)
            spread = [
                Link(
                    self,
                    lambda n, d=d: acc.at[n, base, piece(d)],
                    lambda n, d=d: got.at[2, n, base, pl.ds((d - 1) * fine, fine)],
                    peer(d),
                    gives,
                )
                for d in range(1, near_size)
            ]
            final = lambda n: out.at[n, wide, mine]
            left, right, out_right, out_left = line_links(mid, lambda n: acc.at[n, base, mine], base, mine, final)
            fill = [Link(self, final, final, peer(d), me >= 0) for d in range(1, near_size)]
            starts += spread

            def give(n):
                for f in fill:
                    f.start(n)

            def done(n, value):
                out[n, wide, mine] = value
                out_right.start(n)
                out_left.start(n)
                give(n)

            begin, t1 = line_in(t + step_near, mid, left, right, base, mine, done)

            def gathered(n):
                @pl.when(gives)
                def _():
                    for s in spread:
                        s.wait(n)
                    acc[n, base, mine] = total(
                        acc, (n, base, mine),
                        [got[2, n, base, pl.ds((d - 1) * fine, fine)] for d in range(1, near_size)],
                    )
                    begin(n)

            self.stage(t + step_near, gathered)
            t1 = line_out(t1, mid, out_right, out_left, give) + step_near

            def filled(n):
                for d in range(1, near_size):
                    fill[d - 1].wait(n)

            self.stage(t1, filled)
            ends.append(t1)

        def whole(index, root):
            base = pl.ds(first[index], count[index])
            wide = rows_of(core, first[index], count[index])
            every = pl.ds(0, width)
            mine = piece(0)
            final = lambda n: out.at[n, wide, every]
            part = lambda n: out.at[n, wide, mine]
            left, right, out_right, out_left = line_links(root, lambda n: acc.at[n, base, every], base, every, final)
            spread = [
                Link(
                    self,
                    lambda n, d=d: acc.at[n, base, piece(d)],
                    lambda n, d=d: got.at[2, n, base, pl.ds((d - 1) * fine, fine)],
                    peer(d),
                    line == root,
                )
                for d in range(1, near_size)
            ]
            fill = [Link(self, part, part, peer(d), line == root) for d in range(1, near_size)]

            def done(n, value):
                acc[n, base, every] = value
                for s in spread:
                    s.start(n)

            begin, t1 = line_in(t, root, left, right, base, every, done)

            def gathered(n):
                @pl.when(line == root)
                def _():
                    for s in spread:
                        s.wait(n)
                    out[n, wide, mine] = total(
                        acc, (n, base, mine),
                        [got[2, n, base, pl.ds((d - 1) * fine, fine)] for d in range(1, near_size)],
                    )
                    for f in fill:
                        f.start(n)

            def filled(n):
                @pl.when(line == root)
                def _():
                    for f in fill:
                        f.wait(n)
                    out_right.start(n)
                    out_left.start(n)

            self.stage(t1 + step_near, gathered)
            self.stage(t1 + 2 * step_near, filled)
            t1 = line_out(t1 + 2 * step_near, root, out_right, out_left, lambda n: None)
            ends.append(t1)
            return begin

        begins = [whole(i, root) for i, root in ((1, mid), (2, last)) if count[i]]

        def paired(n):
            @pl.when(gives)
            def _():
                swap.wait(n)
                acc[n] = total(acc, (n,), [g[n, rows_of(core, 0, half)]])
                for s in starts:
                    s.start(n)
                for begin in begins:
                    begin(n)

        self.stage(t, paired)
        t = max(ends)
        self.stage(t, join.start)
        self.stage(t + step_core, join.wait)
        self.length = self.chunks + t + step_core

    def stage(self, at, fn):
        self.stages.append((at, fn))

    def advance(self, i, finish):
        end = max(at for at, _ in self.stages)
        for at, fn in sorted(self.stages, key=lambda s: -s[0]):
            n = i - at

            @pl.when((n >= 0) & (n < self.chunks))
            def _():
                fn(n)
                if at == end:
                    finish(n)

    def drain(self):
        for link in self.links:
            link.drain()


BLOCK = 256
RENEW_STEPS = 4
HALO_PIECES = 8
HALO_LEAD = 10
NEAR_AT = 19
NEAR_EVERY = 2


def sizes_of_seq():
    chips = lax.axis_size("seq") // CORES
    near = 1
    while near * near * 4 <= chips:
        near *= 2
    return near, chips // near


def greet(near_size, far_size):
    me = lax.axis_index("seq")
    strides = (1, CORES, CORES * near_size)
    sizes = (CORES, near_size, far_size)
    all_count = CORES * near_size * far_size
    barrier = pltpu.get_barrier_semaphore()
    targets = [{"seq": (me + d) % all_count} for d in (1, all_count - 1)]
    for stride, size in zip(strides, sizes):
        place = (me // stride) % size
        for d in range(1, size):
            targets.append({"seq": me + ((place + d) % size - place) * stride})
    mine = lax.axis_index("head")
    heads = lax.axis_size("head")
    for d in range(1, heads):
        targets.append({"head": (mine + d) % heads})
    for target in targets:
        pl.semaphore_signal(barrier, inc=1, device_id=target, device_id_type=pl.DeviceIdType.MESH)
    pl.semaphore_wait(barrier, len(targets))


def fast_output(x, wb, head):
    first = mm(x, wb[head, 0], 1, 0)
    third = mm(x, wb[head, 1], 1, 0)
    act = (first * jax.nn.sigmoid(first) * third).astype(jnp.bfloat16)
    y = mm(act, wb[head, 2], 1, 1)
    return y / jnp.sqrt(jnp.mean(y * y, axis=1, keepdims=True) + epsilon)


def share_squares(sq_all, sq_ref, sq_send, sq_recv):
    mine = lax.axis_index("head")
    heads = lax.axis_size("head")
    copies = []
    for d in range(1, heads):
        copies.append(
            pltpu.make_async_remote_copy(
                src_ref=sq_all.at[mine],
                dst_ref=sq_all.at[mine],
                send_sem=sq_send.at[d],
                recv_sem=sq_recv.at[d],
                device_id={"head": (mine + d) % heads},
                device_id_type=pl.DeviceIdType.MESH,
            )
        )
    for c in copies:
        c.start()
    for c in copies:
        c.wait()
    sq_ref[...] = jnp.sum(sq_all[...], axis=0)


def block_kernel(second, near_size, far_size, total_count, *refs):
    refs = list(refs)

    def take(count):
        out = refs[:count]
        del refs[:count]
        return out

    if second:
        edge_ref, win_ref, rate_ref, sq_in, keys, values, queries, targets, weights = take(9)
        g_in, attn = take(2)
        sums, sq_ref, mixed, base = take(4)
    else:
        edge_ref, win_ref, rate_ref, keys, values, queries, targets, weights = take(8)
        sums, sq_ref, attn = take(3)
    kbuf, qbuf, tbuf, wbuf, wb, g, res, acc, got, dbuf, stage, sq_all = take(12)
    send, recv, sq_send, sq_recv, load, wload, out_sem, stage_sem = take(8)
    vbuf, halo_send, halo_recv = take(3)
    if second:
        gbuf, mstage, in_sem, own_sem, base_sem = take(5)
    pad = WIN
    assert not refs

    heads = weights.shape[0]
    local, hd = qbuf.shape[1:]
    me = lax.axis_index("seq")
    count = lax.axis_size("seq")
    mine = lax.axis_index("head")
    anchor = me * local
    early = 8 * me < 5 * count
    late = 8 * (me + 1) > 3 * count
    works = late if second else early
    far = me // (CORES * near_size)
    line = far_size - 1 - far if second else far
    gives = line <= (5 * far_size - 1) // 8
    pieces = hd // CHUNK
    per = 3 * pieces
    blocks = local // BLOCK
    units = blocks * heads
    begin = (heads - 1) * (per - 1)
    ahead = per - 3
    assert blocks % ahead == 0
    halo_blocks = WIN // BLOCK
    plain = (blocks - halo_blocks) * heads
    here = heads - heads // 2

    low, away = (here, heads - here) if second else (0, here)

    def own_values(h):
        k = h - low
        return pltpu.make_async_copy(columns(values, h, pl.ds(0, WIN)), vbuf.at[k, pl.ds(WIN, WIN)], own_sem.at[k])

    def attention(q, v_all, h, start):
        span = WIN + BLOCK
        scores = mm(q, kbuf[h, pl.ds(start, span)], 1, 1) * (hd ** (-0.5))
        row = lax.broadcasted_iota(jnp.int32, (BLOCK, span), 0)
        colm = lax.broadcasted_iota(jnp.int32, (BLOCK, span), 1)
        back = row + WIN - colm
        live = (back >= 0) & (back < win_ref[h]) & (colm >= WIN - start - anchor)
        scores = jnp.where(live, scores, -1e30)
        peak = jnp.max(scores, axis=1, keepdims=True)
        expo = jnp.exp(scores - peak)
        probs = (expo * (1.0 / jnp.sum(expo, axis=1, keepdims=True))).astype(jnp.bfloat16)
        return mm(probs, v_all[pl.ds(start, span)], 1, 0)
    edge = edge_ref[0]

    def columns(ref, h, rows=None):
        cols = pl.ds(pl.multiple_of(h * hd, 128), hd)
        return ref.at[pl.ds(0, local) if rows is None else rows, cols]

    def load_weights(h):
        copies = [pltpu.make_async_copy(weights.at[h], wbuf, wload.at[0])]
        if second:
            copies.append(
                pltpu.make_async_copy(g_in.at[pl.ds(pl.multiple_of(h * per, per), per)], gbuf, wload.at[1])
            )
        return copies

    def load_one(i, h):
        src = (keys, targets, queries, None if second else values)[i]
        dst = (kbuf, tbuf, qbuf, None if second else vbuf)[i]
        at = dst.at[h, pl.ds(pad, local)] if i in (0, 3) else dst.at[h]
        return pltpu.make_async_copy(columns(src, h), at, load.at[i, h])

    def place(u):
        return blocks - 1 - u // heads, u % heads

    def block_of(ref, block, h):
        return columns(ref, h, pl.ds(pl.multiple_of(block * BLOCK, BLOCK), BLOCK))

    def attn_in(u):
        return pltpu.make_async_copy(block_of(attn, *place(u)), stage.at[u % 2], in_sem.at[u % 2])

    def block_out(block, h, slot):
        src, dst = (mstage, mixed) if second else (stage, attn)
        return pltpu.make_async_copy(src.at[slot], block_of(dst, block, h), stage_sem.at[slot])

    for c in load_weights(0):
        c.start()
    for i in (0, 1):
        load_one(i, 0).start()
    sq_all[mine] = jnp.zeros(sq_all.shape[1:], jnp.float32)

    @pl.when(gives & jnp.logical_not(works))
    def _():
        @pl.loop(0, g.shape[0])
        def _(n):
            g[n] = jnp.zeros(g.shape[1:], g.dtype)

    if away:

        @pl.when(me == 0)
        def _():
            @pl.loop(0, away)
            def _(k):
                kbuf[low + k, pl.ds(0, WIN)] = jnp.zeros((WIN, hd), kbuf.dtype)
                vbuf[k, pl.ds(0, WIN)] = jnp.zeros((WIN, hd), vbuf.dtype)

    greet(near_size, far_size)

    def halo(h, first=0, size=WIN):
        rows = pl.ds(pl.multiple_of(local - WIN + first, 16), size)
        out = []
        for i, (src, dst) in enumerate(((keys, kbuf.at[h]), (values, vbuf.at[h - low]))):
            out.append(
                pltpu.make_async_remote_copy(
                    src_ref=columns(src, h, rows),
                    dst_ref=dst.at[pl.ds(first, size)],
                    send_sem=halo_send.at[i],
                    recv_sem=halo_recv.at[i, h - low],
                    device_id={"seq": me + 1},
                    device_id_type=pl.DeviceIdType.MESH,
                )
            )
        return out

    netw = Net(second, near_size, far_size, g, res, acc, got, send, recv)

    def position(rows):
        return anchor + rows + lax.broadcasted_iota(jnp.int32, (BLOCK, 1), 0)

    def keep(h):
        return pltpu.make_async_copy(wbuf, base.at[h], base_sem.at[0])

    def load_next(h):
        @pl.when(h + 1 < heads)
        def _():
            for c in load_weights(h + 1):
                c.start()

    def prepare(h):
        for c in load_weights(h):
            c.wait()
        if second:
            coef = fast_rate / jnp.sqrt(jnp.sum(sq_in[...]) / total_count + epsilon)
        for j in range(3):
            for p in range(pieces):
                rows = pl.ds(p * CHUNK, CHUNK)
                w = wbuf[j, rows]
                if second:
                    w = w - coef * gbuf[j * pieces + p].astype(jnp.float32)
                    wbuf[j, rows] = w
                wb[h, j, rows] = w.astype(jnp.bfloat16)

        if second:
            keep(h).start()
        else:
            load_next(h)

    def backward(h, kind):
        @pl.when(kind == 0)
        def _():
            for k in (0, 1):
                load_one(k, h).wait()

        for turn in range(0, blocks, ahead):
            b = kind + turn
            start = pl.multiple_of(b * BLOCK, BLOCK)
            rows = pl.ds(start, BLOCK)
            x = kbuf[h, pl.ds(pad + start, BLOCK)]
            rate = rate_ref[pl.ds(h, 1), rows]
            down = lax.broadcasted_iota(jnp.int32, (BLOCK, BLOCK), 0)
            across = lax.broadcasted_iota(jnp.int32, (BLOCK, BLOCK), 1)
            scaled = jnp.sum(jnp.where(down == across, rate, 0.0), axis=1, keepdims=True)
            inside = (position(start) >= edge) if second else (position(start) < edge)
            scaled = scaled * jnp.where(inside, 1.0, 0.0)
            first = mm(x, wb[h, 0], 1, 0)
            third = mm(x, wb[h, 1], 1, 0)
            d_out = (-scaled * tbuf[h, rows].astype(jnp.float32)).astype(jnp.bfloat16)
            d_act = mm(d_out, wb[h, 2], 1, 0)
            sigma = jax.nn.sigmoid(first)
            swish = first * sigma
            dbuf[0, rows] = (d_act * third * sigma * (1.0 + first * (1.0 - sigma))).astype(jnp.bfloat16)
            dbuf[1, rows] = (d_act * swish).astype(jnp.bfloat16)
            dbuf[2, rows] = (swish * third).astype(jnp.bfloat16)
            dbuf[3, rows] = d_out

    def outer(h, j):
        left = kbuf[h, pl.ds(pad, local)] if j < 2 else dbuf[3]
        value = mm(left, dbuf[j], 0, 0).astype(jnp.bfloat16)
        for p in range(pieces):
            g[h * per + j * pieces + p] = value[p * CHUNK : (p + 1) * CHUNK]

    def attend(block, h, order):
        start = pl.multiple_of(block * BLOCK, BLOCK)
        slot = order % 2

        @pl.when(block == blocks - 1)
        def _():
            for k in (2, 3):
                load_one(k, h).wait()

            @pl.when(jnp.logical_not(early))
            def _():
                for k in (0, 1):
                    load_one(k, h).wait()

        @pl.when((block == halo_blocks - 1) & (h < here) & (me > 0))
        def _():
            for c in halo(h):
                c.wait_recv()

        @pl.when(order >= 2)
        def _():
            block_out(block, h, slot).wait()

        q = qbuf[h, pl.ds(start, BLOCK)]
        inside = (block >= halo_blocks) | (h < here)

        @pl.when(inside)
        def _():
            stage[slot] = attention(q, vbuf.at[h], h, start)

        @pl.when(jnp.logical_not(inside))
        def _():
            stage[slot] = jnp.zeros(stage.shape[1:], jnp.float32)

        @pl.when(early)
        def _():
            y = fast_output(q, wb, h)
            stage[slot] += jnp.where(position(start) < edge, y, 0.0)

        block_out(block, h, slot).start()

    def combine(u):
        block, h = place(u)
        start = pl.multiple_of(block * BLOCK, BLOCK)
        slot = u % 2

        @pl.when(u + 1 < units)
        def _():
            attn_in(u + 1).start()

        attn_in(u).wait()

        @pl.when(block == blocks - 1)
        def _():
            load_one(2, h).wait()

            @pl.when(jnp.logical_not(late))
            def _():
                for k in (0, 1):
                    load_one(k, h).wait()

        @pl.when(u >= 2)
        def _():
            block_out(block, h, slot).wait()

        if here < heads:

            @pl.when((block == halo_blocks - 1) & (h >= here))
            def _():
                own_values(h).wait()

            @pl.when((block == halo_blocks - 1) & (h >= here) & (me > 0))
            def _():
                for c in halo(h):
                    c.wait_recv()

            @pl.when((block < halo_blocks) & (h >= here))
            def _():
                q = qbuf[h, pl.ds(start, BLOCK)]
                stage[slot] += attention(q, vbuf.at[h - here], h, start)

        @pl.when(late)
        def _():
            y = fast_output(qbuf[h, pl.ds(start, BLOCK)], wb, h)
            mstage[slot] = (stage[slot] + jnp.where(position(start) >= edge, y, 0.0)).astype(jnp.bfloat16)

        @pl.when(jnp.logical_not(late))
        def _():
            mstage[slot] = stage[slot].astype(jnp.bfloat16)

        block_out(block, h, slot).start()

    def put(n):
        return pltpu.make_async_copy(res.at[n], sums.at[n], out_sem.at[0])

    def finish(n):
        put(n).start()
        part = jnp.square(res[n].astype(jnp.float32))
        sq_all[mine] += jnp.sum(part.reshape(-1, *sq_all.shape[1:]), axis=0)

    def gradient(i):
        h = i // per
        kind = i % per

        @pl.when((h < heads) & works)
        def _():
            @pl.when(kind < ahead)
            def _():
                backward(h, kind)

            for j in range(3):

                @pl.when(kind == ahead + j)
                def _():
                    outer(h, j)

        if second:

            @pl.when((h < heads) & (kind == 1))
            def _():
                keep(h).wait()
                load_next(h)

        @pl.when((h < heads - 1) & (kind == per - 1) & prepares)
        def _():
            prepare(h + 1)

    def send_halo(i):
        size = WIN // HALO_PIECES

        @pl.when((i < away * HALO_PIECES) & (me < count - 1))
        def _():
            for c in halo(low + i // HALO_PIECES, pl.multiple_of((i % HALO_PIECES) * size, size), size):
                c.start()

    if away:

        @pl.loop(0, HALO_LEAD)
        def _(i):
            send_halo(i)

    prepares = (me >= 0) if second else works

    @pl.when(prepares)
    def _():
        prepare(0)

    for h in range(heads):
        for i in (0, 1, 2) if second else (0, 1, 2, 3):
            if h > 0 or i > 1:
                load_one(i, h).start()
    if second:
        attn_in(0).start()
        for h in range(here, heads):
            own_values(h).start()

    @pl.loop(0, ahead)
    def _(i):
        gradient(i)

    if second:
        steps = [begin + units]
    else:
        near_at = max(NEAR_AT, begin + plain)
        steps = [begin + plain, near_at + NEAR_EVERY * (units - plain)]

    @pl.loop(0, max(netw.length, *steps))
    def _(i):
        if away:

            @pl.when(i % 2 == 0)
            def _():
                send_halo(i // 2 + HALO_LEAD)


        gradient(i + ahead)

        netw.advance(i, finish)
        u = i - begin
        if second:

            @pl.when((u >= 0) & (u < units))
            def _():
                combine(u)
        else:

            @pl.when((u >= 0) & (u < plain))
            def _():
                block, h = place(u)
                attend(block, h, u)

            v = i - near_at
            w = v // NEAR_EVERY

            @pl.when((v >= 0) & (v % NEAR_EVERY == 0) & (w < units - plain))
            def _():
                attend(halo_blocks - 1 - w % halo_blocks, w // halo_blocks, plain + w)

    share_squares(sq_all, sq_ref, sq_send, sq_recv)
    netw.drain()
    if away:

        @pl.when(me < count - 1)
        def _():
            for i in range(2):
                every = kbuf.at[pl.ds(low, away), pl.ds(0, WIN)]
                pltpu.make_async_remote_copy(
                    src_ref=every, dst_ref=every, send_sem=halo_send.at[i], recv_sem=halo_recv.at[i, 0],
                    device_id={"seq": me + 1}, device_id_type=pl.DeviceIdType.MESH,
                ).wait_send()

    if not second:

        @pl.when(jnp.logical_not(works))
        def _():
            for c in load_weights(0):
                c.wait()

    for slot in range(2):
        block_out(0, 0, slot).wait()
    pltpu.make_async_copy(res, sums, out_sem.at[0]).wait()


def block_step(second, arrays, total_count):
    near, far = sizes_of_seq()
    if second:
        keys, weights = arrays[4], arrays[8]
    else:
        keys, weights = arrays[3], arrays[7]
    heads, _, hd, hid = weights.shape
    local = keys.shape[0]
    chunks = heads * 3 * hd // CHUNK
    vmem = pl.BlockSpec(memory_space=pltpu.VMEM)
    smem = pl.BlockSpec(memory_space=pltpu.SMEM)
    hbm = pl.BlockSpec(memory_space=pl.ANY)
    half = CHUNK // CORES
    more = (jax.ShapeDtypeStruct(weights.shape, jnp.float32),) if second else ()
    kinds = link_kinds(near)
    ranks = lax.axis_size("head")
    dma = pltpu.SemaphoreType.DMA
    bf16, f32 = jnp.bfloat16, jnp.float32
    pad = WIN
    away = max(heads // 2, 1)
    scratch = [
        pltpu.VMEM((heads, pad + local, hd), bf16),
        pltpu.VMEM((heads, local, hd), bf16),
        pltpu.VMEM((heads, local, hd), bf16),
        pltpu.VMEM((3, hd, hid), f32),
        pltpu.VMEM((heads, 3, hd, hid), bf16),
        pltpu.VMEM((chunks, CHUNK, hid), bf16),
        pltpu.VMEM((chunks, CHUNK, hid), bf16),
        pltpu.VMEM((chunks, half, hid), bf16),
        pltpu.VMEM((3, chunks, half, hid), bf16),
        pltpu.VMEM((4, local, hd), bf16),
        pltpu.VMEM((2, BLOCK, hd), f32),
        pltpu.VMEM((ranks, 8, hid), f32),
        dma((kinds,)),
        dma((kinds, chunks)),
        dma((ranks,)),
        dma((ranks,)),
        dma((4, heads)),
        dma((2,)),
        dma((1,)),
        dma((2,)),
    ]
    scratch += [
        pltpu.VMEM((away, 2 * WIN, hd) if second else (heads, pad + local, hd), bf16),
        dma((2,)),
        dma((2, heads)),
    ]
    if second:
        scratch += [
            pltpu.VMEM((3 * hd // CHUNK, CHUNK, hid), bf16),
            pltpu.VMEM((2, BLOCK, hd), bf16),
            dma((2,)),
            dma((away,)),
            dma((1,)),
        ]
        in_specs = [smem, smem, vmem, vmem] + [hbm] * 7
        wide = jax.ShapeDtypeStruct(keys.shape, bf16)
    else:
        in_specs = [smem, smem, vmem, hbm, hbm, hbm, hbm, hbm]
        wide = jax.ShapeDtypeStruct(keys.shape, f32)
    return pl.pallas_call(
        functools.partial(block_kernel, second, near, far, total_count),
        in_specs=in_specs,
        out_specs=(hbm, vmem, hbm) + (hbm,) * len(more),
        out_shape=(
            jax.ShapeDtypeStruct((chunks, CHUNK, hid), bf16),
            jax.ShapeDtypeStruct((8, hid), f32),
            wide,
        )
        + more,
        scratch_shapes=scratch,
        compiler_params=pltpu.CompilerParams(
            collective_id=int(second), has_side_effects=True, vmem_limit_bytes=67043328
        ),
        cost_estimate=pl.CostEstimate(flops=10**11, bytes_accessed=60 << 20, transcendentals=0),
        name="second" if second else "first",
    )(*arrays)


def renew_kernel(total_count, sq_ref, w_ref, g_ref, mixed_ref, out_ref, copy_ref):
    coef = fast_rate / jnp.sqrt(jnp.sum(sq_ref[...]) / total_count + epsilon)
    out_ref[...] = w_ref[...] - coef * g_ref[...].astype(jnp.float32)
    copy_ref[...] = mixed_ref[...]


def renew(total_count, sq, weights, g, mixed):
    flat = (-1, weights.shape[-1])
    w = weights.reshape(flat)
    steps = RENEW_STEPS
    small = pl.BlockSpec(sq.shape, lambda i: (0, 0))
    tile = pl.BlockSpec((w.shape[0] // steps, w.shape[1]), lambda i: (i, 0))
    rows = pl.BlockSpec((mixed.shape[0] // steps, mixed.shape[1]), lambda i: (i, 0))
    out, mixed = pl.pallas_call(
        functools.partial(renew_kernel, total_count),
        grid=(steps,),
        in_specs=[small, tile, tile, rows],
        out_specs=(tile, rows),
        out_shape=(
            jax.ShapeDtypeStruct(w.shape, jnp.float32),
            jax.ShapeDtypeStruct(mixed.shape, mixed.dtype),
        ),
        compiler_params=pltpu.CompilerParams(vmem_limit_bytes=67043328),
        cost_estimate=pl.CostEstimate(flops=4 * w.size, bytes_accessed=16 * w.size, transcendentals=0),
        name="renew",
    )(sq, w, g.reshape(flat), mixed)
    return mixed, out.reshape(weights.shape)


def per_device(queries, keys, values, targets, token_rate, window, split, fast_init):
    total_count = float(fast_init.size * lax.axis_size("head"))
    g0, sq0, attn = block_step(
        False, (split, window, token_rate.T, keys, values, queries, targets, fast_init), total_count
    )
    g1, sq1, mixed, base = block_step(
        True,
        (split, window, token_rate.T, sq0, keys, values, queries, targets, fast_init, g0, attn),
        total_count,
    )
    return renew(total_count, sq1, base, g1, mixed)


def solution(mesh):
    return jax.shard_map(
        per_device,
        mesh=mesh,
        in_specs=(
            P("seq", "head"),
            P("seq", "head"),
            P("seq", "head"),
            P("seq", "head"),
            P("seq", "head"),
            P("head"),
            P(),
            P("head", None, None, None),
        ),
        out_specs=(P("seq", "head"), P("head", None, None, None)),
        check_vma=False,
    )
```

```python
import functools

import jax
import jax.numpy as jnp
from jax import lax
from jax.experimental import pallas as pl
from jax.experimental.pallas import tpu as pltpu
from jax.sharding import PartitionSpec as P

WIN = 512
fast_rate = 0.01
epsilon = 1e-06
CORES = 2


def mm(a, b, ca, cb):
    return lax.dot_general(
        a, b, (((ca,), (cb,)), ((), ())), preferred_element_type=jnp.float32
    )


SHARES = ((8, 4, 4), (8, 4, 4))
STEPS = ((2, 2, 2), (2, 2, 2))
CHUNK = 256


class Link:
    def __init__(self, net, src, dst, to, gives):
        self.net, self.src, self.dst, self.to, self.gives = net, src, dst, to, gives
        self.kind = len(net.links)
        net.links.append(self)

    def copy(self, n, slot):
        return pltpu.make_async_remote_copy(
            src_ref=self.src(n),
            dst_ref=self.dst(n),
            send_sem=self.net.send.at[self.kind],
            recv_sem=self.net.recv.at[self.kind, slot],
            device_id={"seq": self.to},
            device_id_type=pl.DeviceIdType.MESH,
        )

    def start(self, n):
        @pl.when(self.gives)
        def _():
            self.copy(n, n).start()

    def wait(self, n):
        self.copy(n, n).wait_recv()

    def drain(self):
        @pl.when(self.gives)
        def _():
            self.copy(pl.ds(0, self.net.chunks), 0).wait_send()


def total(ref, at, parts):
    out = ref[at].astype(jnp.float32)
    for part in parts:
        out += part.astype(jnp.float32)
    return out.astype(ref.dtype)


def link_kinds(near):
    return 2 + (4 + 2 * (near - 1)) + 2 * (4 + 2 * (near - 1))


class Net:
    def __init__(self, mirror, near_size, far_size, g, out, acc, got, send, recv):
        self.links, self.stages = [], []
        self.send, self.recv = send, recv
        self.chunks, rows, width = g.shape
        half = rows // CORES
        fine = width // near_size
        me = lax.axis_index("seq")
        core = me % CORES
        near = (me // CORES) % near_size
        far = me // (CORES * near_size)
        line = far_size - 1 - far if mirror else far
        last = (5 * far_size - 1) // 8
        gives = line <= last
        step_core, step_near, step_line = STEPS[mirror]

        def device(line_to, near_to, core_to):
            far_to = far_size - 1 - line_to if mirror else line_to
            return (far_to * near_size + near_to) * CORES + core_to

        def peer(d):
            return device(line, (near + d) % near_size, core)

        def piece(d):
            index = (near + d) % near_size
            return pl.ds(pl.multiple_of(index * fine, 128), fine)

        def rows_of(c, first, count):
            return pl.ds(pl.multiple_of(c * half + first, 16), count)

        other = 1 - core
        mate = device(line, near, other)
        swap = Link(self, lambda n: g.at[n, rows_of(other, 0, half)], lambda n: acc.at[n], mate, gives)
        join = Link(
            self,
            lambda n: out.at[n, rows_of(core, 0, half)],
            lambda n: out.at[n, rows_of(core, 0, half)],
            mate,
            me >= 0,
        )
        self.stage(0, swap.start)

        shares = SHARES[mirror]
        unit = half // sum(shares)
        count = [s * unit for s in shares]
        first = [sum(count[:i]) for i in range(3)]
        mid = last // 2
        ends = []
        starts = []

        def line_links(root, src, base, n_cols, final):
            left = Link(self, src, lambda n: got.at[0, n, base, n_cols], device(line + 1, near, core), line < root)
            right = Link(
                self, src, lambda n: got.at[1, n, base, n_cols], device(line - 1, near, core),
                (line > root) & gives,
            )
            out_right = Link(self, final, final, device(line + 1, near, core), (line >= root) & (line < far_size - 1))
            out_left = Link(self, final, final, device(line - 1, near, core), (line <= root) & (line > 0))
            return left, right, out_right, out_left

        def line_in(at, root, left, right, base, cols, done):
            depth = max(root, last - root)

            def begin(n):
                @pl.when(line == 0)
                def _():
                    left.start(n)

                @pl.when(line == last)
                def _():
                    right.start(n)

            def hop(k, n):
                if k < root:
                    @pl.when(line == k)
                    def _():
                        left.wait(n)
                        acc[n, base, cols] = total(acc, (n, base, cols), [got[0, n, base, cols]])
                        left.start(n)
                if last - k > root:
                    @pl.when(line == last - k)
                    def _():
                        right.wait(n)
                        acc[n, base, cols] = total(acc, (n, base, cols), [got[1, n, base, cols]])
                        right.start(n)

            def end(n):
                @pl.when(line == root)
                def _():
                    parts = []
                    if root > 0:
                        left.wait(n)
                        parts.append(got[0, n, base, cols])
                    if last > root:
                        right.wait(n)
                        parts.append(got[1, n, base, cols])
                    done(n, total(acc, (n, base, cols), parts))

            for k in range(1, depth):
                self.stage(at + k * step_line, functools.partial(hop, k))
            self.stage(at + depth * step_line, end)
            return begin, at + depth * step_line

        def line_out(at, root, out_right, out_left, then):
            def hop(k, n):
                if root + k < far_size:
                    @pl.when(line == root + k)
                    def _():
                        out_right.wait(n)
                        out_right.start(n)
                        then(n)
                if root - k >= 0:
                    @pl.when(line == root - k)
                    def _():
                        out_left.wait(n)
                        out_left.start(n)
                        then(n)

            depth = max(far_size - 1 - root, root)
            for k in range(1, depth + 1):
                self.stage(at + k * step_line, functools.partial(hop, k))
            return at + depth * step_line

        t = step_core

        if count[0]:
            base = pl.ds(first[0], count[0])
            wide = rows_of(core, first[0], count[0])
            mine = piece(0)
            spread = [
                Link(
                    self,
                    lambda n, d=d: acc.at[n, base, piece(d)],
                    lambda n, d=d: got.at[2, n, base, pl.ds((d - 1) * fine, fine)],
                    peer(d),
                    gives,
                )
                for d in range(1, near_size)
            ]
            final = lambda n: out.at[n, wide, mine]
            left, right, out_right, out_left = line_links(mid, lambda n: acc.at[n, base, mine], base, mine, final)
            fill = [Link(self, final, final, peer(d), me >= 0) for d in range(1, near_size)]
            starts += spread

            def give(n):
                for f in fill:
                    f.start(n)

            def done(n, value):
                out[n, wide, mine] = value
                out_right.start(n)
                out_left.start(n)
                give(n)

            begin, t1 = line_in(t + step_near, mid, left, right, base, mine, done)

            def gathered(n):
                @pl.when(gives)
                def _():
                    for s in spread:
                        s.wait(n)
                    acc[n, base, mine] = total(
                        acc, (n, base, mine),
                        [got[2, n, base, pl.ds((d - 1) * fine, fine)] for d in range(1, near_size)],
                    )
                    begin(n)

            self.stage(t + step_near, gathered)
            t1 = line_out(t1, mid, out_right, out_left, give) + step_near

            def filled(n):
                for d in range(1, near_size):
                    fill[d - 1].wait(n)

            self.stage(t1, filled)
            ends.append(t1)

        def whole(index, root):
            base = pl.ds(first[index], count[index])
            wide = rows_of(core, first[index], count[index])
            every = pl.ds(0, width)
            mine = piece(0)
            final = lambda n: out.at[n, wide, every]
            part = lambda n: out.at[n, wide, mine]
            left, right, out_right, out_left = line_links(root, lambda n: acc.at[n, base, every], base, every, final)
            spread = [
                Link(
                    self,
                    lambda n, d=d: acc.at[n, base, piece(d)],
                    lambda n, d=d: got.at[2, n, base, pl.ds((d - 1) * fine, fine)],
                    peer(d),
                    line == root,
                )
                for d in range(1, near_size)
            ]
            fill = [Link(self, part, part, peer(d), line == root) for d in range(1, near_size)]

            def done(n, value):
                acc[n, base, every] = value
                for s in spread:
                    s.start(n)

            begin, t1 = line_in(t, root, left, right, base, every, done)

            def gathered(n):
                @pl.when(line == root)
                def _():
                    for s in spread:
                        s.wait(n)
                    out[n, wide, mine] = total(
                        acc, (n, base, mine),
                        [got[2, n, base, pl.ds((d - 1) * fine, fine)] for d in range(1, near_size)],
                    )
                    for f in fill:
                        f.start(n)

            def filled(n):
                @pl.when(line == root)
                def _():
                    for f in fill:
                        f.wait(n)
                    out_right.start(n)
                    out_left.start(n)

            self.stage(t1 + step_near, gathered)
            self.stage(t1 + 2 * step_near, filled)
            t1 = line_out(t1 + 2 * step_near, root, out_right, out_left, lambda n: None)
            ends.append(t1)
            return begin

        begins = [whole(i, root) for i, root in ((1, mid), (2, last)) if count[i]]

        def paired(n):
            @pl.when(gives)
            def _():
                swap.wait(n)
                acc[n] = total(acc, (n,), [g[n, rows_of(core, 0, half)]])
                for s in starts:
                    s.start(n)
                for begin in begins:
                    begin(n)

        self.stage(t, paired)
        t = max(ends)
        self.stage(t, join.start)
        self.stage(t + step_core, join.wait)
        self.length = self.chunks + t + step_core

    def stage(self, at, fn):
        self.stages.append((at, fn))

    def advance(self, i, finish):
        end = max(at for at, _ in self.stages)
        for at, fn in sorted(self.stages, key=lambda s: -s[0]):
            n = i - at

            @pl.when((n >= 0) & (n < self.chunks))
            def _():
                fn(n)
                if at == end:
                    finish(n)

    def drain(self):
        for link in self.links:
            link.drain()


BLOCK = 256
RENEW_STEPS = 4
HALO_PIECES = 16
HALO_LEAD = 20
NEAR_AT = 19
NEAR_EVERY = 2


def sizes_of_seq():
    chips = lax.axis_size("seq") // CORES
    near = 1
    while near * near * 4 <= chips:
        near *= 2
    return near, chips // near


def greet(near_size, far_size):
    me = lax.axis_index("seq")
    strides = (1, CORES, CORES * near_size)
    sizes = (CORES, near_size, far_size)
    all_count = CORES * near_size * far_size
    barrier = pltpu.get_barrier_semaphore()
    targets = [{"seq": (me + d) % all_count} for d in (1, all_count - 1)]
    for stride, size in zip(strides, sizes):
        place = (me // stride) % size
        for d in range(1, size):
            targets.append({"seq": me + ((place + d) % size - place) * stride})
    mine = lax.axis_index("head")
    heads = lax.axis_size("head")
    for d in range(1, heads):
        targets.append({"head": (mine + d) % heads})
    for target in targets:
        pl.semaphore_signal(barrier, inc=1, device_id=target, device_id_type=pl.DeviceIdType.MESH)
    pl.semaphore_wait(barrier, len(targets))


def fast_output(x, wb, head):
    first = mm(x, wb[head, 0], 1, 0)
    third = mm(x, wb[head, 1], 1, 0)
    act = (first * jax.nn.sigmoid(first) * third).astype(jnp.bfloat16)
    y = mm(act, wb[head, 2], 1, 1)
    return y / jnp.sqrt(jnp.mean(y * y, axis=1, keepdims=True) + epsilon)


def share_squares(sq_all, sq_ref, sq_send, sq_recv):
    mine = lax.axis_index("head")
    heads = lax.axis_size("head")
    copies = []
    for d in range(1, heads):
        copies.append(
            pltpu.make_async_remote_copy(
                src_ref=sq_all.at[mine],
                dst_ref=sq_all.at[mine],
                send_sem=sq_send.at[d],
                recv_sem=sq_recv.at[d],
                device_id={"head": (mine + d) % heads},
                device_id_type=pl.DeviceIdType.MESH,
            )
        )
    for c in copies:
        c.start()
    for c in copies:
        c.wait()
    sq_ref[...] = jnp.sum(sq_all[...], axis=0)


def block_kernel(second, near_size, far_size, total_count, *refs):
    refs = list(refs)

    def take(count):
        out = refs[:count]
        del refs[:count]
        return out

    if second:
        edge_ref, win_ref, rate_ref, sq_in, keys, values, queries, targets, weights = take(9)
        g_in, attn = take(2)
        sums, sq_ref, mixed, base = take(4)
    else:
        edge_ref, win_ref, rate_ref, keys, values, queries, targets, weights = take(8)
        sums, sq_ref, attn = take(3)
    kbuf, qbuf, tbuf, wbuf, wb, g, res, acc, got, dbuf, stage, sq_all = take(12)
    send, recv, sq_send, sq_recv, load, wload, out_sem, stage_sem = take(8)
    vbuf, halo_send, halo_recv = take(3)
    if second:
        gbuf, mstage, in_sem, own_sem, base_sem = take(5)
    pad = WIN
    assert not refs

    heads = weights.shape[0]
    local, hd = qbuf.shape[1:]
    me = lax.axis_index("seq")
    count = lax.axis_size("seq")
    mine = lax.axis_index("head")
    anchor = me * local
    early = 8 * me < 5 * count
    late = 8 * (me + 1) > 3 * count
    works = late if second else early
    far = me // (CORES * near_size)
    line = far_size - 1 - far if second else far
    gives = line <= (5 * far_size - 1) // 8
    pieces = hd // CHUNK
    per = 3 * pieces
    blocks = local // BLOCK
    units = blocks * heads
    begin = (heads - 1) * (per - 1)
    ahead = per - 3
    assert blocks % ahead == 0
    halo_blocks = WIN // BLOCK
    plain = (blocks - halo_blocks) * heads
    here = heads - heads // 2

    low, away = (here, heads - here) if second else (0, here)

    def own_values(h):
        k = h - low
        return pltpu.make_async_copy(columns(values, h, pl.ds(0, WIN)), vbuf.at[k, pl.ds(WIN, WIN)], own_sem.at[k])

    def attention(q, v_all, h, start):
        span = WIN + BLOCK
        scores = mm(q, kbuf[h, pl.ds(start, span)], 1, 1) * (hd ** (-0.5))
        row = lax.broadcasted_iota(jnp.int32, (BLOCK, span), 0)
        colm = lax.broadcasted_iota(jnp.int32, (BLOCK, span), 1)
        back = row + WIN - colm
        live = (back >= 0) & (back < win_ref[h]) & (colm >= WIN - start - anchor)
        scores = jnp.where(live, scores, -1e30)
        peak = jnp.max(scores, axis=1, keepdims=True)
        expo = jnp.exp(scores - peak)
        probs = (expo * (1.0 / jnp.sum(expo, axis=1, keepdims=True))).astype(jnp.bfloat16)
        return mm(probs, v_all[pl.ds(start, span)], 1, 0)
    edge = edge_ref[0]

    def columns(ref, h, rows=None):
        cols = pl.ds(pl.multiple_of(h * hd, 128), hd)
        return ref.at[pl.ds(0, local) if rows is None else rows, cols]

    def load_weights(h):
        copies = [pltpu.make_async_copy(weights.at[h], wbuf, wload.at[0])]
        if second:
            copies.append(
                pltpu.make_async_copy(g_in.at[pl.ds(pl.multiple_of(h * per, per), per)], gbuf, wload.at[1])
            )
        return copies

    def load_one(i, h):
        src = (keys, targets, queries, None if second else values)[i]
        dst = (kbuf, tbuf, qbuf, None if second else vbuf)[i]
        at = dst.at[h, pl.ds(pad, local)] if i in (0, 3) else dst.at[h]
        return pltpu.make_async_copy(columns(src, h), at, load.at[i, h])

    def place(u):
        return blocks - 1 - u // heads, u % heads

    def block_of(ref, block, h):
        return columns(ref, h, pl.ds(pl.multiple_of(block * BLOCK, BLOCK), BLOCK))

    def attn_in(u):
        return pltpu.make_async_copy(block_of(attn, *place(u)), stage.at[u % 2], in_sem.at[u % 2])

    def block_out(block, h, slot):
        src, dst = (mstage, mixed) if second else (stage, attn)
        return pltpu.make_async_copy(src.at[slot], block_of(dst, block, h), stage_sem.at[slot])

    for c in load_weights(0):
        c.start()
    for i in (0, 1):
        load_one(i, 0).start()
    sq_all[mine] = jnp.zeros(sq_all.shape[1:], jnp.float32)

    @pl.when(gives & jnp.logical_not(works))
    def _():
        @pl.loop(0, g.shape[0])
        def _(n):
            g[n] = jnp.zeros(g.shape[1:], g.dtype)

    if away:

        @pl.when(me == 0)
        def _():
            @pl.loop(0, away)
            def _(k):
                kbuf[low + k, pl.ds(0, WIN)] = jnp.zeros((WIN, hd), kbuf.dtype)
                vbuf[k, pl.ds(0, WIN)] = jnp.zeros((WIN, hd), vbuf.dtype)

    greet(near_size, far_size)

    def halo(h, first=0, size=WIN):
        rows = pl.ds(pl.multiple_of(local - WIN + first, 16), size)
        out = []
        for i, (src, dst) in enumerate(((keys, kbuf.at[h]), (values, vbuf.at[h - low]))):
            out.append(
                pltpu.make_async_remote_copy(
                    src_ref=columns(src, h, rows),
                    dst_ref=dst.at[pl.ds(first, size)],
                    send_sem=halo_send.at[i],
                    recv_sem=halo_recv.at[i, h - low],
                    device_id={"seq": me + 1},
                    device_id_type=pl.DeviceIdType.MESH,
                )
            )
        return out

    netw = Net(second, near_size, far_size, g, res, acc, got, send, recv)

    def position(rows):
        return anchor + rows + lax.broadcasted_iota(jnp.int32, (BLOCK, 1), 0)

    def keep(h):
        return pltpu.make_async_copy(wbuf, base.at[h], base_sem.at[0])

    def load_next(h):
        @pl.when(h + 1 < heads)
        def _():
            for c in load_weights(h + 1):
                c.start()

    def prepare(h):
        for c in load_weights(h):
            c.wait()
        if second:
            coef = fast_rate / jnp.sqrt(jnp.sum(sq_in[...]) / total_count + epsilon)
        for j in range(3):
            for p in range(pieces):
                rows = pl.ds(p * CHUNK, CHUNK)
                w = wbuf[j, rows]
                if second:
                    w = w - coef * gbuf[j * pieces + p].astype(jnp.float32)
                    wbuf[j, rows] = w
                wb[h, j, rows] = w.astype(jnp.bfloat16)

        if second:
            keep(h).start()
        else:
            load_next(h)

    def backward(h, kind):
        @pl.when(kind == 0)
        def _():
            for k in (0, 1):
                load_one(k, h).wait()

        for turn in range(0, blocks, ahead):
            b = kind + turn
            start = pl.multiple_of(b * BLOCK, BLOCK)
            rows = pl.ds(start, BLOCK)
            x = kbuf[h, pl.ds(pad + start, BLOCK)]
            rate = rate_ref[pl.ds(h, 1), rows]
            down = lax.broadcasted_iota(jnp.int32, (BLOCK, BLOCK), 0)
            across = lax.broadcasted_iota(jnp.int32, (BLOCK, BLOCK), 1)
            scaled = jnp.sum(jnp.where(down == across, rate, 0.0), axis=1, keepdims=True)
            inside = (position(start) >= edge) if second else (position(start) < edge)
            scaled = scaled * jnp.where(inside, 1.0, 0.0)
            first = mm(x, wb[h, 0], 1, 0)
            third = mm(x, wb[h, 1], 1, 0)
            d_out = (-scaled * tbuf[h, rows].astype(jnp.float32)).astype(jnp.bfloat16)
            d_act = mm(d_out, wb[h, 2], 1, 0)
            sigma = jax.nn.sigmoid(first)
            swish = first * sigma
            dbuf[0, rows] = (d_act * third * sigma * (1.0 + first * (1.0 - sigma))).astype(jnp.bfloat16)
            dbuf[1, rows] = (d_act * swish).astype(jnp.bfloat16)
            dbuf[2, rows] = (swish * third).astype(jnp.bfloat16)
            dbuf[3, rows] = d_out

    def outer(h, j):
        left = kbuf[h, pl.ds(pad, local)] if j < 2 else dbuf[3]
        value = mm(left, dbuf[j], 0, 0).astype(jnp.bfloat16)
        for p in range(pieces):
            g[h * per + j * pieces + p] = value[p * CHUNK : (p + 1) * CHUNK]

    def attend(block, h, order):
        start = pl.multiple_of(block * BLOCK, BLOCK)
        slot = order % 2

        @pl.when(block == blocks - 1)
        def _():
            for k in (2, 3):
                load_one(k, h).wait()

            @pl.when(jnp.logical_not(early))
            def _():
                for k in (0, 1):
                    load_one(k, h).wait()

        @pl.when((block == halo_blocks - 1) & (h < here) & (me > 0))
        def _():
            for c in halo(h):
                c.wait_recv()

        @pl.when(order >= 2)
        def _():
            block_out(block, h, slot).wait()

        q = qbuf[h, pl.ds(start, BLOCK)]
        inside = (block >= halo_blocks) | (h < here)

        @pl.when(inside)
        def _():
            stage[slot] = attention(q, vbuf.at[h], h, start)

        @pl.when(jnp.logical_not(inside))
        def _():
            stage[slot] = jnp.zeros(stage.shape[1:], jnp.float32)

        @pl.when(early)
        def _():
            y = fast_output(q, wb, h)
            stage[slot] += jnp.where(position(start) < edge, y, 0.0)

        block_out(block, h, slot).start()

    def combine(u):
        block, h = place(u)
        start = pl.multiple_of(block * BLOCK, BLOCK)
        slot = u % 2

        @pl.when(u + 1 < units)
        def _():
            attn_in(u + 1).start()

        attn_in(u).wait()

        @pl.when(block == blocks - 1)
        def _():
            load_one(2, h).wait()

            @pl.when(jnp.logical_not(late))
            def _():
                for k in (0, 1):
                    load_one(k, h).wait()

        @pl.when(u >= 2)
        def _():
            block_out(block, h, slot).wait()

        if here < heads:

            @pl.when((block == halo_blocks - 1) & (h >= here))
            def _():
                own_values(h).wait()

            @pl.when((block == halo_blocks - 1) & (h >= here) & (me > 0))
            def _():
                for c in halo(h):
                    c.wait_recv()

            @pl.when((block < halo_blocks) & (h >= here))
            def _():
                q = qbuf[h, pl.ds(start, BLOCK)]
                stage[slot] += attention(q, vbuf.at[h - here], h, start)

        @pl.when(late)
        def _():
            y = fast_output(qbuf[h, pl.ds(start, BLOCK)], wb, h)
            mstage[slot] = (stage[slot] + jnp.where(position(start) >= edge, y, 0.0)).astype(jnp.bfloat16)

        @pl.when(jnp.logical_not(late))
        def _():
            mstage[slot] = stage[slot].astype(jnp.bfloat16)

        block_out(block, h, slot).start()

    def put(n):
        return pltpu.make_async_copy(res.at[n], sums.at[n], out_sem.at[0])

    def finish(n):
        put(n).start()
        part = jnp.square(res[n].astype(jnp.float32))
        sq_all[mine] += jnp.sum(part.reshape(-1, *sq_all.shape[1:]), axis=0)

    def gradient(i):
        h = i // per
        kind = i % per

        @pl.when((h < heads) & works)
        def _():
            @pl.when(kind < ahead)
            def _():
                backward(h, kind)

            for j in range(3):

                @pl.when(kind == ahead + j)
                def _():
                    outer(h, j)

        if second:

            @pl.when((h < heads) & (kind == 1))
            def _():
                keep(h).wait()
                load_next(h)

        @pl.when((h < heads - 1) & (kind == per - 1) & prepares)
        def _():
            prepare(h + 1)

    def send_halo(i):
        size = WIN // HALO_PIECES

        @pl.when((i < away * HALO_PIECES) & (me < count - 1))
        def _():
            for c in halo(low + i // HALO_PIECES, pl.multiple_of((i % HALO_PIECES) * size, size), size):
                c.start()

    if away:

        @pl.loop(0, HALO_LEAD)
        def _(i):
            send_halo(i)

    prepares = (me >= 0) if second else works

    @pl.when(prepares)
    def _():
        prepare(0)

    for h in range(heads):
        for i in (0, 1, 2) if second else (0, 1, 2, 3):
            if h > 0 or i > 1:
                load_one(i, h).start()
    if second:
        attn_in(0).start()
        for h in range(here, heads):
            own_values(h).start()

    @pl.loop(0, ahead)
    def _(i):
        gradient(i)

    if second:
        steps = [begin + units]
    else:
        near_at = max(NEAR_AT, begin + plain)
        steps = [begin + plain, near_at + NEAR_EVERY * (units - plain)]

    @pl.loop(0, max(netw.length, *steps))
    def _(i):
        if away:

            send_halo(i + HALO_LEAD)


        gradient(i + ahead)

        netw.advance(i, finish)
        u = i - begin
        if second:

            @pl.when((u >= 0) & (u < units))
            def _():
                combine(u)
        else:

            @pl.when((u >= 0) & (u < plain))
            def _():
                block, h = place(u)
                attend(block, h, u)

            v = i - near_at
            w = v // NEAR_EVERY

            @pl.when((v >= 0) & (v % NEAR_EVERY == 0) & (w < units - plain))
            def _():
                attend(halo_blocks - 1 - w % halo_blocks, w // halo_blocks, plain + w)

    share_squares(sq_all, sq_ref, sq_send, sq_recv)
    netw.drain()
    if away:

        @pl.when(me < count - 1)
        def _():
            for i in range(2):
                every = kbuf.at[pl.ds(low, away), pl.ds(0, WIN)]
                pltpu.make_async_remote_copy(
                    src_ref=every, dst_ref=every, send_sem=halo_send.at[i], recv_sem=halo_recv.at[i, 0],
                    device_id={"seq": me + 1}, device_id_type=pl.DeviceIdType.MESH,
                ).wait_send()

    if not second:

        @pl.when(jnp.logical_not(works))
        def _():
            for c in load_weights(0):
                c.wait()

    for slot in range(2):
        block_out(0, 0, slot).wait()
    pltpu.make_async_copy(res, sums, out_sem.at[0]).wait()


def block_step(second, arrays, total_count):
    near, far = sizes_of_seq()
    if second:
        keys, weights = arrays[4], arrays[8]
    else:
        keys, weights = arrays[3], arrays[7]
    heads, _, hd, hid = weights.shape
    local = keys.shape[0]
    chunks = heads * 3 * hd // CHUNK
    vmem = pl.BlockSpec(memory_space=pltpu.VMEM)
    smem = pl.BlockSpec(memory_space=pltpu.SMEM)
    hbm = pl.BlockSpec(memory_space=pl.ANY)
    half = CHUNK // CORES
    more = (jax.ShapeDtypeStruct(weights.shape, jnp.float32),) if second else ()
    kinds = link_kinds(near)
    ranks = lax.axis_size("head")
    dma = pltpu.SemaphoreType.DMA
    bf16, f32 = jnp.bfloat16, jnp.float32
    pad = WIN
    away = max(heads // 2, 1)
    scratch = [
        pltpu.VMEM((heads, pad + local, hd), bf16),
        pltpu.VMEM((heads, local, hd), bf16),
        pltpu.VMEM((heads, local, hd), bf16),
        pltpu.VMEM((3, hd, hid), f32),
        pltpu.VMEM((heads, 3, hd, hid), bf16),
        pltpu.VMEM((chunks, CHUNK, hid), bf16),
        pltpu.VMEM((chunks, CHUNK, hid), bf16),
        pltpu.VMEM((chunks, half, hid), bf16),
        pltpu.VMEM((3, chunks, half, hid), bf16),
        pltpu.VMEM((4, local, hd), bf16),
        pltpu.VMEM((2, BLOCK, hd), f32),
        pltpu.VMEM((ranks, 8, hid), f32),
        dma((kinds,)),
        dma((kinds, chunks)),
        dma((ranks,)),
        dma((ranks,)),
        dma((4, heads)),
        dma((2,)),
        dma((1,)),
        dma((2,)),
    ]
    scratch += [
        pltpu.VMEM((away, 2 * WIN, hd) if second else (heads, pad + local, hd), bf16),
        dma((2,)),
        dma((2, heads)),
    ]
    if second:
        scratch += [
            pltpu.VMEM((3 * hd // CHUNK, CHUNK, hid), bf16),
            pltpu.VMEM((2, BLOCK, hd), bf16),
            dma((2,)),
            dma((away,)),
            dma((1,)),
        ]
        in_specs = [smem, smem, vmem, vmem] + [hbm] * 7
        wide = jax.ShapeDtypeStruct(keys.shape, bf16)
    else:
        in_specs = [smem, smem, vmem, hbm, hbm, hbm, hbm, hbm]
        wide = jax.ShapeDtypeStruct(keys.shape, f32)
    return pl.pallas_call(
        functools.partial(block_kernel, second, near, far, total_count),
        in_specs=in_specs,
        out_specs=(hbm, vmem, hbm) + (hbm,) * len(more),
        out_shape=(
            jax.ShapeDtypeStruct((chunks, CHUNK, hid), bf16),
            jax.ShapeDtypeStruct((8, hid), f32),
            wide,
        )
        + more,
        scratch_shapes=scratch,
        compiler_params=pltpu.CompilerParams(
            collective_id=int(second), has_side_effects=True, vmem_limit_bytes=67043328
        ),
        cost_estimate=pl.CostEstimate(flops=10**11, bytes_accessed=60 << 20, transcendentals=0),
        name="second" if second else "first",
    )(*arrays)


def renew_kernel(total_count, sq_ref, w_ref, g_ref, mixed_ref, out_ref, copy_ref):
    coef = fast_rate / jnp.sqrt(jnp.sum(sq_ref[...]) / total_count + epsilon)
    out_ref[...] = w_ref[...] - coef * g_ref[...].astype(jnp.float32)
    copy_ref[...] = mixed_ref[...]


def renew(total_count, sq, weights, g, mixed):
    flat = (-1, weights.shape[-1])
    w = weights.reshape(flat)
    steps = RENEW_STEPS
    small = pl.BlockSpec(sq.shape, lambda i: (0, 0))
    tile = pl.BlockSpec((w.shape[0] // steps, w.shape[1]), lambda i: (i, 0))
    rows = pl.BlockSpec((mixed.shape[0] // steps, mixed.shape[1]), lambda i: (i, 0))
    out, mixed = pl.pallas_call(
        functools.partial(renew_kernel, total_count),
        grid=(steps,),
        in_specs=[small, tile, tile, rows],
        out_specs=(tile, rows),
        out_shape=(
            jax.ShapeDtypeStruct(w.shape, jnp.float32),
            jax.ShapeDtypeStruct(mixed.shape, mixed.dtype),
        ),
        compiler_params=pltpu.CompilerParams(vmem_limit_bytes=67043328),
        cost_estimate=pl.CostEstimate(flops=4 * w.size, bytes_accessed=16 * w.size, transcendentals=0),
        name="renew",
    )(sq, w, g.reshape(flat), mixed)
    return mixed, out.reshape(weights.shape)


def per_device(queries, keys, values, targets, token_rate, window, split, fast_init):
    total_count = float(fast_init.size * lax.axis_size("head"))
    g0, sq0, attn = block_step(
        False, (split, window, token_rate.T, keys, values, queries, targets, fast_init), total_count
    )
    g1, sq1, mixed, base = block_step(
        True,
        (split, window, token_rate.T, sq0, keys, values, queries, targets, fast_init, g0, attn),
        total_count,
    )
    return renew(total_count, sq1, base, g1, mixed)


def solution(mesh):
    return jax.shard_map(
        per_device,
        mesh=mesh,
        in_specs=(
            P("seq", "head"),
            P("seq", "head"),
            P("seq", "head"),
            P("seq", "head"),
            P("seq", "head"),
            P("head"),
            P(),
            P("head", None, None, None),
        ),
        out_specs=(P("seq", "head"), P("head", None, None, None)),
        check_vma=False,
    )
```

```python
import functools

import jax
import jax.numpy as jnp
from jax import lax
from jax.experimental import pallas as pl
from jax.experimental.pallas import tpu as pltpu
from jax.sharding import PartitionSpec as P

WIN = 512
fast_rate = 0.01
epsilon = 1e-06
CORES = 2


def mm(a, b, ca, cb):
    return lax.dot_general(
        a, b, (((ca,), (cb,)), ((), ())), preferred_element_type=jnp.float32
    )


SHARES = ((8, 4, 4), (8, 4, 4))
STEPS = ((2, 2, 2), (2, 2, 2))
CHUNK = 256


class Link:
    def __init__(self, net, src, dst, to, gives):
        self.net, self.src, self.dst, self.to, self.gives = net, src, dst, to, gives
        self.kind = len(net.links)
        net.links.append(self)

    def copy(self, n, slot):
        return pltpu.make_async_remote_copy(
            src_ref=self.src(n),
            dst_ref=self.dst(n),
            send_sem=self.net.send.at[self.kind],
            recv_sem=self.net.recv.at[self.kind, slot],
            device_id={"seq": self.to},
            device_id_type=pl.DeviceIdType.MESH,
        )

    def start(self, n):
        @pl.when(self.gives)
        def _():
            self.copy(n, n).start()

    def wait(self, n):
        self.copy(n, n).wait_recv()

    def drain(self):
        @pl.when(self.gives)
        def _():
            self.copy(pl.ds(0, self.net.chunks), 0).wait_send()


def total(ref, at, parts):
    out = ref[at].astype(jnp.float32)
    for part in parts:
        out += part.astype(jnp.float32)
    return out.astype(ref.dtype)


def link_kinds(near):
    return 2 + (4 + 2 * (near - 1)) + 2 * (4 + 2 * (near - 1))


class Net:
    def __init__(self, mirror, near_size, far_size, g, out, acc, got, send, recv):
        self.links, self.stages = [], []
        self.send, self.recv = send, recv
        self.chunks, rows, width = g.shape
        half = rows // CORES
        fine = width // near_size
        me = lax.axis_index("seq")
        core = me % CORES
        near = (me // CORES) % near_size
        far = me // (CORES * near_size)
        line = far_size - 1 - far if mirror else far
        last = (5 * far_size - 1) // 8
        gives = line <= last
        step_core, step_near, step_line = STEPS[mirror]

        def device(line_to, near_to, core_to):
            far_to = far_size - 1 - line_to if mirror else line_to
            return (far_to * near_size + near_to) * CORES + core_to

        def peer(d):
            return device(line, (near + d) % near_size, core)

        def piece(d):
            index = (near + d) % near_size
            return pl.ds(pl.multiple_of(index * fine, 128), fine)

        def rows_of(c, first, count):
            return pl.ds(pl.multiple_of(c * half + first, 16), count)

        other = 1 - core
        mate = device(line, near, other)
        swap = Link(self, lambda n: g.at[n, rows_of(other, 0, half)], lambda n: acc.at[n], mate, gives)
        join = Link(
            self,
            lambda n: out.at[n, rows_of(core, 0, half)],
            lambda n: out.at[n, rows_of(core, 0, half)],
            mate,
            me >= 0,
        )
        self.stage(0, swap.start)

        shares = SHARES[mirror]
        unit = half // sum(shares)
        count = [s * unit for s in shares]
        first = [sum(count[:i]) for i in range(3)]
        mid = last // 2
        ends = []
        starts = []

        def line_links(root, src, base, n_cols, final):
            left = Link(self, src, lambda n: got.at[0, n, base, n_cols], device(line + 1, near, core), line < root)
            right = Link(
                self, src, lambda n: got.at[1, n, base, n_cols], device(line - 1, near, core),
                (line > root) & gives,
            )
            out_right = Link(self, final, final, device(line + 1, near, core), (line >= root) & (line < far_size - 1))
            out_left = Link(self, final, final, device(line - 1, near, core), (line <= root) & (line > 0))
            return left, right, out_right, out_left

        def line_in(at, root, left, right, base, cols, done):
            depth = max(root, last - root)

            def begin(n):
                @pl.when(line == 0)
                def _():
                    left.start(n)

                @pl.when(line == last)
                def _():
                    right.start(n)

            def hop(k, n):
                if k < root:
                    @pl.when(line == k)
                    def _():
                        left.wait(n)
                        acc[n, base, cols] = total(acc, (n, base, cols), [got[0, n, base, cols]])
                        left.start(n)
                if last - k > root:
                    @pl.when(line == last - k)
                    def _():
                        right.wait(n)
                        acc[n, base, cols] = total(acc, (n, base, cols), [got[1, n, base, cols]])
                        right.start(n)

            def end(n):
                @pl.when(line == root)
                def _():
                    parts = []
                    if root > 0:
                        left.wait(n)
                        parts.append(got[0, n, base, cols])
                    if last > root:
                        right.wait(n)
                        parts.append(got[1, n, base, cols])
                    done(n, total(acc, (n, base, cols), parts))

            for k in range(1, depth):
                self.stage(at + k * step_line, functools.partial(hop, k))
            self.stage(at + depth * step_line, end)
            return begin, at + depth * step_line

        def line_out(at, root, out_right, out_left, then):
            def hop(k, n):
                if root + k < far_size:
                    @pl.when(line == root + k)
                    def _():
                        out_right.wait(n)
                        out_right.start(n)
                        then(n)
                if root - k >= 0:
                    @pl.when(line == root - k)
                    def _():
                        out_left.wait(n)
                        out_left.start(n)
                        then(n)

            depth = max(far_size - 1 - root, root)
            for k in range(1, depth + 1):
                self.stage(at + k * step_line, functools.partial(hop, k))
            return at + depth * step_line

        t = step_core

        if count[0]:
            base = pl.ds(first[0], count[0])
            wide = rows_of(core, first[0], count[0])
            mine = piece(0)
            spread = [
                Link(
                    self,
                    lambda n, d=d: acc.at[n, base, piece(d)],
                    lambda n, d=d: got.at[2, n, base, pl.ds((d - 1) * fine, fine)],
                    peer(d),
                    gives,
                )
                for d in range(1, near_size)
            ]
            final = lambda n: out.at[n, wide, mine]
            left, right, out_right, out_left = line_links(mid, lambda n: acc.at[n, base, mine], base, mine, final)
            fill = [Link(self, final, final, peer(d), me >= 0) for d in range(1, near_size)]
            starts += spread

            def give(n):
                for f in fill:
                    f.start(n)

            def done(n, value):
                out[n, wide, mine] = value
                out_right.start(n)
                out_left.start(n)
                give(n)

            begin, t1 = line_in(t + step_near, mid, left, right, base, mine, done)

            def gathered(n):
                @pl.when(gives)
                def _():
                    for s in spread:
                        s.wait(n)
                    acc[n, base, mine] = total(
                        acc, (n, base, mine),
                        [got[2, n, base, pl.ds((d - 1) * fine, fine)] for d in range(1, near_size)],
                    )
                    begin(n)

            self.stage(t + step_near, gathered)
            t1 = line_out(t1, mid, out_right, out_left, give) + step_near

            def filled(n):
                for d in range(1, near_size):
                    fill[d - 1].wait(n)

            self.stage(t1, filled)
            ends.append(t1)

        def whole(index, root):
            base = pl.ds(first[index], count[index])
            wide = rows_of(core, first[index], count[index])
            every = pl.ds(0, width)
            mine = piece(0)
            final = lambda n: out.at[n, wide, every]
            part = lambda n: out.at[n, wide, mine]
            left, right, out_right, out_left = line_links(root, lambda n: acc.at[n, base, every], base, every, final)
            spread = [
                Link(
                    self,
                    lambda n, d=d: acc.at[n, base, piece(d)],
                    lambda n, d=d: got.at[2, n, base, pl.ds((d - 1) * fine, fine)],
                    peer(d),
                    line == root,
                )
                for d in range(1, near_size)
            ]
            fill = [Link(self, part, part, peer(d), line == root) for d in range(1, near_size)]

            def done(n, value):
                acc[n, base, every] = value
                for s in spread:
                    s.start(n)

            begin, t1 = line_in(t, root, left, right, base, every, done)

            def gathered(n):
                @pl.when(line == root)
                def _():
                    for s in spread:
                        s.wait(n)
                    out[n, wide, mine] = total(
                        acc, (n, base, mine),
                        [got[2, n, base, pl.ds((d - 1) * fine, fine)] for d in range(1, near_size)],
                    )
                    for f in fill:
                        f.start(n)

            def filled(n):
                @pl.when(line == root)
                def _():
                    for f in fill:
                        f.wait(n)
                    out_right.start(n)
                    out_left.start(n)

            self.stage(t1 + step_near, gathered)
            self.stage(t1 + 2 * step_near, filled)
            t1 = line_out(t1 + 2 * step_near, root, out_right, out_left, lambda n: None)
            ends.append(t1)
            return begin

        begins = [whole(i, root) for i, root in ((1, mid), (2, last)) if count[i]]

        def paired(n):
            @pl.when(gives)
            def _():
                swap.wait(n)
                acc[n] = total(acc, (n,), [g[n, rows_of(core, 0, half)]])
                for s in starts:
                    s.start(n)
                for begin in begins:
                    begin(n)

        self.stage(t, paired)
        t = max(ends)
        self.stage(t, join.start)
        self.stage(t + step_core, join.wait)
        self.length = self.chunks + t + step_core

    def stage(self, at, fn):
        self.stages.append((at, fn))

    def advance(self, i, finish):
        end = max(at for at, _ in self.stages)
        for at, fn in sorted(self.stages, key=lambda s: -s[0]):
            n = i - at

            @pl.when((n >= 0) & (n < self.chunks))
            def _():
                fn(n)
                if at == end:
                    finish(n)

    def drain(self):
        for link in self.links:
            link.drain()


BLOCK = 256
RENEW_STEPS = 3
HALO_PIECES = 16
HALO_LEAD = 20
NEAR_AT = 19
NEAR_EVERY = 2


def sizes_of_seq():
    chips = lax.axis_size("seq") // CORES
    near = 1
    while near * near * 4 <= chips:
        near *= 2
    return near, chips // near


def greet(near_size, far_size):
    me = lax.axis_index("seq")
    strides = (1, CORES, CORES * near_size)
    sizes = (CORES, near_size, far_size)
    all_count = CORES * near_size * far_size
    barrier = pltpu.get_barrier_semaphore()
    targets = [{"seq": (me + d) % all_count} for d in (1, all_count - 1)]
    for stride, size in zip(strides, sizes):
        place = (me // stride) % size
        for d in range(1, size):
            targets.append({"seq": me + ((place + d) % size - place) * stride})
    mine = lax.axis_index("head")
    heads = lax.axis_size("head")
    for d in range(1, heads):
        targets.append({"head": (mine + d) % heads})
    for target in targets:
        pl.semaphore_signal(barrier, inc=1, device_id=target, device_id_type=pl.DeviceIdType.MESH)
    pl.semaphore_wait(barrier, len(targets))


def fast_output(x, wb, head):
    first = mm(x, wb[head, 0], 1, 0)
    third = mm(x, wb[head, 1], 1, 0)
    act = (first * jax.nn.sigmoid(first) * third).astype(jnp.bfloat16)
    y = mm(act, wb[head, 2], 1, 1)
    return y / jnp.sqrt(jnp.mean(y * y, axis=1, keepdims=True) + epsilon)


def share_squares(sq_all, sq_ref, sq_send, sq_recv):
    mine = lax.axis_index("head")
    heads = lax.axis_size("head")
    copies = []
    for d in range(1, heads):
        copies.append(
            pltpu.make_async_remote_copy(
                src_ref=sq_all.at[mine],
                dst_ref=sq_all.at[mine],
                send_sem=sq_send.at[d],
                recv_sem=sq_recv.at[d],
                device_id={"head": (mine + d) % heads},
                device_id_type=pl.DeviceIdType.MESH,
            )
        )
    for c in copies:
        c.start()
    for c in copies:
        c.wait()
    sq_ref[...] = jnp.sum(sq_all[...], axis=0)


def block_kernel(second, near_size, far_size, total_count, *refs):
    refs = list(refs)

    def take(count):
        out = refs[:count]
        del refs[:count]
        return out

    if second:
        edge_ref, win_ref, rate_ref, sq_in, keys, values, queries, targets, weights = take(9)
        g_in, attn = take(2)
        sums, sq_ref, mixed, base = take(4)
    else:
        edge_ref, win_ref, rate_ref, keys, values, queries, targets, weights = take(8)
        sums, sq_ref, attn = take(3)
    kbuf, qbuf, tbuf, wbuf, wb, g, res, acc, got, dbuf, stage, sq_all = take(12)
    send, recv, sq_send, sq_recv, load, wload, out_sem, stage_sem = take(8)
    vbuf, halo_send, halo_recv = take(3)
    if second:
        gbuf, mstage, in_sem, own_sem, base_sem = take(5)
    pad = WIN
    assert not refs

    heads = weights.shape[0]
    local, hd = qbuf.shape[1:]
    me = lax.axis_index("seq")
    count = lax.axis_size("seq")
    mine = lax.axis_index("head")
    anchor = me * local
    early = 8 * me < 5 * count
    late = 8 * (me + 1) > 3 * count
    works = late if second else early
    far = me // (CORES * near_size)
    line = far_size - 1 - far if second else far
    gives = line <= (5 * far_size - 1) // 8
    pieces = hd // CHUNK
    per = 3 * pieces
    blocks = local // BLOCK
    units = blocks * heads
    begin = (heads - 1) * (per - 1)
    ahead = per - 3
    assert blocks % ahead == 0
    halo_blocks = WIN // BLOCK
    plain = (blocks - halo_blocks) * heads
    here = heads - heads // 2

    low, away = (here, heads - here) if second else (0, here)

    def own_values(h):
        k = h - low
        return pltpu.make_async_copy(columns(values, h, pl.ds(0, WIN)), vbuf.at[k, pl.ds(WIN, WIN)], own_sem.at[k])

    def attention(q, v_all, h, start):
        span = WIN + BLOCK
        scores = mm(q, kbuf[h, pl.ds(start, span)], 1, 1) * (hd ** (-0.5))
        row = lax.broadcasted_iota(jnp.int32, (BLOCK, span), 0)
        colm = lax.broadcasted_iota(jnp.int32, (BLOCK, span), 1)
        back = row + WIN - colm
        live = (back >= 0) & (back < win_ref[h]) & (colm >= WIN - start - anchor)
        scores = jnp.where(live, scores, -1e30)
        peak = jnp.max(scores, axis=1, keepdims=True)
        expo = jnp.exp(scores - peak)
        probs = (expo * (1.0 / jnp.sum(expo, axis=1, keepdims=True))).astype(jnp.bfloat16)
        return mm(probs, v_all[pl.ds(start, span)], 1, 0)
    edge = edge_ref[0]

    def columns(ref, h, rows=None):
        cols = pl.ds(pl.multiple_of(h * hd, 128), hd)
        return ref.at[pl.ds(0, local) if rows is None else rows, cols]

    def load_weights(h):
        copies = [pltpu.make_async_copy(weights.at[h], wbuf, wload.at[0])]
        if second:
            copies.append(
                pltpu.make_async_copy(g_in.at[pl.ds(pl.multiple_of(h * per, per), per)], gbuf, wload.at[1])
            )
        return copies

    def load_one(i, h):
        src = (keys, targets, queries, None if second else values)[i]
        dst = (kbuf, tbuf, qbuf, None if second else vbuf)[i]
        at = dst.at[h, pl.ds(pad, local)] if i in (0, 3) else dst.at[h]
        return pltpu.make_async_copy(columns(src, h), at, load.at[i, h])

    def place(u):
        return blocks - 1 - u // heads, u % heads

    def block_of(ref, block, h):
        return columns(ref, h, pl.ds(pl.multiple_of(block * BLOCK, BLOCK), BLOCK))

    def attn_in(u):
        return pltpu.make_async_copy(block_of(attn, *place(u)), stage.at[u % 2], in_sem.at[u % 2])

    def block_out(block, h, slot):
        src, dst = (mstage, mixed) if second else (stage, attn)
        return pltpu.make_async_copy(src.at[slot], block_of(dst, block, h), stage_sem.at[slot])

    for c in load_weights(0):
        c.start()
    for i in (0, 1):
        load_one(i, 0).start()
    sq_all[mine] = jnp.zeros(sq_all.shape[1:], jnp.float32)

    @pl.when(gives & jnp.logical_not(works))
    def _():
        @pl.loop(0, g.shape[0])
        def _(n):
            g[n] = jnp.zeros(g.shape[1:], g.dtype)

    if away:

        @pl.when(me == 0)
        def _():
            @pl.loop(0, away)
            def _(k):
                kbuf[low + k, pl.ds(0, WIN)] = jnp.zeros((WIN, hd), kbuf.dtype)
                vbuf[k, pl.ds(0, WIN)] = jnp.zeros((WIN, hd), vbuf.dtype)

    greet(near_size, far_size)

    def halo(h, first=0, size=WIN):
        rows = pl.ds(pl.multiple_of(local - WIN + first, 16), size)
        out = []
        for i, (src, dst) in enumerate(((keys, kbuf.at[h]), (values, vbuf.at[h - low]))):
            out.append(
                pltpu.make_async_remote_copy(
                    src_ref=columns(src, h, rows),
                    dst_ref=dst.at[pl.ds(first, size)],
                    send_sem=halo_send.at[i],
                    recv_sem=halo_recv.at[i, h - low],
                    device_id={"seq": me + 1},
                    device_id_type=pl.DeviceIdType.MESH,
                )
            )
        return out

    netw = Net(second, near_size, far_size, g, res, acc, got, send, recv)

    def position(rows):
        return anchor + rows + lax.broadcasted_iota(jnp.int32, (BLOCK, 1), 0)

    def keep(h):
        return pltpu.make_async_copy(wbuf, base.at[h], base_sem.at[0])

    def load_next(h):
        @pl.when(h + 1 < heads)
        def _():
            for c in load_weights(h + 1):
                c.start()

    def prepare(h):
        for c in load_weights(h):
            c.wait()
        if second:
            coef = fast_rate / jnp.sqrt(jnp.sum(sq_in[...]) / total_count + epsilon)
        for j in range(3):
            for p in range(pieces):
                rows = pl.ds(p * CHUNK, CHUNK)
                w = wbuf[j, rows]
                if second:
                    w = w - coef * gbuf[j * pieces + p].astype(jnp.float32)
                    wbuf[j, rows] = w
                wb[h, j, rows] = w.astype(jnp.bfloat16)

        if second:
            keep(h).start()
        else:
            load_next(h)

    def backward(h, kind):
        @pl.when(kind == 0)
        def _():
            for k in (0, 1):
                load_one(k, h).wait()

        for turn in range(0, blocks, ahead):
            b = kind + turn
            start = pl.multiple_of(b * BLOCK, BLOCK)
            rows = pl.ds(start, BLOCK)
            x = kbuf[h, pl.ds(pad + start, BLOCK)]
            rate = rate_ref[pl.ds(h, 1), rows]
            down = lax.broadcasted_iota(jnp.int32, (BLOCK, BLOCK), 0)
            across = lax.broadcasted_iota(jnp.int32, (BLOCK, BLOCK), 1)
            scaled = jnp.sum(jnp.where(down == across, rate, 0.0), axis=1, keepdims=True)
            inside = (position(start) >= edge) if second else (position(start) < edge)
            scaled = scaled * jnp.where(inside, 1.0, 0.0)
            first = mm(x, wb[h, 0], 1, 0)
            third = mm(x, wb[h, 1], 1, 0)
            d_out = (-scaled * tbuf[h, rows].astype(jnp.float32)).astype(jnp.bfloat16)
            d_act = mm(d_out, wb[h, 2], 1, 0)
            sigma = jax.nn.sigmoid(first)
            swish = first * sigma
            dbuf[0, rows] = (d_act * third * sigma * (1.0 + first * (1.0 - sigma))).astype(jnp.bfloat16)
            dbuf[1, rows] = (d_act * swish).astype(jnp.bfloat16)
            dbuf[2, rows] = (swish * third).astype(jnp.bfloat16)
            dbuf[3, rows] = d_out

    def outer(h, j):
        left = kbuf[h, pl.ds(pad, local)] if j < 2 else dbuf[3]
        value = mm(left, dbuf[j], 0, 0).astype(jnp.bfloat16)
        for p in range(pieces):
            g[h * per + j * pieces + p] = value[p * CHUNK : (p + 1) * CHUNK]

    def attend(block, h, order):
        start = pl.multiple_of(block * BLOCK, BLOCK)
        slot = order % 2

        @pl.when(block == blocks - 1)
        def _():
            for k in (2, 3):
                load_one(k, h).wait()

            @pl.when(jnp.logical_not(early))
            def _():
                for k in (0, 1):
                    load_one(k, h).wait()

        @pl.when((block == halo_blocks - 1) & (h < here) & (me > 0))
        def _():
            for c in halo(h):
                c.wait_recv()

        @pl.when(order >= 2)
        def _():
            block_out(block, h, slot).wait()

        q = qbuf[h, pl.ds(start, BLOCK)]
        inside = (block >= halo_blocks) | (h < here)

        @pl.when(inside)
        def _():
            stage[slot] = attention(q, vbuf.at[h], h, start)

        @pl.when(jnp.logical_not(inside))
        def _():
            stage[slot] = jnp.zeros(stage.shape[1:], jnp.float32)

        @pl.when(early)
        def _():
            y = fast_output(q, wb, h)
            stage[slot] += jnp.where(position(start) < edge, y, 0.0)

        block_out(block, h, slot).start()

    def combine(u):
        block, h = place(u)
        start = pl.multiple_of(block * BLOCK, BLOCK)
        slot = u % 2

        @pl.when(u + 1 < units)
        def _():
            attn_in(u + 1).start()

        attn_in(u).wait()

        @pl.when(block == blocks - 1)
        def _():
            load_one(2, h).wait()

            @pl.when(jnp.logical_not(late))
            def _():
                for k in (0, 1):
                    load_one(k, h).wait()

        @pl.when(u >= 2)
        def _():
            block_out(block, h, slot).wait()

        if here < heads:

            @pl.when((block == halo_blocks - 1) & (h >= here))
            def _():
                own_values(h).wait()

            @pl.when((block == halo_blocks - 1) & (h >= here) & (me > 0))
            def _():
                for c in halo(h):
                    c.wait_recv()

            @pl.when((block < halo_blocks) & (h >= here))
            def _():
                q = qbuf[h, pl.ds(start, BLOCK)]
                stage[slot] += attention(q, vbuf.at[h - here], h, start)

        @pl.when(late)
        def _():
            y = fast_output(qbuf[h, pl.ds(start, BLOCK)], wb, h)
            mstage[slot] = (stage[slot] + jnp.where(position(start) >= edge, y, 0.0)).astype(jnp.bfloat16)

        @pl.when(jnp.logical_not(late))
        def _():
            mstage[slot] = stage[slot].astype(jnp.bfloat16)

        block_out(block, h, slot).start()

    def put(n):
        return pltpu.make_async_copy(res.at[n], sums.at[n], out_sem.at[0])

    def finish(n):
        put(n).start()
        part = jnp.square(res[n].astype(jnp.float32))
        sq_all[mine] += jnp.sum(part.reshape(-1, *sq_all.shape[1:]), axis=0)

    def gradient(i):
        h = i // per
        kind = i % per

        @pl.when((h < heads) & works)
        def _():
            @pl.when(kind < ahead)
            def _():
                backward(h, kind)

            for j in range(3):

                @pl.when(kind == ahead + j)
                def _():
                    outer(h, j)

        if second:

            @pl.when((h < heads) & (kind == 1))
            def _():
                keep(h).wait()
                load_next(h)

        @pl.when((h < heads - 1) & (kind == per - 1) & prepares)
        def _():
            prepare(h + 1)

    def send_halo(i):
        size = WIN // HALO_PIECES

        @pl.when((i < away * HALO_PIECES) & (me < count - 1))
        def _():
            for c in halo(low + i // HALO_PIECES, pl.multiple_of((i % HALO_PIECES) * size, size), size):
                c.start()

    if away:

        @pl.loop(0, HALO_LEAD)
        def _(i):
            send_halo(i)

    prepares = (me >= 0) if second else works

    @pl.when(prepares)
    def _():
        prepare(0)

    for h in range(heads):
        for i in (0, 1, 2) if second else (0, 1, 2, 3):
            if h > 0 or i > 1:
                load_one(i, h).start()
    if second:
        attn_in(0).start()
        for h in range(here, heads):
            own_values(h).start()

    @pl.loop(0, ahead)
    def _(i):
        gradient(i)

    if second:
        steps = [begin + units]
    else:
        near_at = max(NEAR_AT, begin + plain)
        steps = [begin + plain, near_at + NEAR_EVERY * (units - plain)]

    @pl.loop(0, max(netw.length, *steps))
    def _(i):
        if away:

            send_halo(i + HALO_LEAD)


        gradient(i + ahead)

        netw.advance(i, finish)
        u = i - begin
        if second:

            @pl.when((u >= 0) & (u < units))
            def _():
                combine(u)
        else:

            @pl.when((u >= 0) & (u < plain))
            def _():
                block, h = place(u)
                attend(block, h, u)

            v = i - near_at
            w = v // NEAR_EVERY

            @pl.when((v >= 0) & (v % NEAR_EVERY == 0) & (w < units - plain))
            def _():
                attend(halo_blocks - 1 - w % halo_blocks, w // halo_blocks, plain + w)

    share_squares(sq_all, sq_ref, sq_send, sq_recv)
    netw.drain()
    if away:

        @pl.when(me < count - 1)
        def _():
            for i in range(2):
                every = kbuf.at[pl.ds(low, away), pl.ds(0, WIN)]
                pltpu.make_async_remote_copy(
                    src_ref=every, dst_ref=every, send_sem=halo_send.at[i], recv_sem=halo_recv.at[i, 0],
                    device_id={"seq": me + 1}, device_id_type=pl.DeviceIdType.MESH,
                ).wait_send()

    if not second:

        @pl.when(jnp.logical_not(works))
        def _():
            for c in load_weights(0):
                c.wait()

    for slot in range(2):
        block_out(0, 0, slot).wait()
    pltpu.make_async_copy(res, sums, out_sem.at[0]).wait()


def block_step(second, arrays, total_count):
    near, far = sizes_of_seq()
    if second:
        keys, weights = arrays[4], arrays[8]
    else:
        keys, weights = arrays[3], arrays[7]
    heads, _, hd, hid = weights.shape
    local = keys.shape[0]
    chunks = heads * 3 * hd // CHUNK
    vmem = pl.BlockSpec(memory_space=pltpu.VMEM)
    smem = pl.BlockSpec(memory_space=pltpu.SMEM)
    hbm = pl.BlockSpec(memory_space=pl.ANY)
    half = CHUNK // CORES
    more = (jax.ShapeDtypeStruct(weights.shape, jnp.float32),) if second else ()
    kinds = link_kinds(near)
    ranks = lax.axis_size("head")
    dma = pltpu.SemaphoreType.DMA
    bf16, f32 = jnp.bfloat16, jnp.float32
    pad = WIN
    away = max(heads // 2, 1)
    scratch = [
        pltpu.VMEM((heads, pad + local, hd), bf16),
        pltpu.VMEM((heads, local, hd), bf16),
        pltpu.VMEM((heads, local, hd), bf16),
        pltpu.VMEM((3, hd, hid), f32),
        pltpu.VMEM((heads, 3, hd, hid), bf16),
        pltpu.VMEM((chunks, CHUNK, hid), bf16),
        pltpu.VMEM((chunks, CHUNK, hid), bf16),
        pltpu.VMEM((chunks, half, hid), bf16),
        pltpu.VMEM((3, chunks, half, hid), bf16),
        pltpu.VMEM((4, local, hd), bf16),
        pltpu.VMEM((2, BLOCK, hd), f32),
        pltpu.VMEM((ranks, 8, hid), f32),
        dma((kinds,)),
        dma((kinds, chunks)),
        dma((ranks,)),
        dma((ranks,)),
        dma((4, heads)),
        dma((2,)),
        dma((1,)),
        dma((2,)),
    ]
    scratch += [
        pltpu.VMEM((away, 2 * WIN, hd) if second else (heads, pad + local, hd), bf16),
        dma((2,)),
        dma((2, heads)),
    ]
    if second:
        scratch += [
            pltpu.VMEM((3 * hd // CHUNK, CHUNK, hid), bf16),
            pltpu.VMEM((2, BLOCK, hd), bf16),
            dma((2,)),
            dma((away,)),
            dma((1,)),
        ]
        in_specs = [smem, smem, vmem, vmem] + [hbm] * 7
        wide = jax.ShapeDtypeStruct(keys.shape, bf16)
    else:
        in_specs = [smem, smem, vmem, hbm, hbm, hbm, hbm, hbm]
        wide = jax.ShapeDtypeStruct(keys.shape, f32)
    return pl.pallas_call(
        functools.partial(block_kernel, second, near, far, total_count),
        in_specs=in_specs,
        out_specs=(hbm, vmem, hbm) + (hbm,) * len(more),
        out_shape=(
            jax.ShapeDtypeStruct((chunks, CHUNK, hid), bf16),
            jax.ShapeDtypeStruct((8, hid), f32),
            wide,
        )
        + more,
        scratch_shapes=scratch,
        compiler_params=pltpu.CompilerParams(
            collective_id=int(second), has_side_effects=True, vmem_limit_bytes=67043328
        ),
        cost_estimate=pl.CostEstimate(flops=10**11, bytes_accessed=60 << 20, transcendentals=0),
        name="second" if second else "first",
    )(*arrays)


def renew_kernel(total_count, sq_ref, w_ref, g_ref, mixed_ref, out_ref, copy_ref):
    coef = fast_rate / jnp.sqrt(jnp.sum(sq_ref[...]) / total_count + epsilon)
    out_ref[...] = w_ref[...] - coef * g_ref[...].astype(jnp.float32)
    copy_ref[...] = mixed_ref[...]


def renew(total_count, sq, weights, g, mixed):
    flat = (-1, weights.shape[-1])
    w = weights.reshape(flat)
    steps = RENEW_STEPS
    small = pl.BlockSpec(sq.shape, lambda i: (0, 0))
    tile = pl.BlockSpec((w.shape[0] // steps, w.shape[1]), lambda i: (i, 0))
    rows = pl.BlockSpec((mixed.shape[0] // steps, mixed.shape[1]), lambda i: (i, 0))
    out, mixed = pl.pallas_call(
        functools.partial(renew_kernel, total_count),
        grid=(steps,),
        in_specs=[small, tile, tile, rows],
        out_specs=(tile, rows),
        out_shape=(
            jax.ShapeDtypeStruct(w.shape, jnp.float32),
            jax.ShapeDtypeStruct(mixed.shape, mixed.dtype),
        ),
        compiler_params=pltpu.CompilerParams(vmem_limit_bytes=67043328),
        cost_estimate=pl.CostEstimate(flops=4 * w.size, bytes_accessed=16 * w.size, transcendentals=0),
        name="renew",
    )(sq, w, g.reshape(flat), mixed)
    return mixed, out.reshape(weights.shape)


def per_device(queries, keys, values, targets, token_rate, window, split, fast_init):
    total_count = float(fast_init.size * lax.axis_size("head"))
    g0, sq0, attn = block_step(
        False, (split, window, token_rate.T, keys, values, queries, targets, fast_init), total_count
    )
    g1, sq1, mixed, base = block_step(
        True,
        (split, window, token_rate.T, sq0, keys, values, queries, targets, fast_init, g0, attn),
        total_count,
    )
    return renew(total_count, sq1, base, g1, mixed)


def solution(mesh):
    return jax.shard_map(
        per_device,
        mesh=mesh,
        in_specs=(
            P("seq", "head"),
            P("seq", "head"),
            P("seq", "head"),
            P("seq", "head"),
            P("seq", "head"),
            P("head"),
            P(),
            P("head", None, None, None),
        ),
        out_specs=(P("seq", "head"), P("head", None, None, None)),
        check_vma=False,
    )
```
